256 devices in a mesh: emb: 32 (over z_hi, y, core), wide: 8 (over x, z_lo).
Axes of the slice: x: 4, y: 4, z: 8 (z_hi: 4, z_lo: 2; z = z_hi * 2 + z_lo), core: 2. Of those that a mesh axis runs over, the one named last changes fastest.
Arguments:
- tables: bfloat16 [512, 512, 256], P('emb'), may hold values from -3 to 3
- bag_ids: int32 [8, 128, 512, 4], P('wide', None, 'emb'), may hold values from 0 to 511
- bag_lengths: int32 [8, 128, 512], P('wide', None, 'emb'), may hold values from 1 to 4
- slot_field: int32 [512], replicated, may hold values from 0 to 511, each once
- proj_y: bfloat16 [512, 256], replicated, may hold values from -0.25 to 0.25
- proj_p: bfloat16 [128, 512], replicated, may hold values from -0.25 to 0.25
- linear_w: bfloat16 [384, 512], replicated, may hold values from -0.25 to 0.25
- fm_gain: float32 [256], replicated, may hold values from 0.5 to 1.5
- w_up: bfloat16 [8192, 256], P('wide'), may hold values from -0.375 to 0.375
- w_down: bfloat16 [8192, 256], P('wide'), may hold values from -0.0625 to 0.0625
- out_gain: float32 [256], replicated, may hold values from 0.5 to 1.5
- cotangent: bfloat16 [8, 128, 512, 256], P('wide', 'emb'), may hold values from -6 to 6
Outputs:
- layer_out: bfloat16 [8, 128, 512, 256], P('wide', 'emb')
- pooled_grad: bfloat16 [8, 128, 512, 256], P('wide', None, 'emb')
- grad_up: float32 [8192, 256], P('wide')
- grad_down: float32 [8192, 256], P('wide')
The draws below stay inside these ranges and needn't reach their ends.
Inputs may be any that keep to these rules, and one draw needn't show every extreme that they name: `bag_ids`: each id indexes a bucket of the table of its slot. `slot_field`: each field appears in exactly one slot.
All inputs are finite; a program needn't handle non-finite values.
Results may differ from the reference program's by a relative error of at most 0.008.
Values may be sent and summed in bfloat16 or wider, within the bound.
A program may use at most 128 MiB of HBM per device.

```python
import math
import jax
import jax.numpy as jnp
import numpy as np
from jax import lax

E = 256
FIELDS = 512
K = 256
HID = 8192
NF = 128
B_DEV = 4
ROWS = 512
BAG = 4
NL = 384
GROUPS = 8
GROUP_B = 128


def set_ends(entries, rng, least, largest):
    index_at = [jax.random.randint(jax.random.fold_in(rng, axis), (), 0, length) for axis, length in enumerate(entries.shape)]
    widest = entries.shape.index(max(entries.shape))
    next_to = index_at[:widest] + [(index_at[widest] + 1) % entries.shape[widest]] + index_at[widest + 1:]
    return entries.at[tuple(index_at)].set(least).at[tuple(next_to)].set(largest)


def steps_of(key, extent, shards, smallest, top_value):
    level = 1.0
    for dim, blocks in shards:
        steps = jax.random.uniform(jax.random.fold_in(jax.random.fold_in(key, 6), dim), (blocks,), jnp.float32, smallest / len(shards), top_value / len(shards))
        level = level * jnp.repeat(jnp.exp(steps), extent[dim] // blocks).reshape((-1,) + (1,) * (len(extent) - 1 - dim))
    return level


def rank_bounds(count, lean):
    portions = [(1 << 20) // math.isqrt(rank ** lean) + 1 for rank in range(1, count + 1)]
    width = 1 + sum(portions) // (1 << 30)
    return np.cumsum(np.array([max(1, weight // width) for weight in portions]))


def skewed_ids(rng, shape, count, lean):
    grid = rank_bounds(count, lean)
    ticket = jax.random.randint(jax.random.fold_in(rng, 1), shape, 0, int(grid[count - 1]))
    rank = jnp.searchsorted(jnp.asarray(grid, jnp.int32), ticket, side="right")
    return jax.random.permutation(jax.random.fold_in(rng, 2), count)[rank].astype(jnp.int32)


def gaussian(key, dims, scale, bound, cuts=(), held_as=jnp.bfloat16):
    level = steps_of(key, dims, cuts, -0.22, 0.18) if cuts else 1.0
    values = jax.random.normal(key, dims, jnp.float32) * scale * level
    return jnp.minimum(jnp.maximum(values, -bound), bound).astype(held_as)


def setup_inputs(seed: int = 0) -> dict:
    streams_of = jax.random.split(jax.random.key(seed), 13)
    tables = gaussian(streams_of[0], (FIELDS, ROWS, E), 0.5, 3.0, ((0, 32),))
    bag_ids = set_ends(skewed_ids(streams_of[1], (GROUPS, GROUP_B, FIELDS, BAG), ROWS, 2), jax.random.fold_in(streams_of[1], 3), 0, ROWS - 1).astype(jnp.int32)
    bag_lengths = set_ends(jax.random.randint(streams_of[2], (GROUPS, GROUP_B, FIELDS), 1, BAG + 1), jax.random.fold_in(streams_of[2], 1), 1, BAG).astype(jnp.int32)
    slot_field = jax.random.permutation(streams_of[3], FIELDS).astype(jnp.int32)
    proj_y = gaussian(streams_of[4], (FIELDS, K), FIELDS ** -0.5, 0.25)
    proj_p = gaussian(streams_of[5], (NF, FIELDS), FIELDS ** -0.5, 0.25)
    linear_w = gaussian(streams_of[6], (NL, FIELDS), FIELDS ** -0.5, 0.25)
    fm_gain = jnp.clip(1.0 + 0.1 * jax.random.normal(streams_of[7], (K,), jnp.float32), 0.5, 1.5)
    w_up = gaussian(streams_of[8], (HID, K), K ** -0.5, 0.375, ((0, 8),))
    w_down = gaussian(streams_of[9], (HID, E), HID ** -0.5, 0.0625, ((0, 8),))
    out_gain = jnp.clip(1.0 + 0.1 * jax.random.normal(streams_of[10], (E,), jnp.float32), 0.5, 1.5)
    cotangent = gaussian(streams_of[11], (GROUPS, GROUP_B, FIELDS, E), 1.0, 6.0, ((0, 8), (1, 32)))
    return dict(tables=tables, bag_ids=bag_ids, bag_lengths=bag_lengths, slot_field=slot_field, proj_y=proj_y, proj_p=proj_p, linear_w=linear_w, fm_gain=fm_gain, w_up=w_up, w_down=w_down, out_gain=out_gain, cotangent=cotangent)


norm_eps = 1e-05

def mult(form, left, right):
    return jnp.einsum(form, left.astype(jnp.float32), right.astype(jnp.float32), precision=lax.Precision.HIGHEST)

def layer_norm(values):
    centre = lax.optimization_barrier(jnp.mean(values, axis=-1, keepdims=True))
    shifted = values - centre
    scale = lax.rsqrt(lax.optimization_barrier(jnp.mean(shifted * shifted, axis=-1, keepdims=True)) + norm_eps)
    return (shifted * scale, scale)

def norm_back(unit, scale, gain, upstream):
    scaled = upstream * gain
    return scale * (scaled - lax.optimization_barrier(jnp.mean(scaled, axis=-1, keepdims=True)) - unit * lax.optimization_barrier(jnp.mean(scaled * unit, axis=-1, keepdims=True)))

def silu_back(values):
    sigma = jax.nn.sigmoid(values)
    return sigma * (1.0 + values * (1.0 - sigma))

def pool_bags(tables, ids, lengths):
    field_index = jnp.arange(FIELDS, dtype=jnp.int32)[None, :, None]
    gathered = tables[field_index, ids]
    live = (jnp.arange(BAG, dtype=jnp.int32)[None, None, :] < lengths[:, :, None]).astype(jnp.float32)
    return lax.optimization_barrier(jnp.sum(gathered.astype(jnp.float32) * live[..., None], axis=2)).astype(jnp.bfloat16)

def reference(tables, bag_ids, bag_lengths, slot_field, proj_y, proj_p, linear_w, fm_gain, w_up, w_down, out_gain, cotangent):
    ids_blocks = bag_ids.reshape(-1, B_DEV, FIELDS, BAG)
    length_blocks = bag_lengths.reshape(-1, B_DEV, FIELDS)
    cot_blocks = cotangent.reshape(-1, B_DEV, FIELDS, E)

    def one_block(carry, inputs):
        up_total, down_total = carry
        ids_now, lengths_now, cot_now = inputs
        pooled = pool_bags(tables, ids_now, lengths_now)
        embeds = jnp.zeros_like(pooled).at[:, slot_field].set(pooled)
        crossed = mult('bfe,fk->bek', embeds, proj_y).astype(jnp.bfloat16)
        mixing = mult('nf,bfe->bne', proj_p, embeds).astype(jnp.bfloat16)
        inter = mult('bne,bek->bnk', mixing, crossed)
        inter_unit, inter_scale = layer_norm(inter)
        inter_norm = (inter_unit * fm_gain).astype(jnp.bfloat16)
        inter_rows = inter_norm.reshape(B_DEV * NF, K)
        gate_pre = mult('rk,hk->rh', inter_rows, w_up)
        hidden = jax.nn.silu(gate_pre).astype(jnp.bfloat16)
        ff_rows = mult('rh,he->re', hidden, w_down)
        linear_out = mult('lf,bfe->ble', linear_w, embeds)
        summed = jnp.concatenate([ff_rows.reshape(B_DEV, NF, E), linear_out], axis=1) + embeds.astype(jnp.float32)
        summed_unit, summed_scale = layer_norm(summed)
        layer_out = (summed_unit * out_gain).astype(jnp.bfloat16)
        grad_summed = norm_back(summed_unit, summed_scale, out_gain, cot_now.astype(jnp.float32))
        grad_ff = grad_summed[:, :NF].astype(jnp.bfloat16)
        grad_lin = grad_summed[:, NF:].astype(jnp.bfloat16)
        grad_ff_rows = grad_ff.reshape(B_DEV * NF, E)
        down_part = mult('rh,re->he', hidden, grad_ff_rows)
        grad_hidden = mult('re,he->rh', grad_ff_rows, w_down)
        grad_gate = (grad_hidden * silu_back(gate_pre)).astype(jnp.bfloat16)
        up_part = mult('rh,rk->hk', grad_gate, inter_rows)
        grad_norm = mult('rh,hk->rk', grad_gate, w_up).reshape(B_DEV, NF, K)
        grad_inter = norm_back(inter_unit, inter_scale, fm_gain, grad_norm).astype(jnp.bfloat16)
        grad_mixing = mult('bnk,bek->bne', grad_inter, crossed).astype(jnp.bfloat16)
        grad_crossed = mult('bne,bnk->bek', mixing, grad_inter).astype(jnp.bfloat16)
        grad_embeds = grad_summed + mult('lf,ble->bfe', linear_w, grad_lin) + mult('nf,bne->bfe', proj_p, grad_mixing) + mult('fk,bek->bfe', proj_y, grad_crossed)
        grad_embeds = grad_embeds.astype(jnp.bfloat16)
        slot_grads = grad_embeds[:, slot_field]
        return ((up_total + up_part, down_total + down_part), (layer_out, slot_grads))
    start_carry = (jnp.zeros((HID, K), jnp.float32), jnp.zeros((HID, E), jnp.float32))
    (grad_up, grad_down), (outs, grads) = lax.scan(one_block, start_carry, (ids_blocks, length_blocks, cot_blocks))
    layer_out = outs.reshape(GROUPS, GROUP_B, FIELDS, E)
    pooled_grad = grads.reshape(GROUPS, GROUP_B, FIELDS, E)
    return (layer_out, pooled_grad, grad_up, grad_down)
```

```python
import functools

import jax
import jax.numpy as jnp
from jax import lax
from jax.experimental import pallas as pl
from jax.experimental.pallas import tpu as pltpu
from jax.sharding import PartitionSpec as P

MESH = pl.DeviceIdType.MESH
F32 = jnp.float32
BF16 = jnp.bfloat16

E = 256
FIELDS = 512
ROWS = 512
NF = 128
NL = 384
BAG = 4
SAMPLES = 4
SLOTS = 16
GROUP_B = 128
EMB = 32
XS = 4
YS = 4
ZS = 4
SLICE = 1024
TH = 512
TILES = 8
NROW = SAMPLES * NF
norm_eps = 1e-05


def dot(a, b, ca=1, cb=0):
    return lax.dot_general(a, b, (((ca,), (cb,)), ((), ())), preferred_element_type=F32)


def send(src, dst, send_sem, recv_sem, **device):
    return pltpu.make_async_remote_copy(
        src_ref=src,
        dst_ref=dst,
        send_sem=send_sem,
        recv_sem=recv_sem,
        device_id=device,
        device_id_type=MESH,
    )


def signal(sem, **device):
    pl.semaphore_signal(sem, inc=1, device_id=device, device_id_type=MESH)


def norm_forward(values):
    centre = jnp.mean(values, axis=-1, keepdims=True)
    shifted = values - centre
    scale = lax.rsqrt(jnp.mean(shifted * shifted, axis=-1, keepdims=True) + norm_eps)
    return shifted * scale, scale


def norm_back(unit, scale, gain, upstream):
    scaled = upstream * gain
    return scale * (
        scaled
        - jnp.mean(scaled, axis=-1, keepdims=True)
        - unit * jnp.mean(scaled * unit, axis=-1, keepdims=True)
    )


def pool_kernel(
    ids, lengths, tables, w_up, w_down, slots_out, up_all, down_all,
    held, pooled, outgoing, table_sem, bag_send, bag_recv, w_send, w_recv, w_local,
):
    me = lax.axis_index("emb")
    wide = lax.axis_index("wide")
    x = wide // 2
    z_lo = lax.rem(wide, 2)

    def fetch(s):
        return pltpu.make_async_copy(tables.at[s], held.at[s], table_sem.at[s])

    @pl.loop(0, SLOTS)
    def _(s):
        fetch(s).start()

    barrier = pltpu.get_barrier_semaphore()

    @pl.loop(1, EMB)
    def _(k):
        signal(barrier, emb=lax.rem(me + k, EMB))

    for k in range(1, XS):
        signal(barrier, wide=lax.rem(x + k, XS) * 2 + z_lo)
    pl.semaphore_wait(barrier, EMB - 1 + XS - 1)

    weights = ((w_up, up_all), (w_down, down_all))
    local = [
        pltpu.make_async_copy(w, full.at[x], w_local.at[i]) for i, (w, full) in enumerate(weights)
    ]
    remote = [
        send(w, full.at[x], w_send.at[i, k - 1], w_recv.at[i, k - 1], wide=lax.rem(x + k, XS) * 2 + z_lo)
        for k in range(1, XS)
        for i, (w, full) in enumerate(weights)
    ]
    for copy in remote + local:
        copy.start()

    bucket = lax.broadcasted_iota(jnp.int32, (ROWS, GROUP_B), 0)

    for s in range(SLOTS):
        fetch(s).wait()
        live = lengths[s : s + 1, :]
        counts = jnp.zeros((ROWS, GROUP_B), F32)
        for j in range(BAG):
            wanted = jnp.where(live > j, ids[s, j : j + 1, :], -1)
            counts = counts + jnp.where(bucket == wanted, 1.0, 0.0)
        rows = dot(counts.astype(BF16), held[s], 0, 0)
        for half in range(2):
            pooled[half, pl.ds(s, GROUP_B, stride=SLOTS), :] = rows[:, half * 128 : half * 128 + 128]

    for half in range(2):
        outgoing[:, :, half * 128 : half * 128 + 128] = (
            pooled[half].astype(BF16).reshape(GROUP_B, SLOTS, 128)
        )

    mine = pl.ds(pl.multiple_of(me * SLOTS, SLOTS), SLOTS)

    def bags(k):
        peer = lax.rem(me + k, EMB)
        return send(
            outgoing.at[pl.ds(peer * SAMPLES, SAMPLES)],
            slots_out.at[:, mine, :],
            bag_send.at[k],
            bag_recv.at[k],
            emb=peer,
        )

    @pl.loop(1, EMB)
    def _(k):
        bags(k).start()

    slots_out[:, mine, :] = outgoing[pl.ds(me * SAMPLES, SAMPLES)]

    @pl.loop(1, EMB)
    def _(k):
        source = lax.rem(me + EMB - k, EMB)
        there = pl.ds(pl.multiple_of(source * SLOTS, SLOTS), SLOTS)
        send(
            outgoing.at[pl.ds(source * SAMPLES, SAMPLES)],
            slots_out.at[:, there, :],
            bag_send.at[k],
            bag_recv.at[k],
            emb=source,
        ).wait_recv()
        bags(k).wait_send()

    for copy in local:
        copy.wait()
    for copy in remote:
        copy.wait_send()
    for k in range(1, XS):
        source = lax.rem(x + XS - k, XS)
        for i, (w, full) in enumerate(weights):
            send(
                w, full.at[source], w_send.at[i, k - 1], w_recv.at[i, k - 1], wide=source * 2 + z_lo
            ).wait_recv()


def pool_and_gather(ids, lengths, tables, w_up, w_down):
    any_space = pl.BlockSpec(memory_space=pl.ANY)
    vmem = pl.BlockSpec(memory_space=pltpu.VMEM)
    return pl.pallas_call(
        pool_kernel,
        name="pool_and_gather",
        out_shape=(
            jax.ShapeDtypeStruct((SAMPLES, FIELDS, E), BF16),
            jax.ShapeDtypeStruct((XS, SLICE, E), BF16),
            jax.ShapeDtypeStruct((XS, SLICE, E), BF16),
        ),
        in_specs=[vmem, vmem, any_space, any_space, any_space],
        out_specs=(vmem, any_space, any_space),
        scratch_shapes=[
            pltpu.VMEM((SLOTS, ROWS, E), BF16),
            pltpu.VMEM((2, GROUP_B * SLOTS, 128), F32),
            pltpu.VMEM((GROUP_B, SLOTS, E), BF16),
            pltpu.SemaphoreType.DMA((SLOTS,)),
            pltpu.SemaphoreType.DMA((EMB,)),
            pltpu.SemaphoreType.DMA((EMB,)),
            pltpu.SemaphoreType.DMA((2, XS - 1)),
            pltpu.SemaphoreType.DMA((2, XS - 1)),
            pltpu.SemaphoreType.DMA((2,)),
        ],
        compiler_params=pltpu.CompilerParams(
            collective_id=0, has_side_effects=True, vmem_limit_bytes=32 << 20
        ),
    )(ids, lengths, tables, w_up, w_down)


def layer_kernel(
    slots, field_row, field_column, proj_y, proj_p, linear_w, fm_gain, w_up, w_down, out_gain, cotangent,
    layer_out, slot_grads, grads,
    embeds, crossed, mixing, inter_unit, inter_scale, rows, rows_t, hidden, slope, ff, ff_out, ff_in,
    linear_out, grad_summed, grad_rows, grad_rows_t, grad_lin, weight_sum, norm_out, norm_in,
    send_sem, recv_sem,
):
    wide = lax.axis_index("wide")
    partner = wide + 1 - 2 * lax.rem(wide, 2)

    barrier = pltpu.get_barrier_semaphore()
    signal(barrier, wide=partner)

    def exchange(src, dst, n):
        return send(src, dst, send_sem.at[n], recv_sem.at[n], wide=partner)

    by_field = jnp.where(
        lax.broadcasted_iota(jnp.int32, (FIELDS, FIELDS), 0) == field_row[...], 1.0, 0.0
    ).astype(BF16)

    def embed(b, _):
        x = dot(by_field, slots[b]).astype(BF16)
        embeds[b] = x
        cross = dot(x, proj_y[...], 0, 0).astype(BF16)
        crossed[b] = cross
        mix = dot(proj_p[...], x).astype(BF16)
        mixing[b] = mix
        unit, scale = norm_forward(dot(mix, cross))
        inter_unit[b] = unit
        inter_scale[b] = jnp.broadcast_to(scale, (NF, 128))
        rows[0, pl.ds(pl.multiple_of(b * NF, NF), NF), :] = (unit * fm_gain[...]).astype(BF16)
        return 0

    lax.fori_loop(0, SAMPLES, embed, 0)

    pl.semaphore_wait(barrier, 1)
    rows_copy = exchange(rows.at[0], rows.at[1], 0)
    rows_copy.start()

    ff[...] = jnp.zeros_like(ff)

    def forward(group, tile):
        gate = dot(rows[group], w_up[tile], 1, 1)
        sigma = 0.5 * jnp.tanh(0.5 * gate) + 0.5
        act = gate * sigma
        slope[group, tile] = (sigma + act * (1.0 - sigma)).astype(BF16)
        act = act.astype(BF16)
        hidden[group, tile] = act
        ff[group] += dot(act, w_down[tile])

    def forward_tiles(group, first, last):
        @pl.loop(first, last)
        def _(tile):
            forward(group, tile)

    forward_tiles(0, 0, TILES // 2)

    def linear(b, _):
        linear_out[b] = dot(linear_w[...], embeds[b])
        return 0

    lax.fori_loop(0, SAMPLES, linear, 0)
    rows_copy.wait()
    forward_tiles(1, 0, TILES)
    ff_out[...] = ff[1].astype(BF16)
    ff_copy = exchange(ff_out, ff_in, 1)
    ff_copy.start()
    forward_tiles(0, TILES // 2, TILES)
    rows_t[0] = rows[0].astype(F32).T.astype(BF16)
    rows_t[1] = rows[1].astype(F32).T.astype(BF16)
    ff_copy.wait()

    def finish(values, b, first, count):
        here = slice(first, first + count)
        unit, scale = norm_forward(values + embeds[b, here, :].astype(F32))
        layer_out[b, here, :] = (unit * out_gain[...]).astype(BF16)
        grad = norm_back(unit, scale, out_gain[...], cotangent[b, here, :].astype(F32))
        grad_summed[b, here, :] = grad
        return grad.astype(BF16)

    def finish_ff(b, _):
        mine = pl.ds(pl.multiple_of(b * NF, NF), NF)
        total = ff[0, mine, :] + ff_in[mine, :].astype(F32)
        grad_rows[0, mine, :] = finish(total, b, 0, NF)
        return 0

    lax.fori_loop(0, SAMPLES, finish_ff, 0)
    grad_copy = exchange(grad_rows.at[0], grad_rows.at[1], 2)
    grad_copy.start()

    def finish_linear(b, _):
        grad_lin[b] = finish(linear_out[b], b, NF, NL)
        grad_summed[b] += dot(linear_w[...], grad_lin[b], 0, 0)
        return 0

    lax.fori_loop(0, SAMPLES, finish_linear, 0)
    grad_rows_t[0] = grad_rows[0].astype(F32).T.astype(BF16)
    grad_copy.wait()
    grad_rows_t[1] = grad_rows[1].astype(F32).T.astype(BF16)

    ff[...] = jnp.zeros_like(ff)

    def backward(group, tile):
        grad_gate = (dot(grad_rows[group], w_down[tile], 1, 1) * slope[group, tile].astype(F32)).astype(BF16)
        ff[group] += dot(grad_gate, w_up[tile])
        up = dot(rows_t[group], grad_gate)
        down = dot(grad_rows_t[group], hidden[group, tile])
        return up, down

    @pl.loop(0, TILES)
    def _(tile):
        up, down = backward(1, tile)
        weight_sum[0, tile] = up
        weight_sum[1, tile] = down

    norm_out[...] = ff[1].astype(BF16)
    norm_copy = exchange(norm_out, norm_in, 3)
    norm_copy.start()

    @pl.loop(0, TILES)
    def _(tile):
        up, down = backward(0, tile)
        for kind, part in enumerate((up, down)):
            whole = (weight_sum[kind, tile] + part).astype(BF16)
            for half in range(2):
                grads[kind, tile * 2 + half] = whole[:, half * 256 : (half + 1) * 256]

    norm_copy.wait()

    by_slot = jnp.where(
        lax.broadcasted_iota(jnp.int32, (FIELDS, FIELDS), 1) == field_column[...], 1.0, 0.0
    ).astype(BF16)

    def tail(b, _):
        mine = pl.ds(pl.multiple_of(b * NF, NF), NF)
        upstream = ff[0, mine, :] + norm_in[mine, :].astype(F32)
        grad_inter = norm_back(inter_unit[b], inter_scale[b, :, 0:1], fm_gain[...], upstream).astype(BF16)
        grad_mixing = dot(grad_inter, crossed[b], 1, 1).astype(BF16)
        grad_crossed = dot(mixing[b], grad_inter, 0, 0).astype(BF16)
        total = grad_summed[b] + dot(proj_p[...], grad_mixing, 0, 0)
        total = total + dot(proj_y[...], grad_crossed, 1, 1)
        slot_grads[b] = dot(by_slot, total.astype(BF16)).astype(BF16)
        return 0

    lax.fori_loop(0, SAMPLES, tail, 0)


def layer(*operands):
    vmem = pl.BlockSpec(memory_space=pltpu.VMEM)
    return pl.pallas_call(
        layer_kernel,
        name="layer",
        out_shape=(
            jax.ShapeDtypeStruct((SAMPLES, FIELDS, E), BF16),
            jax.ShapeDtypeStruct((SAMPLES, FIELDS, E), BF16),
            jax.ShapeDtypeStruct((2, TILES * 2, 256, 256), BF16),
        ),
        in_specs=[vmem] * len(operands),
        out_specs=(vmem,) * 3,
        scratch_shapes=[
            pltpu.VMEM((SAMPLES, FIELDS, E), BF16),
            pltpu.VMEM((SAMPLES, E, E), BF16),
            pltpu.VMEM((SAMPLES, NF, E), BF16),
            pltpu.VMEM((SAMPLES, NF, E), F32),
            pltpu.VMEM((SAMPLES, NF, 128), F32),
            pltpu.VMEM((2, NROW, E), BF16),
            pltpu.VMEM((2, E, NROW), BF16),
            pltpu.VMEM((2, TILES, NROW, TH), BF16),
            pltpu.VMEM((2, TILES, NROW, TH), BF16),
            pltpu.VMEM((2, NROW, E), F32),
            pltpu.VMEM((NROW, E), BF16),
            pltpu.VMEM((NROW, E), BF16),
            pltpu.VMEM((SAMPLES, NL, E), F32),
            pltpu.VMEM((SAMPLES, FIELDS, E), F32),
            pltpu.VMEM((2, NROW, E), BF16),
            pltpu.VMEM((2, E, NROW), BF16),
            pltpu.VMEM((SAMPLES, NL, E), BF16),
            pltpu.VMEM((2, TILES, E, TH), F32),
            pltpu.VMEM((NROW, E), BF16),
            pltpu.VMEM((NROW, E), BF16),
            pltpu.SemaphoreType.DMA((4,)),
            pltpu.SemaphoreType.DMA((4,)),
        ],
        compiler_params=pltpu.CompilerParams(
            collective_id=1, has_side_effects=True, vmem_limit_bytes=60 << 20
        ),
    )(*operands)


def reduce_kernel(
    slot_grads, grads, bag_grads, up_out, down_out,
    from_core, to_x, from_x, to_y, from_y, to_z, from_z, whole,
    bag_send, bag_recv, send_sem, recv_sem,
):
    me = lax.axis_index("emb")
    wide = lax.axis_index("wide")
    x = wide // 2
    z_lo = lax.rem(wide, 2)
    core = lax.rem(me, 2)
    y = lax.rem(me // 2, YS)
    z = me // (2 * YS)
    sibling = me + 1 - 2 * core

    def emb_at(z_at, y_at):
        return (z_at * YS + y_at) * 2 + core

    barrier = pltpu.get_barrier_semaphore()

    @pl.loop(1, EMB)
    def _(k):
        signal(barrier, emb=lax.rem(me + k, EMB))

    for k in range(1, XS):
        signal(barrier, wide=lax.rem(x + k, XS) * 2 + z_lo)
    pl.semaphore_wait(barrier, EMB - 1 + XS - 1)

    core_copy = send(grads.at[1 - core], from_core, send_sem.at[0], recv_sem.at[0], emb=sibling)
    core_copy.start()

    def bags(k):
        peer = lax.rem(me + k, EMB)
        return send(
            slot_grads.at[:, pl.ds(pl.multiple_of(peer * SLOTS, SLOTS), SLOTS), :],
            bag_grads.at[pl.ds(me * SAMPLES, SAMPLES)],
            bag_send.at[k],
            bag_recv.at[k],
            emb=peer,
        )

    @pl.loop(1, EMB)
    def _(k):
        bags(k).start()

    bag_grads[pl.ds(me * SAMPLES, SAMPLES)] = slot_grads[:, pl.ds(pl.multiple_of(me * SLOTS, SLOTS), SLOTS), :]

    core_copy.wait()

    @pl.loop(0, TILES * 2)
    def _(t):
        to_x[t] = (grads[core, t].astype(F32) + from_core[t].astype(F32)).astype(BF16)

    x_copies = []
    for k in range(1, XS):
        peer = lax.rem(x + k, XS)
        x_copies.append(
            send(
                to_x.at[pl.ds(peer * 4, 4)],
                from_x.at[k - 1],
                send_sem.at[k],
                recv_sem.at[k],
                wide=peer * 2 + z_lo,
            )
        )
    for copy in x_copies:
        copy.start()
    for copy in x_copies:
        copy.wait()

    @pl.loop(0, 4)
    def _(t):
        mine = x * 4 + t
        total = grads[core, mine].astype(F32) + from_core[mine].astype(F32)
        for k in range(XS - 1):
            total = total + from_x[k, t].astype(F32)
        to_y[t] = total.astype(BF16)

    y_copies = []
    for k in range(1, YS):
        peer = lax.rem(y + k, YS)
        y_copies.append(
            send(to_y.at[peer], from_y.at[k - 1], send_sem.at[3 + k], recv_sem.at[3 + k], emb=emb_at(z, peer))
        )
    for copy in y_copies:
        copy.start()
    for copy in y_copies:
        copy.wait()

    total = to_y[y].astype(F32)
    for k in range(YS - 1):
        total = total + from_y[k].astype(F32)
    for part in range(ZS):
        to_z[part] = total[
            (part % 2) * 128 : (part % 2) * 128 + 128, (part // 2) * 128 : (part // 2) * 128 + 128
        ].astype(BF16)

    z_copies = []
    for k in range(1, ZS):
        peer = lax.rem(z + k, ZS)
        z_copies.append(
            send(to_z.at[peer], from_z.at[k - 1], send_sem.at[6 + k], recv_sem.at[6 + k], emb=emb_at(peer, y))
        )
    for copy in z_copies:
        copy.start()
    for copy in z_copies:
        copy.wait()

    total = to_z[z].astype(F32)
    for k in range(ZS - 1):
        total = total + from_z[k].astype(F32)

    def piece(z_at):
        row = pl.multiple_of(y * 256 + (z_at // 2) * 128, 128)
        column = pl.multiple_of(lax.rem(z_at, 2) * 128, 128)
        return whole.at[core, pl.ds(row, 128), pl.ds(column, 128)]

    row = pl.multiple_of(y * 256 + (z // 2) * 128, 128)
    column = pl.multiple_of(lax.rem(z, 2) * 128, 128)
    whole[core, pl.ds(row, 128), pl.ds(column, 128)] = total.T.astype(BF16)

    for k in range(1, ZS):
        send(
            piece(z), piece(z), send_sem.at[9 + k], recv_sem.at[9 + k], emb=emb_at(lax.rem(z + k, ZS), y)
        ).start()
    for k in range(1, ZS):
        source = lax.rem(z + ZS - k, ZS)
        copy = send(piece(z), piece(source), send_sem.at[9 + k], recv_sem.at[9 + k], emb=emb_at(source, y))
        copy.wait_send()
        copy.wait_recv()

    def band(y_at):
        return whole.at[core, pl.ds(pl.multiple_of(y_at * 256, 256), 256), :]

    for k in range(1, YS):
        send(
            band(y), band(y), send_sem.at[12 + k], recv_sem.at[12 + k], emb=emb_at(z, lax.rem(y + k, YS))
        ).start()
    for k in range(1, YS):
        source = lax.rem(y + YS - k, YS)
        copy = send(band(y), band(source), send_sem.at[12 + k], recv_sem.at[12 + k], emb=emb_at(z, source))
        copy.wait_send()
        copy.wait_recv()

    send(whole.at[core], whole.at[core], send_sem.at[16], recv_sem.at[16], emb=sibling).start()
    copy = send(whole.at[core], whole.at[1 - core], send_sem.at[16], recv_sem.at[16], emb=sibling)
    copy.wait_send()
    copy.wait_recv()
    up_out[...] = whole[0].astype(F32)
    down_out[...] = whole[1].astype(F32)

    @pl.loop(1, EMB)
    def _(k):
        source = lax.rem(me + EMB - k, EMB)
        send(
            slot_grads.at[:, pl.ds(pl.multiple_of(source * SLOTS, SLOTS), SLOTS), :],
            bag_grads.at[pl.ds(source * SAMPLES, SAMPLES)],
            bag_send.at[k],
            bag_recv.at[k],
            emb=source,
        ).wait_recv()
        bags(k).wait_send()


def reduce_and_return(slot_grads, grads):
    vmem = pl.BlockSpec(memory_space=pltpu.VMEM)
    return pl.pallas_call(
        reduce_kernel,
        name="reduce_and_return",
        out_shape=(
            jax.ShapeDtypeStruct((GROUP_B, SLOTS, E), BF16),
            jax.ShapeDtypeStruct((SLICE, E), F32),
            jax.ShapeDtypeStruct((SLICE, E), F32),
        ),
        in_specs=[vmem, vmem],
        out_specs=(vmem,) * 3,
        scratch_shapes=[
            pltpu.VMEM((TILES * 2, 256, 256), BF16),
            pltpu.VMEM((TILES * 2, 256, 256), BF16),
            pltpu.VMEM((XS - 1, 4, 256, 256), BF16),
            pltpu.VMEM((YS, 256, 256), BF16),
            pltpu.VMEM((YS - 1, 256, 256), BF16),
            pltpu.VMEM((ZS, 128, 128), BF16),
            pltpu.VMEM((ZS - 1, 128, 128), BF16),
            pltpu.VMEM((2, SLICE, E), BF16),
            pltpu.SemaphoreType.DMA((EMB,)),
            pltpu.SemaphoreType.DMA((EMB,)),
            pltpu.SemaphoreType.DMA((17,)),
            pltpu.SemaphoreType.DMA((17,)),
        ],
        compiler_params=pltpu.CompilerParams(
            collective_id=2, has_side_effects=True, vmem_limit_bytes=48 << 20
        ),
    )(slot_grads, grads)


def body(
    tables,
    bag_ids,
    bag_lengths,
    slot_field,
    proj_y,
    proj_p,
    linear_w,
    fm_gain,
    w_up,
    w_down,
    out_gain,
    cotangent,
):
    ids = bag_ids[0].transpose(1, 2, 0)
    lengths = bag_lengths[0].transpose(1, 0)
    slots, up_all, down_all = pool_and_gather(ids, lengths, tables, w_up, w_down)
    layer_out, slot_grads, grads = layer(
        slots,
        slot_field.reshape(1, FIELDS),
        slot_field.reshape(FIELDS, 1),
        proj_y,
        proj_p,
        linear_w,
        fm_gain.reshape(1, E),
        up_all.reshape(TILES, TH, E),
        down_all.reshape(TILES, TH, E),
        out_gain.reshape(1, E),
        cotangent[0],
    )
    bag_grads, grad_up, grad_down = reduce_and_return(slot_grads, grads)
    return (layer_out[None], bag_grads[None], grad_up, grad_down)


def solution(mesh):
    placed = (
        P("emb", None, None),
        P("wide", None, "emb", None),
        P("wide", None, "emb"),
        P(),
        P(),
        P(),
        P(),
        P(),
        P("wide", None),
        P("wide", None),
        P(),
        P("wide", "emb", None, None),
    )
    return jax.shard_map(
        body,
        mesh=mesh,
        in_specs=placed,
        out_specs=(
            P("wide", "emb", None, None),
            P("wide", None, "emb", None),
            P("wide", None),
            P("wide", None),
        ),
        check_vma=False,
    )
```

```python
import functools

import jax
import jax.numpy as jnp
from jax import lax
from jax.experimental import pallas as pl
from jax.experimental.pallas import tpu as pltpu
from jax.sharding import PartitionSpec as P

MESH = pl.DeviceIdType.MESH
F32 = jnp.float32
BF16 = jnp.bfloat16

E = 256
FIELDS = 512
ROWS = 512
NF = 128
NL = 384
BAG = 4
SAMPLES = 4
SLOTS = 16
GROUP_B = 128
EMB = 32
XS = 4
YS = 4
ZS = 4
SLICE = 1024
TH = 512
TILES = 8
NROW = SAMPLES * NF
norm_eps = 1e-05


def dot(a, b, ca=1, cb=0):
    return lax.dot_general(a, b, (((ca,), (cb,)), ((), ())), preferred_element_type=F32)


def send(src, dst, send_sem, recv_sem, **device):
    return pltpu.make_async_remote_copy(
        src_ref=src,
        dst_ref=dst,
        send_sem=send_sem,
        recv_sem=recv_sem,
        device_id=device,
        device_id_type=MESH,
    )


def signal(sem, **device):
    pl.semaphore_signal(sem, inc=1, device_id=device, device_id_type=MESH)


def norm_forward(values):
    centre = jnp.mean(values, axis=-1, keepdims=True)
    shifted = values - centre
    scale = lax.rsqrt(jnp.mean(shifted * shifted, axis=-1, keepdims=True) + norm_eps)
    return shifted * scale, scale


def norm_back(unit, scale, gain, upstream):
    scaled = upstream * gain
    return scale * (
        scaled
        - jnp.mean(scaled, axis=-1, keepdims=True)
        - unit * jnp.mean(scaled * unit, axis=-1, keepdims=True)
    )


def layer_kernel(
    ids, lengths, field_row, field_column, fm_gain, out_gain,
    tables, w_up_hbm, w_down_hbm, proj_y_hbm, proj_p_hbm, linear_w_hbm, cotangent_hbm,
    layer_out_hbm, bag_grads, whole,
    pooled, outgoing, slots, w_up, w_down, proj_y, proj_p, linear_w, cotangent, layer_out,
    embeds, crossed, mixing, inter_unit, inter_scale, rows, rows_t, hidden, slope, ff, ff_out, ff_in,
    linear_out, grad_summed, grad_rows, grad_rows_t, grad_lin, norm_out, norm_in,
    slot_grads, grads, from_core, to_x, from_x, to_y, from_y, to_z, from_z,
    table_sem, local_sem, bag_send, bag_recv, back_send, back_recv, w_send, w_recv, pair_send, pair_recv,
    core_send, core_recv, sum_send, sum_recv,
):
    me = lax.axis_index("emb")
    wide = lax.axis_index("wide")
    x = wide // 2
    z_lo = lax.rem(wide, 2)
    partner = wide + 1 - 2 * z_lo
    core = lax.rem(me, 2)
    y = lax.rem(me // 2, YS)
    z = me // (2 * YS)
    sibling = me + 1 - 2 * core

    def x_at(offset):
        return lax.rem(x + XS + offset, XS)

    def wide_at(x_to):
        return x_to * 2 + z_lo

    def emb_at(z_to, y_to):
        return (z_to * YS + y_to) * 2 + core

    def table(s):
        return hidden.at[s // TILES, s % TILES, :, pl.ds(0, E)]

    def fetch(s):
        return pltpu.make_async_copy(tables.at[s], table(s), table_sem.at[s])

    for s in range(SLOTS):
        fetch(s).start()
    staged = [
        pltpu.make_async_copy(src, dst, local_sem.at[n])
        for n, (src, dst) in enumerate(
            (
                (w_up_hbm, w_up.at[x]),
                (w_down_hbm, w_down.at[x]),
                (proj_y_hbm, proj_y),
                (proj_p_hbm, proj_p),
                (linear_w_hbm, linear_w),
                (cotangent_hbm, cotangent),
            )
        )
    ]
    for copy in staged:
        copy.start()

    barrier = pltpu.get_barrier_semaphore()

    @pl.loop(1, EMB)
    def _(k):
        signal(barrier, emb=lax.rem(me + k, EMB))

    for k in range(1, XS):
        signal(barrier, wide=wide_at(x_at(k)))
    signal(barrier, wide=partner)
    pl.semaphore_wait(barrier, EMB - 1 + XS)

    weights = ((w_up_hbm, w_up), (w_down_hbm, w_down))
    for k in range(1, XS):
        for i, (w, full) in enumerate(weights):
            send(w, full.at[x], w_send.at[i, k - 1], w_recv.at[i, k - 1], wide=wide_at(x_at(k))).start()

    def weights_from(k):
        if k == 0:
            staged[0].wait()
            staged[1].wait()
            return
        for i, (w, full) in enumerate(weights):
            copy = send(
                w, full.at[x_at(-k)], w_send.at[i, k - 1], w_recv.at[i, k - 1], wide=wide_at(x_at(-k))
            )
            copy.wait_recv()
            copy.wait_send()

    bucket = lax.broadcasted_iota(jnp.int32, (ROWS, GROUP_B), 0)

    for s in range(SLOTS):
        fetch(s).wait()
        live = lengths[s : s + 1, :]
        counts = jnp.zeros((ROWS, GROUP_B), F32)
        for j in range(BAG):
            wanted = jnp.where(live > j, ids[s, j : j + 1, :], -1)
            counts = counts + jnp.where(bucket == wanted, 1.0, 0.0)
        bags = dot(counts.astype(BF16), table(s)[...], 0, 0)
        for half in range(2):
            pooled[half, pl.ds(s, GROUP_B, stride=SLOTS), :] = bags[:, half * 128 : half * 128 + 128]

    for half in range(2):
        outgoing[:, :, half * 128 : half * 128 + 128] = (
            pooled[half].astype(BF16).reshape(GROUP_B, SLOTS, 128)
        )

    def slots_at(owner):
        return pl.ds(pl.multiple_of(owner * SLOTS, SLOTS), SLOTS)

    def samples_at(owner):
        return pl.ds(owner * SAMPLES, SAMPLES)

    @pl.loop(1, EMB)
    def _(k):
        peer = lax.rem(me + k, EMB)
        send(
            outgoing.at[samples_at(peer)], slots.at[:, slots_at(me), :], bag_send.at[k], bag_recv.at[k], emb=peer
        ).start()

    slots[:, slots_at(me), :] = outgoing[samples_at(me)]

    by_field = jnp.where(
        lax.broadcasted_iota(jnp.int32, (FIELDS, FIELDS), 0) == field_row[...], 1.0, 0.0
    ).astype(BF16)
    for copy in staged[2:]:
        copy.wait()

    @pl.loop(1, EMB)
    def _(k):
        source = lax.rem(me + EMB - k, EMB)
        copy = send(
            outgoing.at[samples_at(source)],
            slots.at[:, slots_at(source), :],
            bag_send.at[k],
            bag_recv.at[k],
            emb=source,
        )
        copy.wait_recv()
        copy.wait_send()

    def exchange(src, dst, n):
        return send(src, dst, pair_send.at[n], pair_recv.at[n], wide=partner)

    def rows_of(b):
        return pl.ds(pl.multiple_of(b * NF, NF), NF)

    def embed(b, _):
        sample = dot(by_field, slots[b]).astype(BF16)
        embeds[b] = sample
        cross = dot(sample, proj_y[...], 0, 0).astype(BF16)
        crossed[b] = cross
        mix = dot(proj_p[...], sample).astype(BF16)
        mixing[b] = mix
        unit, scale = norm_forward(dot(mix, cross))
        inter_unit[b] = unit
        inter_scale[b] = jnp.broadcast_to(scale, (NF, 128))
        rows[0, rows_of(b), :] = (unit * fm_gain[...]).astype(BF16)
        return 0

    lax.fori_loop(0, SAMPLES, embed, 0)
    rows_copy = exchange(rows.at[0], rows.at[1], 0)
    rows_copy.start()
    ff[...] = jnp.zeros_like(ff)

    def forward(group, k):
        chunk = x_at(-k)

        @pl.loop(0, 2)
        def _(t):
            tile = chunk * 2 + t
            here = pl.ds(pl.multiple_of(t * TH, TH), TH)
            gate = dot(rows[group], w_up[chunk, here, :], 1, 1)
            sigma = 0.5 * jnp.tanh(0.5 * gate) + 0.5
            act = gate * sigma
            slope[group, tile] = (sigma + act * (1.0 - sigma)).astype(BF16)
            act = act.astype(BF16)
            hidden[group, tile] = act
            ff[group] += dot(act, w_down[chunk, here, :])

    weights_from(0)
    forward(0, 0)

    def linear(b, _):
        linear_out[b] = dot(linear_w[...], embeds[b])
        return 0

    lax.fori_loop(0, SAMPLES, linear, 0)
    rows_copy.wait()
    forward(1, 0)
    for k in range(1, XS):
        weights_from(k)
        forward(1, k)
    ff_out[...] = ff[1].astype(BF16)
    ff_copy = exchange(ff_out, ff_in, 1)
    ff_copy.start()
    for k in range(1, XS):
        forward(0, k)
    rows_t[0] = rows[0].astype(F32).T.astype(BF16)
    rows_t[1] = rows[1].astype(F32).T.astype(BF16)
    ff_copy.wait()

    def finish(values, b, first, count):
        here = slice(first, first + count)
        unit, scale = norm_forward(values + embeds[b, here, :].astype(F32))
        layer_out[b, here, :] = (unit * out_gain[...]).astype(BF16)
        grad = norm_back(unit, scale, out_gain[...], cotangent[b, here, :].astype(F32))
        grad_summed[b, here, :] = grad
        return grad.astype(BF16)

    def finish_ff(b, _):
        total = ff[0, rows_of(b), :] + ff_in[rows_of(b), :].astype(F32)
        grad_rows[0, rows_of(b), :] = finish(total, b, 0, NF)
        return 0

    lax.fori_loop(0, SAMPLES, finish_ff, 0)
    grad_copy = exchange(grad_rows.at[0], grad_rows.at[1], 2)
    grad_copy.start()

    def finish_linear(b, _):
        grad_lin[b] = finish(linear_out[b], b, NF, NL)
        grad_summed[b] += dot(linear_w[...], grad_lin[b], 0, 0)
        return 0

    lax.fori_loop(0, SAMPLES, finish_linear, 0)
    layer_copy = pltpu.make_async_copy(layer_out, layer_out_hbm, local_sem.at[6])
    layer_copy.start()
    grad_rows_t[0] = grad_rows[0].astype(F32).T.astype(BF16)
    ff[...] = jnp.zeros_like(ff)
    grad_copy.wait()
    grad_rows_t[1] = grad_rows[1].astype(F32).T.astype(BF16)

    def gate_back(group, chunk, t):
        here = pl.ds(pl.multiple_of(t * TH, TH), TH)
        tile = chunk * 2 + t
        grad_hidden = dot(grad_rows[group], w_down[chunk, here, :], 1, 1)
        grad_gate = (grad_hidden * slope[group, tile].astype(F32)).astype(BF16)
        ff[group] += dot(grad_gate, w_up[chunk, here, :])
        return grad_gate

    @pl.loop(0, TILES)
    def _(tile):
        slope[1, tile] = gate_back(1, tile // 2, lax.rem(tile, 2))

    norm_out[...] = ff[1].astype(BF16)
    norm_copy = exchange(norm_out, norm_in, 3)
    norm_copy.start()

    def over_cores(k):
        chunk = pl.ds(x_at(k) * 4, 4)
        return send(
            grads.at[1 - core, chunk], from_core.at[chunk], core_send.at[k], core_recv.at[k], emb=sibling
        )

    def over_x(k):
        return send(
            to_x.at[pl.ds(x_at(k) * 4, 4)],
            from_x.at[k - 1],
            sum_send.at[k],
            sum_recv.at[k],
            wide=wide_at(x_at(k)),
        )

    def pass_on(k):
        over_cores(k).wait()

        @pl.loop(0, 4)
        def _(t):
            part = x_at(k) * 4 + t
            to_x[part] = (grads[core, part].astype(F32) + from_core[part].astype(F32)).astype(BF16)

        over_x(k).start()

    order = (1, 2, 3, 0)
    for n, k in enumerate(order):
        chunk = x_at(k)

        @pl.loop(0, 2)
        def _(t):
            tile = chunk * 2 + t
            grad_gate = gate_back(0, chunk, t)
            up = dot(rows_t[0], grad_gate) + dot(rows_t[1], slope[1, tile])
            down = dot(grad_rows_t[0], hidden[0, tile]) + dot(grad_rows_t[1], hidden[1, tile])
            for kind, part in enumerate((up, down)):
                part = part.astype(BF16)
                for half in range(2):
                    grads[kind, tile * 2 + half] = part[:, half * 256 : half * 256 + 256]

        over_cores(k).start()
        if n:
            pass_on(order[n - 1])

    norm_copy.wait()

    by_slot = jnp.where(
        lax.broadcasted_iota(jnp.int32, (FIELDS, FIELDS), 1) == field_column[...], 1.0, 0.0
    ).astype(BF16)

    def tail(b, _):
        upstream = ff[0, rows_of(b), :] + norm_in[rows_of(b), :].astype(F32)
        grad_inter = norm_back(inter_unit[b], inter_scale[b, :, 0:1], fm_gain[...], upstream).astype(BF16)
        grad_mixing = dot(grad_inter, crossed[b], 1, 1).astype(BF16)
        grad_crossed = dot(mixing[b], grad_inter, 0, 0).astype(BF16)
        total = grad_summed[b] + dot(proj_p[...], grad_mixing, 0, 0)
        total = total + dot(proj_y[...], grad_crossed, 1, 1)
        slot_grads[b] = dot(by_slot, total.astype(BF16)).astype(BF16)
        return 0

    lax.fori_loop(0, SAMPLES, tail, 0)

    @pl.loop(1, EMB)
    def _(k):
        peer = lax.rem(me + k, EMB)
        send(
            slot_grads.at[:, slots_at(peer), :],
            bag_grads.at[samples_at(me)],
            back_send.at[k],
            back_recv.at[k],
            emb=peer,
        ).start()

    own_bags = pltpu.make_async_copy(
        slot_grads.at[:, slots_at(me), :], bag_grads.at[samples_at(me)], local_sem.at[7]
    )
    own_bags.start()

    over_cores(0).wait()
    for k in range(1, XS):
        over_x(k).wait()

    @pl.loop(0, 4)
    def _(t):
        mine = x * 4 + t
        total = grads[core, mine].astype(F32) + from_core[mine].astype(F32)
        for k in range(XS - 1):
            total = total + from_x[k, t].astype(F32)
        to_y[t] = total.astype(BF16)

    def over_y(k):
        peer = lax.rem(y + k, YS)
        return send(
            to_y.at[peer], from_y.at[k - 1], sum_send.at[3 + k], sum_recv.at[3 + k], emb=emb_at(z, peer)
        )

    for k in range(1, YS):
        over_y(k).start()
    for k in range(1, YS):
        over_y(k).wait()

    total = to_y[y].astype(F32)
    for k in range(YS - 1):
        total = total + from_y[k].astype(F32)
    for part in range(ZS):
        to_z[part] = total[
            (part % 2) * 128 : (part % 2) * 128 + 128, (part // 2) * 128 : (part // 2) * 128 + 128
        ].astype(BF16)

    def over_z(k):
        peer = lax.rem(z + k, ZS)
        return send(
            to_z.at[peer], from_z.at[k - 1], sum_send.at[6 + k], sum_recv.at[6 + k], emb=emb_at(peer, y)
        )

    for k in range(1, ZS):
        over_z(k).start()
    for k in range(1, ZS):
        over_z(k).wait()

    total = to_z[z].astype(F32)
    for k in range(ZS - 1):
        total = total + from_z[k].astype(F32)

    def piece(z_of):
        row = pl.multiple_of(y * 256 + (z_of // 2) * 128, 128)
        column = pl.multiple_of(lax.rem(z_of, 2) * 128, 128)
        return whole.at[core, pl.ds(row, 128), pl.ds(column, 128)]

    row = pl.multiple_of(y * 256 + (z // 2) * 128, 128)
    column = pl.multiple_of(lax.rem(z, 2) * 128, 128)
    whole[core, pl.ds(row, 128), pl.ds(column, 128)] = total.T.astype(BF16)

    def spread(src, dst, n, peer):
        return send(src, dst, sum_send.at[n], sum_recv.at[n], emb=peer)

    for k in range(1, ZS):
        spread(piece(z), piece(z), 9 + k, emb_at(lax.rem(z + k, ZS), y)).start()
    for k in range(1, ZS):
        source = lax.rem(z + ZS - k, ZS)
        spread(piece(z), piece(source), 9 + k, emb_at(source, y)).wait()

    def band(y_of):
        return whole.at[core, pl.ds(pl.multiple_of(y_of * 256, 256), 256), :]

    for k in range(1, YS):
        spread(band(y), band(y), 12 + k, emb_at(z, lax.rem(y + k, YS))).start()
    for k in range(1, YS):
        source = lax.rem(y + YS - k, YS)
        spread(band(y), band(source), 12 + k, emb_at(z, source)).wait()

    spread(whole.at[core], whole.at[core], 16, sibling).start()
    spread(whole.at[core], whole.at[1 - core], 16, sibling).wait()

    @pl.loop(1, EMB)
    def _(k):
        source = lax.rem(me + EMB - k, EMB)
        copy = send(
            slot_grads.at[:, slots_at(source), :],
            bag_grads.at[samples_at(source)],
            back_send.at[k],
            back_recv.at[k],
            emb=source,
        )
        copy.wait_recv()
        copy.wait_send()

    own_bags.wait()
    layer_copy.wait()


def whole_layer(*operands):
    anywhere = pl.BlockSpec(memory_space=pl.ANY)
    vmem = pl.BlockSpec(memory_space=pltpu.VMEM)
    dma = pltpu.SemaphoreType.DMA
    return pl.pallas_call(
        layer_kernel,
        name="whole_layer",
        out_shape=(
            jax.ShapeDtypeStruct((SAMPLES, FIELDS, E), BF16),
            jax.ShapeDtypeStruct((GROUP_B, SLOTS, E), BF16),
            jax.ShapeDtypeStruct((2, SLICE, E), BF16),
        ),
        in_specs=[vmem] * 6 + [anywhere] * 7,
        out_specs=(anywhere, anywhere, vmem),
        scratch_shapes=[
            pltpu.VMEM((2, GROUP_B * SLOTS, 128), F32),
            pltpu.VMEM((GROUP_B, SLOTS, E), BF16),
            pltpu.VMEM((SAMPLES, FIELDS, E), BF16),
            pltpu.VMEM((XS, SLICE, E), BF16),
            pltpu.VMEM((XS, SLICE, E), BF16),
            pltpu.VMEM((FIELDS, E), BF16),
            pltpu.VMEM((NF, FIELDS), BF16),
            pltpu.VMEM((NL, FIELDS), BF16),
            pltpu.VMEM((SAMPLES, FIELDS, E), BF16),
            pltpu.VMEM((SAMPLES, FIELDS, E), BF16),
            pltpu.VMEM((SAMPLES, FIELDS, E), BF16),
            pltpu.VMEM((SAMPLES, E, E), BF16),
            pltpu.VMEM((SAMPLES, NF, E), BF16),
            pltpu.VMEM((SAMPLES, NF, E), F32),
            pltpu.VMEM((SAMPLES, NF, 128), F32),
            pltpu.VMEM((2, NROW, E), BF16),
            pltpu.VMEM((2, E, NROW), BF16),
            pltpu.VMEM((2, TILES, NROW, TH), BF16),
            pltpu.VMEM((2, TILES, NROW, TH), BF16),
            pltpu.VMEM((2, NROW, E), F32),
            pltpu.VMEM((NROW, E), BF16),
            pltpu.VMEM((NROW, E), BF16),
            pltpu.VMEM((SAMPLES, NL, E), F32),
            pltpu.VMEM((SAMPLES, FIELDS, E), F32),
            pltpu.VMEM((2, NROW, E), BF16),
            pltpu.VMEM((2, E, NROW), BF16),
            pltpu.VMEM((SAMPLES, NL, E), BF16),
            pltpu.VMEM((NROW, E), BF16),
            pltpu.VMEM((NROW, E), BF16),
            pltpu.VMEM((SAMPLES, FIELDS, E), BF16),
            pltpu.VMEM((2, TILES * 2, 256, 256), BF16),
            pltpu.VMEM((TILES * 2, 256, 256), BF16),
            pltpu.VMEM((TILES * 2, 256, 256), BF16),
            pltpu.VMEM((XS - 1, 4, 256, 256), BF16),
            pltpu.VMEM((YS, 256, 256), BF16),
            pltpu.VMEM((YS - 1, 256, 256), BF16),
            pltpu.VMEM((ZS, 128, 128), BF16),
            pltpu.VMEM((ZS - 1, 128, 128), BF16),
            dma((SLOTS,)),
            dma((8,)),
            dma((EMB,)),
            dma((EMB,)),
            dma((EMB,)),
            dma((EMB,)),
            dma((2, XS - 1)),
            dma((2, XS - 1)),
            dma((4,)),
            dma((4,)),
            dma((XS,)),
            dma((XS,)),
            dma((17,)),
            dma((17,)),
        ],
        compiler_params=pltpu.CompilerParams(
            collective_id=0, has_side_effects=True, vmem_limit_bytes=62 << 20
        ),
    )(*operands)


def body(
    tables,
    bag_ids,
    bag_lengths,
    slot_field,
    proj_y,
    proj_p,
    linear_w,
    fm_gain,
    w_up,
    w_down,
    out_gain,
    cotangent,
):
    layer_out, bag_grads, weight_grads = whole_layer(
        bag_ids[0].transpose(1, 2, 0),
        bag_lengths[0].transpose(1, 0),
        slot_field.reshape(1, FIELDS),
        slot_field.reshape(FIELDS, 1),
        fm_gain.reshape(1, E),
        out_gain.reshape(1, E),
        tables,
        w_up,
        w_down,
        proj_y,
        proj_p,
        linear_w,
        cotangent[0],
    )
    return (
        layer_out[None],
        bag_grads[None],
        weight_grads[0].astype(F32),
        weight_grads[1].astype(F32),
    )


def solution(mesh):
    placed = (
        P("emb", None, None),
        P("wide", None, "emb", None),
        P("wide", None, "emb"),
        P(),
        P(),
        P(),
        P(),
        P(),
        P("wide", None),
        P("wide", None),
        P(),
        P("wide", "emb", None, None),
    )
    return jax.shard_map(
        body,
        mesh=mesh,
        in_specs=placed,
        out_specs=(
            P("wide", "emb", None, None),
            P("wide", None, "emb", None),
            P("wide", None),
            P("wide", None),
        ),
        check_vma=False,
    )
```

```python
import functools

import jax
import jax.numpy as jnp
from jax import lax
from jax.experimental import pallas as pl
from jax.experimental.pallas import tpu as pltpu
from jax.sharding import PartitionSpec as P

MESH = pl.DeviceIdType.MESH
F32 = jnp.float32
BF16 = jnp.bfloat16

E = 256
FIELDS = 512
ROWS = 512
NF = 128
NL = 384
BAG = 4
SAMPLES = 4
SLOTS = 16
GROUP_B = 128
EMB = 32
XS = 4
YS = 4
ZS = 4
SLICE = 1024
TH = 512
TILES = 8
NROW = SAMPLES * NF
norm_eps = 1e-05


def dot(a, b, ca=1, cb=0):
    return lax.dot_general(a, b, (((ca,), (cb,)), ((), ())), preferred_element_type=F32)


def send(src, dst, send_sem, recv_sem, **device):
    return pltpu.make_async_remote_copy(
        src_ref=src,
        dst_ref=dst,
        send_sem=send_sem,
        recv_sem=recv_sem,
        device_id=device,
        device_id_type=MESH,
    )


def signal(sem, **device):
    pl.semaphore_signal(sem, inc=1, device_id=device, device_id_type=MESH)


def norm_forward(values):
    centre = jnp.mean(values, axis=-1, keepdims=True)
    shifted = values - centre
    scale = lax.rsqrt(jnp.mean(shifted * shifted, axis=-1, keepdims=True) + norm_eps)
    return shifted * scale, scale


def norm_back(unit, scale, gain, upstream):
    scaled = upstream * gain
    return scale * (
        scaled
        - jnp.mean(scaled, axis=-1, keepdims=True)
        - unit * jnp.mean(scaled * unit, axis=-1, keepdims=True)
    )


def layer_kernel(
    ids, lengths, field_row, fm_gain, out_gain,
    tables, w_up_hbm, w_down_hbm, proj_y_hbm, proj_p_hbm, linear_w_hbm, cotangent_hbm,
    layer_out_hbm, bag_grads, whole,
    pooled, outgoing, slots, w_up, w_down, proj_y, proj_p, linear_w, cotangent, layer_out,
    embeds, crossed, mixing, inter_unit, inter_scale, rows, rows_t, hidden, slope, ff, ff_out, ff_in,
    by_slot, linear_out, grad_summed, grad_rows, grad_rows_t, grad_lin, norm_out, norm_in,
    slot_grads, grads, from_core, to_x, from_x, to_y, from_y, to_z, from_z, done_z,
    table_sem, local_sem, bag_send, bag_recv, back_send, back_recv, w_send, w_recv, pair_send, pair_recv,
    core_send, core_recv, sum_send, sum_recv,
):
    me = lax.axis_index("emb")
    wide = lax.axis_index("wide")
    x = wide // 2
    z_lo = lax.rem(wide, 2)
    partner = wide + 1 - 2 * z_lo
    core = lax.rem(me, 2)
    y = lax.rem(me // 2, YS)
    z = me // (2 * YS)
    sibling = me + 1 - 2 * core

    def x_at(offset):
        return lax.rem(x + XS + offset, XS)

    def wide_at(x_to):
        return x_to * 2 + z_lo

    def emb_at(z_to, y_to):
        return (z_to * YS + y_to) * 2 + core

    def table(s):
        return hidden.at[s // TILES, s % TILES, :, pl.ds(0, E)]

    def fetch(s):
        return pltpu.make_async_copy(tables.at[s], table(s), table_sem.at[s])

    for s in range(SLOTS):
        fetch(s).start()
    staged = [
        pltpu.make_async_copy(src, dst, local_sem.at[n])
        for n, (src, dst) in enumerate(
            (
                (w_up_hbm, w_up.at[x]),
                (w_down_hbm, w_down.at[x]),
                (proj_y_hbm, proj_y),
                (proj_p_hbm, proj_p),
                (linear_w_hbm, linear_w),
                (cotangent_hbm, cotangent),
            )
        )
    ]
    for copy in staged:
        copy.start()

    barrier = pltpu.get_barrier_semaphore()

    @pl.loop(1, EMB)
    def _(k):
        signal(barrier, emb=lax.rem(me + k, EMB))

    for k in range(1, XS):
        signal(barrier, wide=wide_at(x_at(k)))
    signal(barrier, wide=partner)
    pl.semaphore_wait(barrier, EMB - 1 + XS)

    def half_of(which):
        return pl.ds(pl.multiple_of(which * TH, TH), TH)

    weights = ((w_up_hbm, w_up), (w_down_hbm, w_down))
    for k in range(1, XS):
        for i, (w, full) in enumerate(weights):
            send(
                w.at[half_of(core)],
                full.at[x, half_of(core)],
                w_send.at[i, k - 1],
                w_recv.at[i, k - 1],
                wide=wide_at(x_at(k)),
            ).start()

    def weights_from(k):
        if k == 0:
            staged[0].wait()
            staged[1].wait()
            return
        for i, (w, full) in enumerate(weights):
            pass_weights(i, k, 1 - core).wait_recv()
            pass_weights(i, k, core).wait_send()

    def pass_weights(i, k, which):
        part = weights[i][1].at[x_at(-k), half_of(which)]
        return send(part, part, w_send.at[2 + i, k - 1], w_recv.at[2 + i, k - 1], emb=sibling)

    bucket = lax.broadcasted_iota(jnp.int32, (ROWS, GROUP_B), 0)

    for s in range(SLOTS):
        fetch(s).wait()
        live = lengths[s : s + 1, :]
        counts = jnp.zeros((ROWS, GROUP_B), F32)
        for j in range(BAG):
            wanted = jnp.where(live > j, ids[s, j : j + 1, :], -1)
            counts = counts + jnp.where(bucket == wanted, 1.0, 0.0)
        bags = dot(counts.astype(BF16), table(s)[...], 0, 0)
        for half in range(2):
            pooled[half, pl.ds(s, GROUP_B, stride=SLOTS), :] = bags[:, half * 128 : half * 128 + 128]

    for half in range(2):
        outgoing[:, :, half * 128 : half * 128 + 128] = (
            pooled[half].astype(BF16).reshape(GROUP_B, SLOTS, 128)
        )

    def slots_at(owner):
        return pl.ds(pl.multiple_of(owner * SLOTS, SLOTS), SLOTS)

    def samples_at(owner):
        return pl.ds(owner * SAMPLES, SAMPLES)

    @pl.loop(1, EMB)
    def _(k):
        peer = lax.rem(me + k, EMB)
        send(
            outgoing.at[samples_at(peer)], slots.at[:, slots_at(me), :], bag_send.at[k], bag_recv.at[k], emb=peer
        ).start()

    slots[:, slots_at(me), :] = outgoing[samples_at(me)]

    by_field = jnp.where(
        lax.broadcasted_iota(jnp.int32, (FIELDS, FIELDS), 0) == field_row[...], 1.0, 0.0
    ).astype(BF16)
    by_slot[...] = by_field.astype(F32).T.astype(BF16)
    for copy in staged[2:]:
        copy.wait()

    for k in (1, 3, 2):
        for i, (w, full) in enumerate(weights):
            copy = send(
                w.at[half_of(core)],
                full.at[x_at(-k), half_of(core)],
                w_send.at[i, k - 1],
                w_recv.at[i, k - 1],
                wide=wide_at(x_at(-k)),
            )
            copy.wait_recv()
            copy.wait_send()
            pass_weights(i, k, core).start()

    @pl.loop(1, EMB)
    def _(k):
        source = lax.rem(me + EMB - k, EMB)
        copy = send(
            outgoing.at[samples_at(source)],
            slots.at[:, slots_at(source), :],
            bag_send.at[k],
            bag_recv.at[k],
            emb=source,
        )
        copy.wait_recv()
        copy.wait_send()

    def exchange(src, dst, n):
        return send(src, dst, pair_send.at[n], pair_recv.at[n], wide=partner)

    def rows_of(b):
        return pl.ds(pl.multiple_of(b * NF, NF), NF)

    def embed(b, _):
        sample = dot(by_field, slots[b]).astype(BF16)
        embeds[b] = sample
        cross = dot(sample, proj_y[...], 0, 0).astype(BF16)
        crossed[b] = cross
        mix = dot(proj_p[...], sample).astype(BF16)
        mixing[b] = mix
        unit, scale = norm_forward(dot(mix, cross))
        inter_unit[b] = unit
        inter_scale[b] = jnp.broadcast_to(scale, (NF, 128))
        rows[0, rows_of(b), :] = (unit * fm_gain[...]).astype(BF16)
        return 0

    lax.fori_loop(0, SAMPLES, embed, 0)
    rows_copy = exchange(rows.at[0], rows.at[1], 0)
    rows_copy.start()
    ff[...] = jnp.zeros_like(ff)

    def forward(group, k):
        chunk = x_at(-k)

        @pl.loop(0, 2)
        def _(t):
            tile = chunk * 2 + t
            here = pl.ds(pl.multiple_of(t * TH, TH), TH)
            gate = dot(rows[group], w_up[chunk, here, :], 1, 1)
            sigma = 0.5 * jnp.tanh(0.5 * gate) + 0.5
            act = gate * sigma
            slope[group, tile] = (sigma + act * (1.0 - sigma)).astype(BF16)
            act = act.astype(BF16)
            hidden[group, tile] = act
            ff[group] += dot(act, w_down[chunk, here, :])

    weights_from(0)
    forward(0, 0)

    def linear(b, _):
        linear_out[b] = dot(linear_w[...], embeds[b])
        return 0

    lax.fori_loop(0, SAMPLES, linear, 0)
    rows_copy.wait()
    forward(1, 0)
    for k in range(1, XS):
        weights_from(k)
        forward(1, k)
    ff_out[...] = ff[1].astype(BF16)
    ff_copy = exchange(ff_out, ff_in, 1)
    ff_copy.start()
    for k in range(1, XS):
        forward(0, k)
    rows_t[0] = rows[0].astype(F32).T.astype(BF16)
    rows_t[1] = rows[1].astype(F32).T.astype(BF16)
    ff_copy.wait()

    def finish(values, b, first, count):
        here = slice(first, first + count)
        unit, scale = norm_forward(values + embeds[b, here, :].astype(F32))
        layer_out[b, here, :] = (unit * out_gain[...]).astype(BF16)
        grad = norm_back(unit, scale, out_gain[...], cotangent[b, here, :].astype(F32))
        grad_summed[b, here, :] = grad
        return grad.astype(BF16)

    def finish_ff(b, _):
        total = ff[0, rows_of(b), :] + ff_in[rows_of(b), :].astype(F32)
        grad_rows[0, rows_of(b), :] = finish(total, b, 0, NF)
        return 0

    lax.fori_loop(0, SAMPLES, finish_ff, 0)
    grad_copy = exchange(grad_rows.at[0], grad_rows.at[1], 2)
    grad_copy.start()

    def finish_linear(b, _):
        grad_lin[b] = finish(linear_out[b], b, NF, NL)
        grad_summed[b] += dot(linear_w[...], grad_lin[b], 0, 0)
        return 0

    lax.fori_loop(0, SAMPLES, finish_linear, 0)
    layer_copy = pltpu.make_async_copy(layer_out, layer_out_hbm, local_sem.at[6])
    layer_copy.start()
    grad_rows_t[0] = grad_rows[0].astype(F32).T.astype(BF16)
    ff[...] = jnp.zeros_like(ff)
    grad_copy.wait()
    grad_rows_t[1] = grad_rows[1].astype(F32).T.astype(BF16)

    def gate_back(group, chunk, t):
        here = pl.ds(pl.multiple_of(t * TH, TH), TH)
        tile = chunk * 2 + t
        grad_hidden = dot(grad_rows[group], w_down[chunk, here, :], 1, 1)
        grad_gate = (grad_hidden * slope[group, tile].astype(F32)).astype(BF16)
        ff[group] += dot(grad_gate, w_up[chunk, here, :])
        return grad_gate

    k_mine = pl.ds(pl.multiple_of(core * 128, 128), 128)
    k_other = pl.ds(pl.multiple_of(128 - core * 128, 128), 128)

    def keep(kind, tile, part):
        part = part.astype(BF16)
        for half in range(2):
            grads[kind, tile * 2 + half] = part[:, half * 256 : half * 256 + 256]

    def over_cores(kind, k):
        chunk = pl.ds(x_at(k) * 4, 4)
        return send(
            grads.at[kind, chunk, k_other],
            from_core.at[kind, chunk],
            core_send.at[kind, k],
            core_recv.at[kind, k],
            emb=sibling,
        )

    def over_x(kind, k):
        return send(
            to_x.at[kind, pl.ds(x_at(k) * 4, 4)],
            from_x.at[kind, k - 1],
            sum_send.at[kind, k],
            sum_recv.at[kind, k],
            wide=wide_at(x_at(k)),
        )

    def over_y(kind, k):
        peer = lax.rem(y + k, YS)
        return send(
            to_y.at[kind, peer],
            from_y.at[kind, k - 1],
            sum_send.at[kind, 3 + k],
            sum_recv.at[kind, 3 + k],
            emb=emb_at(z, peer),
        )

    def over_z(kind, k):
        peer = lax.rem(z + k, ZS)
        return send(
            to_z.at[kind, peer],
            from_z.at[kind, k - 1],
            sum_send.at[kind, 6 + k],
            sum_recv.at[kind, 6 + k],
            emb=emb_at(peer, y),
        )

    def along_z(kind, k, z_of, z_to):
        part = done_z.at[kind, z_of]
        return send(part, part, sum_send.at[kind, 9 + k], sum_recv.at[kind, 9 + k], emb=emb_at(z_to, y))

    def band(kind, y_of, columns):
        return whole.at[kind, pl.ds(pl.multiple_of(y_of * 256, 256), 256), columns]

    def along_y(kind, k, y_of, y_to):
        part = band(kind, y_of, k_mine)
        return send(part, part, sum_send.at[kind, 12 + k], sum_recv.at[kind, 12 + k], emb=emb_at(z, y_to))

    def to_sibling(kind, k, columns):
        part = band(kind, lax.rem(y + YS - k, YS), columns)
        return send(part, part, sum_send.at[kind, 16 + k], sum_recv.at[kind, 16 + k], emb=sibling)

    def pass_on(kind, k):
        over_cores(kind, k).wait()

        @pl.loop(0, 4)
        def _(t):
            part = x_at(k) * 4 + t
            to_x[kind, part] = (
                grads[kind, part, k_mine].astype(F32) + from_core[kind, part].astype(F32)
            ).astype(BF16)

        over_x(kind, k).start()

    def sum_x(kind):
        over_cores(kind, 0).wait()
        for k in range(1, XS):
            over_x(kind, k).wait()

        @pl.loop(0, 4)
        def _(t):
            mine = x * 4 + t
            total = grads[kind, mine, k_mine].astype(F32) + from_core[kind, mine].astype(F32)
            for k in range(XS - 1):
                total = total + from_x[kind, k, t].astype(F32)
            to_y[kind, t] = total.astype(BF16)

        for k in range(1, YS):
            over_y(kind, k).start()

    def sum_y(kind):
        for k in range(1, YS):
            over_y(kind, k).wait()
        total = to_y[kind, y].astype(F32)
        for k in range(YS - 1):
            total = total + from_y[kind, k].astype(F32)
        to_z[kind] = total.astype(BF16).reshape(ZS, 128 // ZS, 256)
        for k in range(1, ZS):
            over_z(kind, k).start()

    def sum_z(kind):
        for k in range(1, ZS):
            over_z(kind, k).wait()
        total = to_z[kind, z].astype(F32)
        for k in range(ZS - 1):
            total = total + from_z[kind, k].astype(F32)
        done_z[kind, z] = total.astype(BF16)
        for k in range(1, ZS):
            along_z(kind, k, z, lax.rem(z + k, ZS)).start()

    def spread_y(kind):
        for k in range(1, ZS):
            source = lax.rem(z + ZS - k, ZS)
            along_z(kind, k, z, source).wait_send()
            along_z(kind, k, source, source).wait_recv()
        part = done_z[kind].reshape(128, 256).astype(F32).T.astype(BF16)
        whole[kind, pl.ds(pl.multiple_of(y * 256, 256), 256), k_mine] = part
        for k in range(1, YS):
            along_y(kind, k, y, lax.rem(y + k, YS)).start()
        to_sibling(kind, 0, k_mine).start()

    def spread_cores(kind):
        for k in range(1, YS):
            source = lax.rem(y + YS - k, YS)
            along_y(kind, k, source, source).wait_recv()
            to_sibling(kind, k, k_mine).start()

    def settle(kind):
        for k in range(1, YS):
            along_y(kind, k, y, lax.rem(y + k, YS)).wait_send()
        for k in range(YS):
            to_sibling(kind, k, k_mine).wait_send()
            to_sibling(kind, k, k_other).wait_recv()

    order = (1, 2, 3, 0)
    for k in order:

        @pl.loop(0, 2)
        def _(t):
            tile = x_at(k) * 2 + t
            keep(1, tile, dot(grad_rows_t[0], hidden[0, tile]) + dot(grad_rows_t[1], hidden[1, tile]))

        over_cores(1, k).start()

    for n, k in enumerate(order):

        @pl.loop(0, 2)
        def _(t):
            slope[1, x_at(k) * 2 + t] = gate_back(1, x_at(k), t)

        if n < 3:
            pass_on(1, k)

    norm_out[...] = ff[1].astype(BF16)
    norm_copy = exchange(norm_out, norm_in, 3)
    norm_copy.start()

    for n, k in enumerate(order):

        @pl.loop(0, 2)
        def _(t):
            tile = x_at(k) * 2 + t
            grad_gate = gate_back(0, x_at(k), t)
            keep(0, tile, dot(rows_t[0], grad_gate) + dot(rows_t[1], slope[1, tile]))

        over_cores(0, k).start()
        if n:
            pass_on(0, order[n - 1])
        (lambda kind: None, sum_x, sum_y, sum_z)[n](1)

    norm_copy.wait()

    def tail(b, _):
        upstream = ff[0, rows_of(b), :] + norm_in[rows_of(b), :].astype(F32)
        grad_inter = norm_back(inter_unit[b], inter_scale[b, :, 0:1], fm_gain[...], upstream).astype(BF16)
        grad_mixing = dot(grad_inter, crossed[b], 1, 1).astype(BF16)
        grad_crossed = dot(mixing[b], grad_inter, 0, 0).astype(BF16)
        total = grad_summed[b] + dot(proj_p[...], grad_mixing, 0, 0)
        total = total + dot(proj_y[...], grad_crossed, 1, 1)
        slot_grads[b] = dot(by_slot[...], total.astype(BF16)).astype(BF16)
        return 0

    lax.fori_loop(0, SAMPLES, tail, 0)

    @pl.loop(1, EMB)
    def _(k):
        peer = lax.rem(me + k, EMB)
        send(
            slot_grads.at[:, slots_at(peer), :],
            bag_grads.at[samples_at(me)],
            back_send.at[k],
            back_recv.at[k],
            emb=peer,
        ).start()

    own_bags = pltpu.make_async_copy(
        slot_grads.at[:, slots_at(me), :], bag_grads.at[samples_at(me)], local_sem.at[7]
    )
    own_bags.start()

    spread_y(1)
    sum_x(0)
    spread_cores(1)
    sum_y(0)
    sum_z(0)
    spread_y(0)
    spread_cores(0)
    settle(1)
    settle(0)

    @pl.loop(1, EMB)
    def _(k):
        source = lax.rem(me + EMB - k, EMB)
        copy = send(
            slot_grads.at[:, slots_at(source), :],
            bag_grads.at[samples_at(source)],
            back_send.at[k],
            back_recv.at[k],
            emb=source,
        )
        copy.wait_recv()
        copy.wait_send()

    own_bags.wait()
    layer_copy.wait()


def whole_layer(*operands):
    anywhere = pl.BlockSpec(memory_space=pl.ANY)
    vmem = pl.BlockSpec(memory_space=pltpu.VMEM)
    dma = pltpu.SemaphoreType.DMA
    return pl.pallas_call(
        layer_kernel,
        name="whole_layer",
        out_shape=(
            jax.ShapeDtypeStruct((SAMPLES, FIELDS, E), BF16),
            jax.ShapeDtypeStruct((GROUP_B, SLOTS, E), BF16),
            jax.ShapeDtypeStruct((2, SLICE, E), BF16),
        ),
        in_specs=[vmem] * 5 + [anywhere] * 7,
        out_specs=(anywhere, anywhere, vmem),
        scratch_shapes=[
            pltpu.VMEM((2, GROUP_B * SLOTS, 128), F32),
            pltpu.VMEM((GROUP_B, SLOTS, E), BF16),
            pltpu.VMEM((SAMPLES, FIELDS, E), BF16),
            pltpu.VMEM((XS, SLICE, E), BF16),
            pltpu.VMEM((XS, SLICE, E), BF16),
            pltpu.VMEM((FIELDS, E), BF16),
            pltpu.VMEM((NF, FIELDS), BF16),
            pltpu.VMEM((NL, FIELDS), BF16),
            pltpu.VMEM((SAMPLES, FIELDS, E), BF16),
            pltpu.VMEM((SAMPLES, FIELDS, E), BF16),
            pltpu.VMEM((SAMPLES, FIELDS, E), BF16),
            pltpu.VMEM((SAMPLES, E, E), BF16),
            pltpu.VMEM((SAMPLES, NF, E), BF16),
            pltpu.VMEM((SAMPLES, NF, E), F32),
            pltpu.VMEM((SAMPLES, NF, 128), F32),
            pltpu.VMEM((2, NROW, E), BF16),
            pltpu.VMEM((2, E, NROW), BF16),
            pltpu.VMEM((2, TILES, NROW, TH), BF16),
            pltpu.VMEM((2, TILES, NROW, TH), BF16),
            pltpu.VMEM((2, NROW, E), F32),
            pltpu.VMEM((NROW, E), BF16),
            pltpu.VMEM((NROW, E), BF16),
            pltpu.VMEM((FIELDS, FIELDS), BF16),
            pltpu.VMEM((SAMPLES, NL, E), F32),
            pltpu.VMEM((SAMPLES, FIELDS, E), F32),
            pltpu.VMEM((2, NROW, E), BF16),
            pltpu.VMEM((2, E, NROW), BF16),
            pltpu.VMEM((SAMPLES, NL, E), BF16),
            pltpu.VMEM((NROW, E), BF16),
            pltpu.VMEM((NROW, E), BF16),
            pltpu.VMEM((SAMPLES, FIELDS, E), BF16),
            pltpu.VMEM((2, TILES * 2, 256, 256), BF16),
            pltpu.VMEM((2, TILES * 2, 128, 256), BF16),
            pltpu.VMEM((2, TILES * 2, 128, 256), BF16),
            pltpu.VMEM((2, XS - 1, 4, 128, 256), BF16),
            pltpu.VMEM((2, YS, 128, 256), BF16),
            pltpu.VMEM((2, YS - 1, 128, 256), BF16),
            pltpu.VMEM((2, ZS, 128 // ZS, 256), BF16),
            pltpu.VMEM((2, ZS - 1, 128 // ZS, 256), BF16),
            pltpu.VMEM((2, ZS, 128 // ZS, 256), BF16),
            dma((SLOTS,)),
            dma((8,)),
            dma((EMB,)),
            dma((EMB,)),
            dma((EMB,)),
            dma((EMB,)),
            dma((4, XS - 1)),
            dma((4, XS - 1)),
            dma((4,)),
            dma((4,)),
            dma((2, XS)),
            dma((2, XS)),
            dma((2, 20)),
            dma((2, 20)),
        ],
        compiler_params=pltpu.CompilerParams(
            collective_id=0, has_side_effects=True, vmem_limit_bytes=62 << 20
        ),
    )(*operands)


def finish_kernel(layer_out, bag_grads, whole, layer_final, bag_final, up, down, up_held, down_held, sem):
    first = pltpu.make_async_copy(layer_out, layer_final, sem.at[0])
    second = pltpu.make_async_copy(bag_grads, bag_final, sem.at[1])
    first.start()
    second.start()
    up_held[...] = whole[0].astype(F32)
    up_copy = pltpu.make_async_copy(up_held, up, sem.at[2])
    up_copy.start()
    down_held[...] = whole[1].astype(F32)
    down_copy = pltpu.make_async_copy(down_held, down, sem.at[3])
    down_copy.start()
    for copy in (first, second, up_copy, down_copy):
        copy.wait()


def finish_outputs(layer_out, bag_grads, whole):
    anywhere = pl.BlockSpec(memory_space=pl.ANY)
    return pl.pallas_call(
        finish_kernel,
        name="finish_outputs",
        out_shape=(
            jax.ShapeDtypeStruct(layer_out.shape, BF16),
            jax.ShapeDtypeStruct(bag_grads.shape, BF16),
            jax.ShapeDtypeStruct((SLICE, E), F32),
            jax.ShapeDtypeStruct((SLICE, E), F32),
        ),
        in_specs=[anywhere, anywhere, pl.BlockSpec(memory_space=pltpu.VMEM)],
        out_specs=(anywhere,) * 4,
        scratch_shapes=[
            pltpu.VMEM((SLICE, E), F32),
            pltpu.VMEM((SLICE, E), F32),
            pltpu.SemaphoreType.DMA((4,)),
        ],
    )(layer_out, bag_grads, whole)


def body(
    tables,
    bag_ids,
    bag_lengths,
    slot_field,
    proj_y,
    proj_p,
    linear_w,
    fm_gain,
    w_up,
    w_down,
    out_gain,
    cotangent,
):
    layer_out, bag_grads, weight_grads = whole_layer(
        bag_ids[0].transpose(1, 2, 0),
        bag_lengths[0].transpose(1, 0),
        slot_field.reshape(1, FIELDS),
        fm_gain.reshape(1, E),
        out_gain.reshape(1, E),
        tables,
        w_up,
        w_down,
        proj_y,
        proj_p,
        linear_w,
        cotangent[0],
    )
    layer_out, bag_grads, grad_up, grad_down = finish_outputs(layer_out, bag_grads, weight_grads)
    return (layer_out[None], bag_grads[None], grad_up, grad_down)


def solution(mesh):
    placed = (
        P("emb", None, None),
        P("wide", None, "emb", None),
        P("wide", None, "emb"),
        P(),
        P(),
        P(),
        P(),
        P(),
        P("wide", None),
        P("wide", None),
        P(),
        P("wide", "emb", None, None),
    )
    return jax.shard_map(
        body,
        mesh=mesh,
        in_specs=placed,
        out_specs=(
            P("wide", "emb", None, None),
            P("wide", None, "emb", None),
            P("wide", None),
            P("wide", None),
        ),
        check_vma=False,
    )
```

```python
import functools

import jax
import jax.numpy as jnp
from jax import lax
from jax.experimental import pallas as pl
from jax.experimental.pallas import tpu as pltpu
from jax.sharding import PartitionSpec as P

MESH = pl.DeviceIdType.MESH
F32 = jnp.float32
BF16 = jnp.bfloat16

E = 256
FIELDS = 512
ROWS = 512
NF = 128
NL = 384
BAG = 4
SAMPLES = 4
SLOTS = 16
GROUP_B = 128
EMB = 32
XS = 4
YS = 4
ZS = 4
PIECES = YS * ZS
PIECE = 32
SLICE = 1024
TH = 512
TILES = 8
NROW = SAMPLES * NF
norm_eps = 1e-05


def dot(a, b, ca=1, cb=0):
    return lax.dot_general(a, b, (((ca,), (cb,)), ((), ())), preferred_element_type=F32)


def send(src, dst, send_sem, recv_sem, **device):
    return pltpu.make_async_remote_copy(
        src_ref=src,
        dst_ref=dst,
        send_sem=send_sem,
        recv_sem=recv_sem,
        device_id=device,
        device_id_type=MESH,
    )


def signal(sem, **device):
    pl.semaphore_signal(sem, inc=1, device_id=device, device_id_type=MESH)


def norm_forward(values):
    centre = jnp.mean(values, axis=-1, keepdims=True)
    shifted = values - centre
    scale = lax.rsqrt(jnp.mean(shifted * shifted, axis=-1, keepdims=True) + norm_eps)
    return shifted * scale, scale


def norm_back(unit, scale, gain, upstream):
    scaled = upstream * gain
    return scale * (
        scaled
        - jnp.mean(scaled, axis=-1, keepdims=True)
        - unit * jnp.mean(scaled * unit, axis=-1, keepdims=True)
    )


def layer_kernel(
    ids, lengths, field_row, fm_gain, out_gain,
    tables, w_up_hbm, w_down_hbm, proj_y_hbm, proj_p_hbm, linear_w_hbm, cotangent_hbm,
    layer_out_hbm, bag_grads, done,
    pooled, outgoing, slots, w_up, w_down, proj_y, proj_p, linear_w, cotangent, layer_out,
    embeds, crossed, mixing, inter_unit, inter_scale, rows, rows_t, hidden, slope, ff, ff_out, ff_in,
    by_slot, linear_out, grad_summed, grad_rows, grad_rows_t, grad_lin, norm_out, norm_in,
    slot_grads, grads, from_core, to_x, from_x, to_piece, from_piece,
    table_sem, local_sem, bag_send, bag_recv, back_send, back_recv, w_send, w_recv, pair_send, pair_recv,
    core_send, core_recv, sum_send, sum_recv, piece_send, piece_recv, done_send, done_recv, last_send, last_recv,
):
    me = lax.axis_index("emb")
    wide = lax.axis_index("wide")
    x = wide // 2
    z_lo = lax.rem(wide, 2)
    partner = wide + 1 - 2 * z_lo
    core = lax.rem(me, 2)
    y = lax.rem(me // 2, YS)
    z = me // (2 * YS)
    sibling = me + 1 - 2 * core

    def x_at(offset):
        return lax.rem(x + XS + offset, XS)

    def wide_at(x_to):
        return x_to * 2 + z_lo

    piece = y * ZS + z

    def piece_at(offset):
        return lax.rem(piece + PIECES + offset, PIECES)

    def owner(of):
        return (lax.rem(of, ZS) * YS + of // ZS) * 2 + core

    def table(s):
        return hidden.at[s // TILES, s % TILES, :, pl.ds(0, E)]

    def fetch(s):
        return pltpu.make_async_copy(tables.at[s], table(s), table_sem.at[s])

    for s in range(SLOTS):
        fetch(s).start()
    staged = [
        pltpu.make_async_copy(src, dst, local_sem.at[n])
        for n, (src, dst) in enumerate(
            (
                (w_up_hbm, w_up.at[x]),
                (w_down_hbm, w_down.at[x]),
                (proj_y_hbm, proj_y),
                (proj_p_hbm, proj_p),
                (linear_w_hbm, linear_w),
                (cotangent_hbm, cotangent),
            )
        )
    ]
    for copy in staged:
        copy.start()

    barrier = pltpu.get_barrier_semaphore()

    @pl.loop(1, EMB)
    def _(k):
        signal(barrier, emb=lax.rem(me + k, EMB))

    for k in range(1, XS):
        signal(barrier, wide=wide_at(x_at(k)))
    signal(barrier, wide=partner)
    pl.semaphore_wait(barrier, EMB - 1 + XS)

    def half_of(which):
        return pl.ds(pl.multiple_of(which * TH, TH), TH)

    weights = ((w_up_hbm, w_up), (w_down_hbm, w_down))
    for k in range(1, XS):
        for i, (w, full) in enumerate(weights):
            send(
                w.at[half_of(core)],
                full.at[x, half_of(core)],
                w_send.at[i, k - 1],
                w_recv.at[i, k - 1],
                wide=wide_at(x_at(k)),
            ).start()

    def weights_from(k):
        if k == 0:
            staged[0].wait()
            staged[1].wait()
            return
        for i, (w, full) in enumerate(weights):
            pass_weights(i, k, 1 - core).wait_recv()
            pass_weights(i, k, core).wait_send()

    def pass_weights(i, k, which):
        part = weights[i][1].at[x_at(-k), half_of(which)]
        return send(part, part, w_send.at[2 + i, k - 1], w_recv.at[2 + i, k - 1], emb=sibling)

    bucket = lax.broadcasted_iota(jnp.int32, (ROWS, GROUP_B), 0)

    for s in range(SLOTS):
        fetch(s).wait()
        live = lengths[s : s + 1, :]
        counts = jnp.zeros((ROWS, GROUP_B), F32)
        for j in range(BAG):
            wanted = jnp.where(live > j, ids[s, j : j + 1, :], -1)
            counts = counts + jnp.where(bucket == wanted, 1.0, 0.0)
        bags = dot(counts.astype(BF16), table(s)[...], 0, 0)
        for half in range(2):
            pooled[half, pl.ds(s, GROUP_B, stride=SLOTS), :] = bags[:, half * 128 : half * 128 + 128]

    for half in range(2):
        outgoing[:, :, half * 128 : half * 128 + 128] = (
            pooled[half].astype(BF16).reshape(GROUP_B, SLOTS, 128)
        )

    def slots_at(owner):
        return pl.ds(pl.multiple_of(owner * SLOTS, SLOTS), SLOTS)

    def samples_at(owner):
        return pl.ds(owner * SAMPLES, SAMPLES)

    @pl.loop(1, EMB)
    def _(k):
        peer = lax.rem(me + k, EMB)
        send(
            outgoing.at[samples_at(peer)], slots.at[:, slots_at(me), :], bag_send.at[k], bag_recv.at[k], emb=peer
        ).start()

    slots[:, slots_at(me), :] = outgoing[samples_at(me)]

    by_field = jnp.where(
        lax.broadcasted_iota(jnp.int32, (FIELDS, FIELDS), 0) == field_row[...], 1.0, 0.0
    ).astype(BF16)
    by_slot[...] = by_field.astype(F32).T.astype(BF16)
    for copy in staged[2:]:
        copy.wait()

    for k in (1, 3, 2):
        for i, (w, full) in enumerate(weights):
            copy = send(
                w.at[half_of(core)],
                full.at[x_at(-k), half_of(core)],
                w_send.at[i, k - 1],
                w_recv.at[i, k - 1],
                wide=wide_at(x_at(-k)),
            )
            copy.wait_recv()
            copy.wait_send()
            pass_weights(i, k, core).start()

    @pl.loop(1, EMB)
    def _(k):
        source = lax.rem(me + EMB - k, EMB)
        copy = send(
            outgoing.at[samples_at(source)],
            slots.at[:, slots_at(source), :],
            bag_send.at[k],
            bag_recv.at[k],
            emb=source,
        )
        copy.wait_recv()
        copy.wait_send()

    def exchange(src, dst, n):
        return send(src, dst, pair_send.at[n], pair_recv.at[n], wide=partner)

    def rows_of(b):
        return pl.ds(pl.multiple_of(b * NF, NF), NF)

    def embed(b, _):
        sample = dot(by_field, slots[b]).astype(BF16)
        embeds[b] = sample
        cross = dot(sample, proj_y[...], 0, 0).astype(BF16)
        crossed[b] = cross
        mix = dot(proj_p[...], sample).astype(BF16)
        mixing[b] = mix
        unit, scale = norm_forward(dot(mix, cross))
        inter_unit[b] = unit
        inter_scale[b] = jnp.broadcast_to(scale, (NF, 128))
        rows[0, rows_of(b), :] = (unit * fm_gain[...]).astype(BF16)
        return 0

    lax.fori_loop(0, SAMPLES, embed, 0)
    rows_copy = exchange(rows.at[0], rows.at[1], 0)
    rows_copy.start()
    ff[...] = jnp.zeros_like(ff)

    def forward(group, k):
        chunk = x_at(-k)

        @pl.loop(0, 2)
        def _(t):
            tile = chunk * 2 + t
            here = pl.ds(pl.multiple_of(t * TH, TH), TH)
            gate = dot(rows[group], w_up[chunk, here, :], 1, 1)
            sigma = 0.5 * jnp.tanh(0.5 * gate) + 0.5
            act = gate * sigma
            slope[group, tile] = (sigma + act * (1.0 - sigma)).astype(BF16)
            act = act.astype(BF16)
            hidden[group, tile] = act
            ff[group] += dot(act, w_down[chunk, here, :])

    weights_from(0)
    forward(0, 0)

    def linear(b, _):
        linear_out[b] = dot(linear_w[...], embeds[b])
        return 0

    lax.fori_loop(0, SAMPLES, linear, 0)
    rows_copy.wait()
    forward(1, 0)
    for k in range(1, XS):
        weights_from(k)
        forward(1, k)
    ff_out[...] = ff[1].astype(BF16)
    ff_copy = exchange(ff_out, ff_in, 1)
    ff_copy.start()
    for k in range(1, XS):
        forward(0, k)
    rows_t[0] = rows[0].astype(F32).T.astype(BF16)
    rows_t[1] = rows[1].astype(F32).T.astype(BF16)
    ff_copy.wait()

    def finish(values, b, first, count):
        here = slice(first, first + count)
        unit, scale = norm_forward(values + embeds[b, here, :].astype(F32))
        layer_out[b, here, :] = (unit * out_gain[...]).astype(BF16)
        grad = norm_back(unit, scale, out_gain[...], cotangent[b, here, :].astype(F32))
        grad_summed[b, here, :] = grad
        return grad.astype(BF16)

    def finish_ff(b, _):
        total = ff[0, rows_of(b), :] + ff_in[rows_of(b), :].astype(F32)
        grad_rows[0, rows_of(b), :] = finish(total, b, 0, NF)
        return 0

    lax.fori_loop(0, SAMPLES, finish_ff, 0)
    grad_copy = exchange(grad_rows.at[0], grad_rows.at[1], 2)
    grad_copy.start()

    def finish_linear(b, _):
        grad_lin[b] = finish(linear_out[b], b, NF, NL)
        grad_summed[b] += dot(linear_w[...], grad_lin[b], 0, 0)
        return 0

    lax.fori_loop(0, SAMPLES, finish_linear, 0)
    layer_copy = pltpu.make_async_copy(layer_out, layer_out_hbm, local_sem.at[6])
    layer_copy.start()
    grad_rows_t[0] = grad_rows[0].astype(F32).T.astype(BF16)
    ff[...] = jnp.zeros_like(ff)
    grad_copy.wait()
    grad_rows_t[1] = grad_rows[1].astype(F32).T.astype(BF16)

    def gate_back(group, chunk, t):
        here = pl.ds(pl.multiple_of(t * TH, TH), TH)
        tile = chunk * 2 + t
        grad_hidden = dot(grad_rows[group], w_down[chunk, here, :], 1, 1)
        grad_gate = (grad_hidden * slope[group, tile].astype(F32)).astype(BF16)
        ff[group] += dot(grad_gate, w_up[chunk, here, :])
        return grad_gate

    k_mine = pl.ds(pl.multiple_of(core * 128, 128), 128)
    k_other = pl.ds(pl.multiple_of(128 - core * 128, 128), 128)

    def keep(kind, tile, part):
        part = part.astype(BF16)
        for half in range(2):
            grads[kind, tile * 2 + half] = part[:, half * 256 : half * 256 + 256]

    def over_cores(kind, k):
        chunk = pl.ds(x_at(k) * 4, 4)
        return send(
            grads.at[kind, chunk, k_other],
            from_core.at[kind, chunk],
            core_send.at[kind, k],
            core_recv.at[kind, k],
            emb=sibling,
        )

    def over_x(kind, k):
        return send(
            to_x.at[kind, pl.ds(x_at(k) * 4, 4)],
            from_x.at[kind, k - 1],
            sum_send.at[kind, k],
            sum_recv.at[kind, k],
            wide=wide_at(x_at(k)),
        )

    def over_pieces(kind, k):
        peer = piece_at(k)
        return send(
            to_piece.at[kind, peer],
            from_piece.at[kind, k],
            piece_send.at[kind, k],
            piece_recv.at[kind, k],
            emb=owner(peer),
        )

    def spread(kind, k, of, to):
        part = done.at[kind, core, of]
        return send(part, part, done_send.at[kind, k], done_recv.at[kind, k], emb=owner(to))

    def to_sibling(kind, k, half):
        part = done.at[kind, half, piece_at(-k)]
        return send(part, part, last_send.at[kind, k], last_recv.at[kind, k], emb=sibling)

    def pass_on(kind, k):
        over_cores(kind, k).wait()

        @pl.loop(0, 4)
        def _(t):
            part = x_at(k) * 4 + t
            to_x[kind, part] = (
                grads[kind, part, k_mine].astype(F32) + from_core[kind, part].astype(F32)
            ).astype(BF16)

        over_x(kind, k).start()

    def sum_x(kind):
        over_cores(kind, 0).wait()
        for k in range(1, XS):
            over_x(kind, k).wait()

        @pl.loop(0, 4)
        def _(t):
            mine = x * 4 + t
            total = grads[kind, mine, k_mine].astype(F32) + from_core[kind, mine].astype(F32)
            for k in range(XS - 1):
                total = total + from_x[kind, k, t].astype(F32)
            to_piece[kind, pl.ds(t * ZS, ZS)] = total.astype(BF16).reshape(ZS, PIECE, 256)

        @pl.loop(1, PIECES)
        def _(k):
            over_pieces(kind, k).start()

    def sum_pieces(kind):
        @pl.loop(1, PIECES)
        def _(k):
            over_pieces(kind, k).wait()

        total = to_piece[kind, piece].astype(F32)
        for k in range(1, PIECES):
            total = total + from_piece[kind, k].astype(F32)
        done[kind, core, piece] = total.astype(BF16)

        @pl.loop(1, PIECES)
        def _(k):
            spread(kind, k, piece, piece_at(k)).start()

        to_sibling(kind, 0, core).start()

    def hand_over(kind):
        @pl.loop(1, PIECES)
        def _(k):
            spread(kind, k, piece_at(-k), piece_at(-k)).wait_recv()
            to_sibling(kind, k, core).start()

    def settle(kind):
        @pl.loop(1, PIECES)
        def _(k):
            spread(kind, k, piece, piece_at(k)).wait_send()

        @pl.loop(0, PIECES)
        def _(k):
            to_sibling(kind, k, core).wait_send()
            to_sibling(kind, k, 1 - core).wait_recv()

    order = (1, 2, 3, 0)
    for k in order:

        @pl.loop(0, 2)
        def _(t):
            tile = x_at(k) * 2 + t
            keep(1, tile, dot(grad_rows_t[0], hidden[0, tile]) + dot(grad_rows_t[1], hidden[1, tile]))

        over_cores(1, k).start()

    for n, k in enumerate(order):

        @pl.loop(0, 2)
        def _(t):
            slope[1, x_at(k) * 2 + t] = gate_back(1, x_at(k), t)

        if n < 3:
            pass_on(1, k)

    norm_out[...] = ff[1].astype(BF16)
    norm_copy = exchange(norm_out, norm_in, 3)
    norm_copy.start()

    for n, k in enumerate(order):

        @pl.loop(0, 2)
        def _(t):
            tile = x_at(k) * 2 + t
            grad_gate = gate_back(0, x_at(k), t)
            keep(0, tile, dot(rows_t[0], grad_gate) + dot(rows_t[1], slope[1, tile]))

        over_cores(0, k).start()
        if n:
            pass_on(0, order[n - 1])
        (lambda kind: None, lambda kind: None, sum_x, sum_pieces)[n](1)

    norm_copy.wait()

    def tail(b, _):
        upstream = ff[0, rows_of(b), :] + norm_in[rows_of(b), :].astype(F32)
        grad_inter = norm_back(inter_unit[b], inter_scale[b, :, 0:1], fm_gain[...], upstream).astype(BF16)
        grad_mixing = dot(grad_inter, crossed[b], 1, 1).astype(BF16)
        grad_crossed = dot(mixing[b], grad_inter, 0, 0).astype(BF16)
        total = grad_summed[b] + dot(proj_p[...], grad_mixing, 0, 0)
        total = total + dot(proj_y[...], grad_crossed, 1, 1)
        slot_grads[b] = dot(by_slot[...], total.astype(BF16)).astype(BF16)
        return 0

    lax.fori_loop(0, SAMPLES, tail, 0)

    @pl.loop(1, EMB)
    def _(k):
        peer = lax.rem(me + k, EMB)
        send(
            slot_grads.at[:, slots_at(peer), :],
            bag_grads.at[samples_at(me)],
            back_send.at[k],
            back_recv.at[k],
            emb=peer,
        ).start()

    own_bags = pltpu.make_async_copy(
        slot_grads.at[:, slots_at(me), :], bag_grads.at[samples_at(me)], local_sem.at[7]
    )
    own_bags.start()

    hand_over(1)
    sum_x(0)
    sum_pieces(0)
    hand_over(0)
    settle(1)
    settle(0)

    @pl.loop(1, EMB)
    def _(k):
        source = lax.rem(me + EMB - k, EMB)
        copy = send(
            slot_grads.at[:, slots_at(source), :],
            bag_grads.at[samples_at(source)],
            back_send.at[k],
            back_recv.at[k],
            emb=source,
        )
        copy.wait_recv()
        copy.wait_send()

    own_bags.wait()
    layer_copy.wait()


def whole_layer(*operands):
    anywhere = pl.BlockSpec(memory_space=pl.ANY)
    vmem = pl.BlockSpec(memory_space=pltpu.VMEM)
    dma = pltpu.SemaphoreType.DMA
    return pl.pallas_call(
        layer_kernel,
        name="whole_layer",
        out_shape=(
            jax.ShapeDtypeStruct((SAMPLES, FIELDS, E), BF16),
            jax.ShapeDtypeStruct((GROUP_B, SLOTS, E), BF16),
            jax.ShapeDtypeStruct((2, 2, PIECES, PIECE, 256), BF16),
        ),
        in_specs=[vmem] * 5 + [anywhere] * 7,
        out_specs=(anywhere, anywhere, vmem),
        scratch_shapes=[
            pltpu.VMEM((2, GROUP_B * SLOTS, 128), F32),
            pltpu.VMEM((GROUP_B, SLOTS, E), BF16),
            pltpu.VMEM((SAMPLES, FIELDS, E), BF16),
            pltpu.VMEM((XS, SLICE, E), BF16),
            pltpu.VMEM((XS, SLICE, E), BF16),
            pltpu.VMEM((FIELDS, E), BF16),
            pltpu.VMEM((NF, FIELDS), BF16),
            pltpu.VMEM((NL, FIELDS), BF16),
            pltpu.VMEM((SAMPLES, FIELDS, E), BF16),
            pltpu.VMEM((SAMPLES, FIELDS, E), BF16),
            pltpu.VMEM((SAMPLES, FIELDS, E), BF16),
            pltpu.VMEM((SAMPLES, E, E), BF16),
            pltpu.VMEM((SAMPLES, NF, E), BF16),
            pltpu.VMEM((SAMPLES, NF, E), F32),
            pltpu.VMEM((SAMPLES, NF, 128), F32),
            pltpu.VMEM((2, NROW, E), BF16),
            pltpu.VMEM((2, E, NROW), BF16),
            pltpu.VMEM((2, TILES, NROW, TH), BF16),
            pltpu.VMEM((2, TILES, NROW, TH), BF16),
            pltpu.VMEM((2, NROW, E), F32),
            pltpu.VMEM((NROW, E), BF16),
            pltpu.VMEM((NROW, E), BF16),
            pltpu.VMEM((FIELDS, FIELDS), BF16),
            pltpu.VMEM((SAMPLES, NL, E), F32),
            pltpu.VMEM((SAMPLES, FIELDS, E), F32),
            pltpu.VMEM((2, NROW, E), BF16),
            pltpu.VMEM((2, E, NROW), BF16),
            pltpu.VMEM((SAMPLES, NL, E), BF16),
            pltpu.VMEM((NROW, E), BF16),
            pltpu.VMEM((NROW, E), BF16),
            pltpu.VMEM((SAMPLES, FIELDS, E), BF16),
            pltpu.VMEM((2, TILES * 2, 256, 256), BF16),
            pltpu.VMEM((2, TILES * 2, 128, 256), BF16),
            pltpu.VMEM((2, TILES * 2, 128, 256), BF16),
            pltpu.VMEM((2, XS - 1, 4, 128, 256), BF16),
            pltpu.VMEM((2, PIECES, PIECE, 256), BF16),
            pltpu.VMEM((2, PIECES, PIECE, 256), BF16),
            dma((SLOTS,)),
            dma((8,)),
            dma((EMB,)),
            dma((EMB,)),
            dma((EMB,)),
            dma((EMB,)),
            dma((4, XS - 1)),
            dma((4, XS - 1)),
            dma((4,)),
            dma((4,)),
            dma((2, XS)),
            dma((2, XS)),
            dma((2, XS)),
            dma((2, XS)),
            dma((2, PIECES)),
            dma((2, PIECES)),
            dma((2, PIECES)),
            dma((2, PIECES)),
            dma((2, PIECES)),
            dma((2, PIECES)),
        ],
        compiler_params=pltpu.CompilerParams(
            collective_id=0, has_side_effects=True, vmem_limit_bytes=62 << 20
        ),
    )(*operands)


def finish_kernel(layer_out, bag_grads, done, layer_final, bag_final, up, down, held, sums, in_sem, out_sem, sum_sem):
    pairs = ((layer_out, layer_final), (bag_grads, bag_final))
    rows = [layer_out.shape[0] // 2, bag_grads.shape[0] // 2]
    incoming, outgoing = [], []
    for n, (src, dst) in enumerate(pairs):
        for half in range(2):
            part = pl.ds(half * rows[n], rows[n])
            here = held[n].at[part]
            incoming.append(pltpu.make_async_copy(src.at[part], here, in_sem.at[n, half]))
            outgoing.append(pltpu.make_async_copy(here, dst.at[part], out_sem.at[n, half]))
    for copy in incoming:
        copy.start()
    sum_copies = []
    for kind, out in enumerate((up, down)):
        for y in range(YS):
            part = pl.ds(y * 256, 256)
            for half in range(2):
                block = done[kind, half, y * ZS : y * ZS + ZS].reshape(128, 256)
                sums[kind, part, half * 128 : half * 128 + 128] = block.astype(F32).T
            copy = pltpu.make_async_copy(sums.at[kind, part], out.at[part], sum_sem.at[kind, y])
            copy.start()
            sum_copies.append(copy)
            n = kind * YS + y
            if n % 2 == 1:
                incoming[n // 2].wait()
                outgoing[n // 2].start()
    for copy in outgoing + sum_copies:
        copy.wait()


def finish_outputs(layer_out, bag_grads, done):
    anywhere = pl.BlockSpec(memory_space=pl.ANY)
    dma = pltpu.SemaphoreType.DMA
    return pl.pallas_call(
        finish_kernel,
        name="finish_outputs",
        out_shape=(
            jax.ShapeDtypeStruct(layer_out.shape, BF16),
            jax.ShapeDtypeStruct(bag_grads.shape, BF16),
            jax.ShapeDtypeStruct((SLICE, E), F32),
            jax.ShapeDtypeStruct((SLICE, E), F32),
        ),
        in_specs=[anywhere, anywhere, pl.BlockSpec(memory_space=pltpu.VMEM)],
        out_specs=(anywhere,) * 4,
        scratch_shapes=[
            [pltpu.VMEM(layer_out.shape, BF16), pltpu.VMEM(bag_grads.shape, BF16)],
            pltpu.VMEM((2, SLICE, E), F32),
            dma((2, 2)),
            dma((2, 2)),
            dma((2, YS)),
        ],
    )(layer_out, bag_grads, done)


def body(
    tables,
    bag_ids,
    bag_lengths,
    slot_field,
    proj_y,
    proj_p,
    linear_w,
    fm_gain,
    w_up,
    w_down,
    out_gain,
    cotangent,
):
    layer_out, bag_grads, done = whole_layer(
        bag_ids[0].transpose(1, 2, 0),
        bag_lengths[0].transpose(1, 0),
        slot_field.reshape(1, FIELDS),
        fm_gain.reshape(1, E),
        out_gain.reshape(1, E),
        tables,
        w_up,
        w_down,
        proj_y,
        proj_p,
        linear_w,
        cotangent[0],
    )
    layer_out, bag_grads, grad_up, grad_down = finish_outputs(layer_out, bag_grads, done)
    return (layer_out[None], bag_grads[None], grad_up, grad_down)


def solution(mesh):
    placed = (
        P("emb", None, None),
        P("wide", None, "emb", None),
        P("wide", None, "emb"),
        P(),
        P(),
        P(),
        P(),
        P(),
        P("wide", None),
        P("wide", None),
        P(),
        P("wide", "emb", None, None),
    )
    return jax.shard_map(
        body,
        mesh=mesh,
        in_specs=placed,
        out_specs=(
            P("wide", "emb", None, None),
            P("wide", None, "emb", None),
            P("wide", None),
            P("wide", None),
        ),
        check_vma=False,
    )
```

```python
import functools

import jax
import jax.numpy as jnp
from jax import lax
from jax.experimental import pallas as pl
from jax.experimental.pallas import tpu as pltpu
from jax.sharding import PartitionSpec as P

MESH = pl.DeviceIdType.MESH
F32 = jnp.float32
BF16 = jnp.bfloat16

E = 256
FIELDS = 512
ROWS = 512
NF = 128
NL = 384
BAG = 4
SAMPLES = 4
SLOTS = 16
GROUP_B = 128
EMB = 32
XS = 4
YS = 4
ZS = 4
SLICE = 1024
TH = 512
TILES = 8
NROW = SAMPLES * NF
norm_eps = 1e-05


def dot(a, b, ca=1, cb=0):
    return lax.dot_general(a, b, (((ca,), (cb,)), ((), ())), preferred_element_type=F32)


def send(src, dst, send_sem, recv_sem, **device):
    return pltpu.make_async_remote_copy(
        src_ref=src,
        dst_ref=dst,
        send_sem=send_sem,
        recv_sem=recv_sem,
        device_id=device,
        device_id_type=MESH,
    )


def signal(sem, **device):
    pl.semaphore_signal(sem, inc=1, device_id=device, device_id_type=MESH)


def norm_forward(values):
    centre = jnp.mean(values, axis=-1, keepdims=True)
    shifted = values - centre
    scale = lax.rsqrt(jnp.mean(shifted * shifted, axis=-1, keepdims=True) + norm_eps)
    return shifted * scale, scale


def norm_back(unit, scale, gain, upstream):
    scaled = upstream * gain
    return scale * (
        scaled
        - jnp.mean(scaled, axis=-1, keepdims=True)
        - unit * jnp.mean(scaled * unit, axis=-1, keepdims=True)
    )


def layer_kernel(
    ids, lengths, field_row, fm_gain, out_gain,
    tables, w_up_hbm, w_down_hbm, proj_y_hbm, proj_p_hbm, linear_w_hbm, cotangent_hbm,
    layer_out_hbm, bag_grads, whole,
    pooled, outgoing, slots, w_up, w_down, proj_y, proj_p, linear_w, cotangent, layer_out,
    embeds, crossed, mixing, inter_unit, inter_scale, rows, rows_t, hidden, slope, ff, ff_out, ff_in,
    by_slot, linear_out, grad_summed, grad_rows, grad_rows_t, grad_lin, norm_out, norm_in,
    slot_grads, grads, from_core, to_x, from_x, to_y, from_y, to_z, from_z, done_z,
    table_sem, local_sem, bag_send, bag_recv, back_send, back_recv, w_send, w_recv, pair_send, pair_recv,
    core_send, core_recv, sum_send, sum_recv,
):
    me = lax.axis_index("emb")
    wide = lax.axis_index("wide")
    x = wide // 2
    z_lo = lax.rem(wide, 2)
    partner = wide + 1 - 2 * z_lo
    core = lax.rem(me, 2)
    y = lax.rem(me // 2, YS)
    z = me // (2 * YS)
    sibling = me + 1 - 2 * core

    def x_at(offset):
        return lax.rem(x + XS + offset, XS)

    def wide_at(x_to):
        return x_to * 2 + z_lo

    def emb_at(z_to, y_to):
        return (z_to * YS + y_to) * 2 + core

    def table(s):
        return hidden.at[s // TILES, s % TILES, :, pl.ds(0, E)]

    def fetch(s):
        return pltpu.make_async_copy(tables.at[s], table(s), table_sem.at[s])

    for s in range(SLOTS):
        fetch(s).start()
    staged = [
        pltpu.make_async_copy(src, dst, local_sem.at[n])
        for n, (src, dst) in enumerate(
            (
                (w_up_hbm, w_up.at[x]),
                (w_down_hbm, w_down.at[x]),
                (proj_y_hbm, proj_y),
                (proj_p_hbm, proj_p),
                (linear_w_hbm, linear_w),
                (cotangent_hbm, cotangent),
            )
        )
    ]
    for copy in staged:
        copy.start()

    barrier = pltpu.get_barrier_semaphore()

    @pl.loop(1, EMB)
    def _(k):
        signal(barrier, emb=lax.rem(me + k, EMB))

    for k in range(1, XS):
        signal(barrier, wide=wide_at(x_at(k)))
    signal(barrier, wide=partner)
    def half_of(which):
        return pl.ds(pl.multiple_of(which * TH, TH), TH)

    weights = ((w_up_hbm, w_up), (w_down_hbm, w_down))
    def weights_from(k):
        if k == 0:
            staged[0].wait()
            staged[1].wait()
            return
        for i, (w, full) in enumerate(weights):
            pass_weights(i, k, 1 - core).wait_recv()
            pass_weights(i, k, core).wait_send()

    def pass_weights(i, k, which):
        part = weights[i][1].at[x_at(-k), half_of(which)]
        return send(part, part, w_send.at[2 + i, k - 1], w_recv.at[2 + i, k - 1], emb=sibling)

    bucket = lax.broadcasted_iota(jnp.int32, (ROWS, GROUP_B), 0)

    for s in range(SLOTS):
        if s == SLOTS // 2:
            pl.semaphore_wait(barrier, EMB - 1 + XS)
            for k in range(1, XS):
                for i, (w, full) in enumerate(weights):
                    send(
                        w.at[half_of(core)],
                        full.at[x, half_of(core)],
                        w_send.at[i, k - 1],
                        w_recv.at[i, k - 1],
                        wide=wide_at(x_at(k)),
                    ).start()
        fetch(s).wait()
        live = lengths[s : s + 1, :]
        counts = jnp.zeros((ROWS, GROUP_B), F32)
        for j in range(BAG):
            wanted = jnp.where(live > j, ids[s, j : j + 1, :], -1)
            counts = counts + jnp.where(bucket == wanted, 1.0, 0.0)
        bags = dot(counts.astype(BF16), table(s)[...], 0, 0)
        for half in range(2):
            pooled[half, pl.ds(s, GROUP_B, stride=SLOTS), :] = bags[:, half * 128 : half * 128 + 128]

    for half in range(2):
        outgoing[:, :, half * 128 : half * 128 + 128] = (
            pooled[half].astype(BF16).reshape(GROUP_B, SLOTS, 128)
        )

    def slots_at(owner):
        return pl.ds(pl.multiple_of(owner * SLOTS, SLOTS), SLOTS)

    def samples_at(owner):
        return pl.ds(owner * SAMPLES, SAMPLES)

    @pl.loop(1, EMB)
    def _(k):
        peer = lax.rem(me + k, EMB)
        send(
            outgoing.at[samples_at(peer)], slots.at[:, slots_at(me), :], bag_send.at[k], bag_recv.at[k], emb=peer
        ).start()

    slots[:, slots_at(me), :] = outgoing[samples_at(me)]

    by_field = jnp.where(
        lax.broadcasted_iota(jnp.int32, (FIELDS, FIELDS), 0) == field_row[...], 1.0, 0.0
    ).astype(BF16)
    by_slot[...] = by_field.astype(F32).T.astype(BF16)
    for copy in staged[2:]:
        copy.wait()

    for k in (1, 3, 2):
        for i, (w, full) in enumerate(weights):
            copy = send(
                w.at[half_of(core)],
                full.at[x_at(-k), half_of(core)],
                w_send.at[i, k - 1],
                w_recv.at[i, k - 1],
                wide=wide_at(x_at(-k)),
            )
            copy.wait_recv()
            copy.wait_send()
            pass_weights(i, k, core).start()

    @pl.loop(1, EMB)
    def _(k):
        source = lax.rem(me + EMB - k, EMB)
        copy = send(
            outgoing.at[samples_at(source)],
            slots.at[:, slots_at(source), :],
            bag_send.at[k],
            bag_recv.at[k],
            emb=source,
        )
        copy.wait_recv()
        copy.wait_send()

    def exchange(src, dst, n):
        return send(src, dst, pair_send.at[n], pair_recv.at[n], wide=partner)

    def rows_of(b):
        return pl.ds(pl.multiple_of(b * NF, NF), NF)

    def embed(b, _):
        sample = dot(by_field, slots[b]).astype(BF16)
        embeds[b] = sample
        cross = dot(sample, proj_y[...], 0, 0).astype(BF16)
        crossed[b] = cross
        mix = dot(proj_p[...], sample).astype(BF16)
        mixing[b] = mix
        unit, scale = norm_forward(dot(mix, cross))
        inter_unit[b] = unit
        inter_scale[b] = jnp.broadcast_to(scale, (NF, 128))
        rows[0, rows_of(b), :] = (unit * fm_gain[...]).astype(BF16)
        return 0

    lax.fori_loop(0, SAMPLES, embed, 0)
    rows_copy = exchange(rows.at[0], rows.at[1], 0)
    rows_copy.start()
    ff[...] = jnp.zeros_like(ff)

    def forward(group, k):
        chunk = x_at(-k)

        @pl.loop(0, 2)
        def _(t):
            tile = chunk * 2 + t
            here = pl.ds(pl.multiple_of(t * TH, TH), TH)
            gate = dot(rows[group], w_up[chunk, here, :], 1, 1)
            sigma = 0.5 * jnp.tanh(0.5 * gate) + 0.5
            act = gate * sigma
            slope[group, tile] = (sigma + act * (1.0 - sigma)).astype(BF16)
            act = act.astype(BF16)
            hidden[group, tile] = act
            ff[group] += dot(act, w_down[chunk, here, :])

    weights_from(0)
    forward(0, 0)

    def linear(b, _):
        linear_out[b] = dot(linear_w[...], embeds[b])
        return 0

    lax.fori_loop(0, SAMPLES, linear, 0)
    rows_copy.wait()
    forward(1, 0)
    for k in range(1, XS):
        weights_from(k)
        forward(1, k)
    ff_out[...] = ff[1].astype(BF16)
    ff_copy = exchange(ff_out, ff_in, 1)
    ff_copy.start()
    for k in range(1, XS):
        forward(0, k)
    rows_t[0] = rows[0].astype(F32).T.astype(BF16)
    rows_t[1] = rows[1].astype(F32).T.astype(BF16)
    ff_copy.wait()

    def finish(values, b, first, count):
        here = slice(first, first + count)
        unit, scale = norm_forward(values + embeds[b, here, :].astype(F32))
        layer_out[b, here, :] = (unit * out_gain[...]).astype(BF16)
        grad = norm_back(unit, scale, out_gain[...], cotangent[b, here, :].astype(F32))
        grad_summed[b, here, :] = grad
        return grad.astype(BF16)

    def finish_ff(b, _):
        total = ff[0, rows_of(b), :] + ff_in[rows_of(b), :].astype(F32)
        grad_rows[0, rows_of(b), :] = finish(total, b, 0, NF)
        return 0

    lax.fori_loop(0, SAMPLES, finish_ff, 0)
    grad_copy = exchange(grad_rows.at[0], grad_rows.at[1], 2)
    grad_copy.start()

    def finish_linear(b, _):
        grad_lin[b] = finish(linear_out[b], b, NF, NL)
        grad_summed[b] += dot(linear_w[...], grad_lin[b], 0, 0)
        return 0

    lax.fori_loop(0, SAMPLES, finish_linear, 0)
    layer_copy = pltpu.make_async_copy(layer_out, layer_out_hbm, local_sem.at[6])
    layer_copy.start()
    grad_rows_t[0] = grad_rows[0].astype(F32).T.astype(BF16)
    ff[...] = jnp.zeros_like(ff)
    grad_copy.wait()
    grad_rows_t[1] = grad_rows[1].astype(F32).T.astype(BF16)

    def gate_back(group, chunk, t):
        here = pl.ds(pl.multiple_of(t * TH, TH), TH)
        tile = chunk * 2 + t
        grad_hidden = dot(grad_rows[group], w_down[chunk, here, :], 1, 1)
        grad_gate = (grad_hidden * slope[group, tile].astype(F32)).astype(BF16)
        ff[group] += dot(grad_gate, w_up[chunk, here, :])
        return grad_gate

    k_mine = pl.ds(pl.multiple_of(core * 128, 128), 128)
    k_other = pl.ds(pl.multiple_of(128 - core * 128, 128), 128)

    def keep(kind, tile, part):
        part = part.astype(BF16)
        for half in range(2):
            grads[kind, tile * 2 + half] = part[:, half * 256 : half * 256 + 256]

    def over_cores(kind, k):
        chunk = pl.ds(x_at(k) * 4, 4)
        return send(
            grads.at[kind, chunk, k_other],
            from_core.at[kind, chunk],
            core_send.at[kind, k],
            core_recv.at[kind, k],
            emb=sibling,
        )

    def over_x(kind, k):
        return send(
            to_x.at[kind, pl.ds(x_at(k) * 4, 4)],
            from_x.at[kind, k - 1],
            sum_send.at[kind, k],
            sum_recv.at[kind, k],
            wide=wide_at(x_at(k)),
        )

    def over_y(kind, k):
        peer = lax.rem(y + k, YS)
        return send(
            to_y.at[kind, peer],
            from_y.at[kind, k - 1],
            sum_send.at[kind, 3 + k],
            sum_recv.at[kind, 3 + k],
            emb=emb_at(z, peer),
        )

    def over_z(kind, k):
        peer = lax.rem(z + k, ZS)
        return send(
            to_z.at[kind, peer],
            from_z.at[kind, k - 1],
            sum_send.at[kind, 6 + k],
            sum_recv.at[kind, 6 + k],
            emb=emb_at(peer, y),
        )

    def along_z(kind, k, z_of, z_to):
        part = done_z.at[kind, z_of]
        return send(part, part, sum_send.at[kind, 9 + k], sum_recv.at[kind, 9 + k], emb=emb_at(z_to, y))

    def band(kind, y_of, columns):
        return whole.at[kind, pl.ds(pl.multiple_of(y_of * 256, 256), 256), columns]

    def along_y(kind, k, y_of, y_to):
        part = band(kind, y_of, k_mine)
        return send(part, part, sum_send.at[kind, 12 + k], sum_recv.at[kind, 12 + k], emb=emb_at(z, y_to))

    def to_sibling(kind, k, columns):
        part = band(kind, lax.rem(y + YS - k, YS), columns)
        return send(part, part, sum_send.at[kind, 16 + k], sum_recv.at[kind, 16 + k], emb=sibling)

    def pass_on(kind, k):
        over_cores(kind, k).wait()

        @pl.loop(0, 4)
        def _(t):
            part = x_at(k) * 4 + t
            to_x[kind, part] = (
                grads[kind, part, k_mine].astype(F32) + from_core[kind, part].astype(F32)
            ).astype(BF16)

        over_x(kind, k).start()

    def sum_x(kind):
        over_cores(kind, 0).wait()
        for k in range(1, XS):
            over_x(kind, k).wait()

        @pl.loop(0, 4)
        def _(t):
            mine = x * 4 + t
            total = grads[kind, mine, k_mine].astype(F32) + from_core[kind, mine].astype(F32)
            for k in range(XS - 1):
                total = total + from_x[kind, k, t].astype(F32)
            to_y[kind, t] = total.astype(BF16)

        for k in range(1, YS):
            over_y(kind, k).start()

    def sum_y(kind):
        for k in range(1, YS):
            over_y(kind, k).wait()
        total = to_y[kind, y].astype(F32)
        for k in range(YS - 1):
            total = total + from_y[kind, k].astype(F32)
        to_z[kind] = total.astype(BF16).reshape(ZS, 128 // ZS, 256)
        for k in range(1, ZS):
            over_z(kind, k).start()

    def sum_z(kind):
        for k in range(1, ZS):
            over_z(kind, k).wait()
        total = to_z[kind, z].astype(F32)
        for k in range(ZS - 1):
            total = total + from_z[kind, k].astype(F32)
        done_z[kind, z] = total.astype(BF16)
        for k in range(1, ZS):
            along_z(kind, k, z, lax.rem(z + k, ZS)).start()

    def spread_y(kind):
        for k in range(1, ZS):
            source = lax.rem(z + ZS - k, ZS)
            along_z(kind, k, z, source).wait_send()
            along_z(kind, k, source, source).wait_recv()
        part = done_z[kind].reshape(128, 256).astype(F32).T.astype(BF16)
        whole[kind, pl.ds(pl.multiple_of(y * 256, 256), 256), k_mine] = part
        for k in range(1, YS):
            along_y(kind, k, y, lax.rem(y + k, YS)).start()
        to_sibling(kind, 0, k_mine).start()

    def spread_cores(kind):
        for k in range(1, YS):
            source = lax.rem(y + YS - k, YS)
            along_y(kind, k, source, source).wait_recv()
            to_sibling(kind, k, k_mine).start()

    def settle(kind):
        for k in range(1, YS):
            along_y(kind, k, y, lax.rem(y + k, YS)).wait_send()
        for k in range(YS):
            to_sibling(kind, k, k_mine).wait_send()
            to_sibling(kind, k, k_other).wait_recv()

    order = (1, 2, 3, 0)
    for k in order:

        @pl.loop(0, 2)
        def _(t):
            tile = x_at(k) * 2 + t
            keep(1, tile, dot(grad_rows_t[0], hidden[0, tile]) + dot(grad_rows_t[1], hidden[1, tile]))

        over_cores(1, k).start()

    for n, k in enumerate(order):

        @pl.loop(0, 2)
        def _(t):
            slope[1, x_at(k) * 2 + t] = gate_back(1, x_at(k), t)

        if n < 3:
            pass_on(1, k)

    norm_out[...] = ff[1].astype(BF16)
    norm_copy = exchange(norm_out, norm_in, 3)
    norm_copy.start()

    for n, k in enumerate(order):

        @pl.loop(0, 2)
        def _(t):
            tile = x_at(k) * 2 + t
            grad_gate = gate_back(0, x_at(k), t)
            keep(0, tile, dot(rows_t[0], grad_gate) + dot(rows_t[1], slope[1, tile]))

        over_cores(0, k).start()
        if n:
            pass_on(0, order[n - 1])
        if n == 2:
            sum_x(1)

    norm_copy.wait()
    sum_y(1)

    def tail(b, _):
        upstream = ff[0, rows_of(b), :] + norm_in[rows_of(b), :].astype(F32)
        grad_inter = norm_back(inter_unit[b], inter_scale[b, :, 0:1], fm_gain[...], upstream).astype(BF16)
        grad_mixing = dot(grad_inter, crossed[b], 1, 1).astype(BF16)
        grad_crossed = dot(mixing[b], grad_inter, 0, 0).astype(BF16)
        total = grad_summed[b] + dot(proj_p[...], grad_mixing, 0, 0)
        total = total + dot(proj_y[...], grad_crossed, 1, 1)
        slot_grads[b] = dot(by_slot[...], total.astype(BF16)).astype(BF16)
        return 0

    lax.fori_loop(0, SAMPLES, tail, 0)

    sum_z(1)

    def bags_back(first, last):
        @pl.loop(first, last)
        def _(k):
            peer = lax.rem(me + k, EMB)
            send(
                slot_grads.at[:, slots_at(peer), :],
                bag_grads.at[samples_at(me)],
                back_send.at[k],
                back_recv.at[k],
                emb=peer,
            ).start()

    bags_back(1, 8)
    own_bags = pltpu.make_async_copy(
        slot_grads.at[:, slots_at(me), :], bag_grads.at[samples_at(me)], local_sem.at[7]
    )
    own_bags.start()
    sum_x(0)
    bags_back(8, 16)
    spread_y(1)
    sum_y(0)
    bags_back(16, 24)
    sum_z(0)
    bags_back(24, EMB)
    spread_cores(1)
    spread_y(0)
    spread_cores(0)
    settle(1)
    settle(0)

    @pl.loop(1, EMB)
    def _(k):
        source = lax.rem(me + EMB - k, EMB)
        copy = send(
            slot_grads.at[:, slots_at(source), :],
            bag_grads.at[samples_at(source)],
            back_send.at[k],
            back_recv.at[k],
            emb=source,
        )
        copy.wait_recv()
        copy.wait_send()

    own_bags.wait()
    layer_copy.wait()


def whole_layer(*operands):
    anywhere = pl.BlockSpec(memory_space=pl.ANY)
    vmem = pl.BlockSpec(memory_space=pltpu.VMEM)
    dma = pltpu.SemaphoreType.DMA
    return pl.pallas_call(
        layer_kernel,
        name="whole_layer",
        out_shape=(
            jax.ShapeDtypeStruct((SAMPLES, FIELDS, E), BF16),
            jax.ShapeDtypeStruct((GROUP_B, SLOTS, E), BF16),
            jax.ShapeDtypeStruct((2, SLICE, E), BF16),
        ),
        in_specs=[vmem] * 5 + [anywhere] * 7,
        out_specs=(anywhere, anywhere, vmem),
        scratch_shapes=[
            pltpu.VMEM((2, GROUP_B * SLOTS, 128), F32),
            pltpu.VMEM((GROUP_B, SLOTS, E), BF16),
            pltpu.VMEM((SAMPLES, FIELDS, E), BF16),
            pltpu.VMEM((XS, SLICE, E), BF16),
            pltpu.VMEM((XS, SLICE, E), BF16),
            pltpu.VMEM((FIELDS, E), BF16),
            pltpu.VMEM((NF, FIELDS), BF16),
            pltpu.VMEM((NL, FIELDS), BF16),
            pltpu.VMEM((SAMPLES, FIELDS, E), BF16),
            pltpu.VMEM((SAMPLES, FIELDS, E), BF16),
            pltpu.VMEM((SAMPLES, FIELDS, E), BF16),
            pltpu.VMEM((SAMPLES, E, E), BF16),
            pltpu.VMEM((SAMPLES, NF, E), BF16),
            pltpu.VMEM((SAMPLES, NF, E), F32),
            pltpu.VMEM((SAMPLES, NF, 128), F32),
            pltpu.VMEM((2, NROW, E), BF16),
            pltpu.VMEM((2, E, NROW), BF16),
            pltpu.VMEM((2, TILES, NROW, TH), BF16),
            pltpu.VMEM((2, TILES, NROW, TH), BF16),
            pltpu.VMEM((2, NROW, E), F32),
            pltpu.VMEM((NROW, E), BF16),
            pltpu.VMEM((NROW, E), BF16),
            pltpu.VMEM((FIELDS, FIELDS), BF16),
            pltpu.VMEM((SAMPLES, NL, E), F32),
            pltpu.VMEM((SAMPLES, FIELDS, E), F32),
            pltpu.VMEM((2, NROW, E), BF16),
            pltpu.VMEM((2, E, NROW), BF16),
            pltpu.VMEM((SAMPLES, NL, E), BF16),
            pltpu.VMEM((NROW, E), BF16),
            pltpu.VMEM((NROW, E), BF16),
            pltpu.VMEM((SAMPLES, FIELDS, E), BF16),
            pltpu.VMEM((2, TILES * 2, 256, 256), BF16),
            pltpu.VMEM((2, TILES * 2, 128, 256), BF16),
            pltpu.VMEM((2, TILES * 2, 128, 256), BF16),
            pltpu.VMEM((2, XS - 1, 4, 128, 256), BF16),
            pltpu.VMEM((2, YS, 128, 256), BF16),
            pltpu.VMEM((2, YS - 1, 128, 256), BF16),
            pltpu.VMEM((2, ZS, 128 // ZS, 256), BF16),
            pltpu.VMEM((2, ZS - 1, 128 // ZS, 256), BF16),
            pltpu.VMEM((2, ZS, 128 // ZS, 256), BF16),
            dma((SLOTS,)),
            dma((8,)),
            dma((EMB,)),
            dma((EMB,)),
            dma((EMB,)),
            dma((EMB,)),
            dma((4, XS - 1)),
            dma((4, XS - 1)),
            dma((4,)),
            dma((4,)),
            dma((2, XS)),
            dma((2, XS)),
            dma((2, 20)),
            dma((2, 20)),
        ],
        compiler_params=pltpu.CompilerParams(
            collective_id=0, has_side_effects=True, vmem_limit_bytes=62 << 20
        ),
    )(*operands)


def finish_kernel(layer_out, bag_grads, whole, layer_final, bag_final, up, down, held, sums, in_sem, out_sem, sum_sem):
    pairs = ((layer_out, layer_final), (bag_grads, bag_final))
    rows = [layer_out.shape[0] // 2, bag_grads.shape[0] // 2]
    incoming, outgoing = [], []
    for n, (src, dst) in enumerate(pairs):
        for half in range(2):
            part = pl.ds(half * rows[n], rows[n])
            here = held[n].at[part]
            incoming.append(pltpu.make_async_copy(src.at[part], here, in_sem.at[n, half]))
            outgoing.append(pltpu.make_async_copy(here, dst.at[part], out_sem.at[n, half]))
    for copy in incoming:
        copy.start()
    sum_copies = []
    for kind, out in enumerate((up, down)):
        for y in range(YS):
            part = pl.ds(y * 256, 256)
            sums[kind, part] = whole[kind, part].astype(F32)
            copy = pltpu.make_async_copy(sums.at[kind, part], out.at[part], sum_sem.at[kind, y])
            copy.start()
            sum_copies.append(copy)
            n = kind * YS + y
            if n % 2 == 1:
                incoming[n // 2].wait()
                outgoing[n // 2].start()
    for copy in outgoing + sum_copies:
        copy.wait()


def finish_outputs(layer_out, bag_grads, whole):
    anywhere = pl.BlockSpec(memory_space=pl.ANY)
    dma = pltpu.SemaphoreType.DMA
    return pl.pallas_call(
        finish_kernel,
        name="finish_outputs",
        out_shape=(
            jax.ShapeDtypeStruct(layer_out.shape, BF16),
            jax.ShapeDtypeStruct(bag_grads.shape, BF16),
            jax.ShapeDtypeStruct((SLICE, E), F32),
            jax.ShapeDtypeStruct((SLICE, E), F32),
        ),
        in_specs=[anywhere, anywhere, pl.BlockSpec(memory_space=pltpu.VMEM)],
        out_specs=(anywhere,) * 4,
        scratch_shapes=[
            [pltpu.VMEM(layer_out.shape, BF16), pltpu.VMEM(bag_grads.shape, BF16)],
            pltpu.VMEM((2, SLICE, E), F32),
            dma((2, 2)),
            dma((2, 2)),
            dma((2, YS)),
        ],
    )(layer_out, bag_grads, whole)


def body(
    tables,
    bag_ids,
    bag_lengths,
    slot_field,
    proj_y,
    proj_p,
    linear_w,
    fm_gain,
    w_up,
    w_down,
    out_gain,
    cotangent,
):
    layer_out, bag_grads, weight_grads = whole_layer(
        bag_ids[0].transpose(1, 2, 0),
        bag_lengths[0].transpose(1, 0),
        slot_field.reshape(1, FIELDS),
        fm_gain.reshape(1, E),
        out_gain.reshape(1, E),
        tables,
        w_up,
        w_down,
        proj_y,
        proj_p,
        linear_w,
        cotangent[0],
    )
    layer_out, bag_grads, grad_up, grad_down = finish_outputs(layer_out, bag_grads, weight_grads)
    return (layer_out[None], bag_grads[None], grad_up, grad_down)


def solution(mesh):
    placed = (
        P("emb", None, None),
        P("wide", None, "emb", None),
        P("wide", None, "emb"),
        P(),
        P(),
        P(),
        P(),
        P(),
        P("wide", None),
        P("wide", None),
        P(),
        P("wide", "emb", None, None),
    )
    return jax.shard_map(
        body,
        mesh=mesh,
        in_specs=placed,
        out_specs=(
            P("wide", "emb", None, None),
            P("wide", None, "emb", None),
            P("wide", None),
            P("wide", None),
        ),
        check_vma=False,
    )
```

```python
import functools

import jax
import jax.numpy as jnp
from jax import lax
from jax.experimental import pallas as pl
from jax.experimental.pallas import tpu as pltpu
from jax.sharding import PartitionSpec as P

MESH = pl.DeviceIdType.MESH
F32 = jnp.float32
BF16 = jnp.bfloat16

E = 256
FIELDS = 512
ROWS = 512
NF = 128
NL = 384
BAG = 4
SAMPLES = 4
SLOTS = 16
GROUP_B = 128
EMB = 32
XS = 4
YS = 4
ZS = 4
SLICE = 1024
TH = 512
TILES = 8
NROW = SAMPLES * NF
norm_eps = 1e-05


def dot(a, b, ca=1, cb=0):
    return lax.dot_general(a, b, (((ca,), (cb,)), ((), ())), preferred_element_type=F32)


def send(src, dst, send_sem, recv_sem, **device):
    return pltpu.make_async_remote_copy(
        src_ref=src,
        dst_ref=dst,
        send_sem=send_sem,
        recv_sem=recv_sem,
        device_id=device,
        device_id_type=MESH,
    )


def signal(sem, **device):
    pl.semaphore_signal(sem, inc=1, device_id=device, device_id_type=MESH)


def norm_forward(values):
    centre = jnp.mean(values, axis=-1, keepdims=True)
    shifted = values - centre
    scale = lax.rsqrt(jnp.mean(shifted * shifted, axis=-1, keepdims=True) + norm_eps)
    return shifted * scale, scale


def norm_back(unit, scale, gain, upstream):
    scaled = upstream * gain
    return scale * (
        scaled
        - jnp.mean(scaled, axis=-1, keepdims=True)
        - unit * jnp.mean(scaled * unit, axis=-1, keepdims=True)
    )


def layer_kernel(
    ids, lengths, field_row, fm_gain, out_gain,
    tables, w_up_hbm, w_down_hbm, proj_y_hbm, proj_p_hbm, linear_w_hbm, cotangent_hbm,
    layer_out_hbm, bag_grads, whole,
    pooled, outgoing, slots, w_up, w_down, proj_y, proj_p, linear_w, cotangent, layer_out,
    embeds, crossed, mixing, inter_unit, inter_scale, rows, rows_t, hidden, slope, ff, ff_out, ff_in,
    by_slot, linear_out, grad_summed, grad_rows, grad_rows_t, grad_lin, norm_out, norm_in,
    slot_grads, grads, from_core, to_x, from_x, to_y, from_y, to_z, from_z, done_z,
    table_sem, local_sem, bag_send, bag_recv, back_send, back_recv, w_send, w_recv, pair_send, pair_recv,
    core_send, core_recv, sum_send, sum_recv,
):
    me = lax.axis_index("emb")
    wide = lax.axis_index("wide")
    x = wide // 2
    z_lo = lax.rem(wide, 2)
    partner = wide + 1 - 2 * z_lo
    core = lax.rem(me, 2)
    y = lax.rem(me // 2, YS)
    z = me // (2 * YS)
    sibling = me + 1 - 2 * core

    def x_at(offset):
        return lax.rem(x + XS + offset, XS)

    def wide_at(x_to):
        return x_to * 2 + z_lo

    def emb_at(z_to, y_to):
        return (z_to * YS + y_to) * 2 + core

    def table(s):
        return hidden.at[s // TILES, s % TILES, :, pl.ds(0, E)]

    def fetch(s):
        return pltpu.make_async_copy(tables.at[s], table(s), table_sem.at[s])

    for s in range(SLOTS):
        fetch(s).start()
    staged = [
        pltpu.make_async_copy(src, dst, local_sem.at[n])
        for n, (src, dst) in enumerate(
            (
                (w_up_hbm, w_up.at[x]),
                (w_down_hbm, w_down.at[x]),
                (proj_y_hbm, proj_y),
                (proj_p_hbm, proj_p),
                (linear_w_hbm, linear_w),
                (cotangent_hbm, cotangent),
            )
        )
    ]
    for copy in staged:
        copy.start()

    barrier = pltpu.get_barrier_semaphore()

    @pl.loop(1, EMB)
    def _(k):
        signal(barrier, emb=lax.rem(me + k, EMB))

    for k in range(1, XS):
        signal(barrier, wide=wide_at(x_at(k)))
    signal(barrier, wide=partner)
    def half_of(which):
        return pl.ds(pl.multiple_of(which * TH, TH), TH)

    weights = ((w_up_hbm, w_up), (w_down_hbm, w_down))
    def weights_from(k):
        if k == 0:
            staged[0].wait()
            staged[1].wait()
            return
        for i, (w, full) in enumerate(weights):
            pass_weights(i, k, 1 - core).wait_recv()
            pass_weights(i, k, core).wait_send()

    def pass_weights(i, k, which):
        part = weights[i][1].at[x_at(-k), half_of(which)]
        return send(part, part, w_send.at[2 + i, k - 1], w_recv.at[2 + i, k - 1], emb=sibling)

    bucket = lax.broadcasted_iota(jnp.int32, (ROWS, GROUP_B), 0)

    for s in range(SLOTS):
        if s == SLOTS // 2:
            pl.semaphore_wait(barrier, EMB - 1 + XS)
            for k in range(1, XS):
                for i, (w, full) in enumerate(weights):
                    send(
                        w.at[half_of(core)],
                        full.at[x, half_of(core)],
                        w_send.at[i, k - 1],
                        w_recv.at[i, k - 1],
                        wide=wide_at(x_at(k)),
                    ).start()
        fetch(s).wait()
        live = lengths[s : s + 1, :]
        counts = jnp.zeros((ROWS, GROUP_B), F32)
        for j in range(BAG):
            wanted = jnp.where(live > j, ids[s, j : j + 1, :], -1)
            counts = counts + jnp.where(bucket == wanted, 1.0, 0.0)
        bags = dot(counts.astype(BF16), table(s)[...], 0, 0)
        for half in range(2):
            pooled[half, pl.ds(s, GROUP_B, stride=SLOTS), :] = bags[:, half * 128 : half * 128 + 128]

    for half in range(2):
        outgoing[:, :, half * 128 : half * 128 + 128] = (
            pooled[half].astype(BF16).reshape(GROUP_B, SLOTS, 128)
        )

    def slots_at(owner):
        return pl.ds(pl.multiple_of(owner * SLOTS, SLOTS), SLOTS)

    def samples_at(owner):
        return pl.ds(owner * SAMPLES, SAMPLES)

    @pl.loop(1, EMB)
    def _(k):
        peer = lax.rem(me + k, EMB)
        send(
            outgoing.at[samples_at(peer)], slots.at[:, slots_at(me), :], bag_send.at[k], bag_recv.at[k], emb=peer
        ).start()

    slots[:, slots_at(me), :] = outgoing[samples_at(me)]

    by_field = jnp.where(
        lax.broadcasted_iota(jnp.int32, (FIELDS, FIELDS), 0) == field_row[...], 1.0, 0.0
    ).astype(BF16)
    by_slot[...] = by_field.astype(F32).T.astype(BF16)
    for copy in staged[2:]:
        copy.wait()

    for k in (1, 3, 2):
        for i, (w, full) in enumerate(weights):
            copy = send(
                w.at[half_of(core)],
                full.at[x_at(-k), half_of(core)],
                w_send.at[i, k - 1],
                w_recv.at[i, k - 1],
                wide=wide_at(x_at(-k)),
            )
            copy.wait_recv()
            copy.wait_send()
            pass_weights(i, k, core).start()

    @pl.loop(1, EMB)
    def _(k):
        source = lax.rem(me + EMB - k, EMB)
        copy = send(
            outgoing.at[samples_at(source)],
            slots.at[:, slots_at(source), :],
            bag_send.at[k],
            bag_recv.at[k],
            emb=source,
        )
        copy.wait_recv()
        copy.wait_send()

    def exchange(src, dst, n):
        return send(src, dst, pair_send.at[n], pair_recv.at[n], wide=partner)

    def rows_of(b):
        return pl.ds(pl.multiple_of(b * NF, NF), NF)

    def embed(b, _):
        sample = dot(by_field, slots[b]).astype(BF16)
        embeds[b] = sample
        cross = dot(sample, proj_y[...], 0, 0).astype(BF16)
        crossed[b] = cross
        mix = dot(proj_p[...], sample).astype(BF16)
        mixing[b] = mix
        unit, scale = norm_forward(dot(mix, cross))
        inter_unit[b] = unit
        inter_scale[b] = jnp.broadcast_to(scale, (NF, 128))
        rows[0, rows_of(b), :] = (unit * fm_gain[...]).astype(BF16)
        return 0

    lax.fori_loop(0, SAMPLES, embed, 0)
    rows_copy = exchange(rows.at[0], rows.at[1], 0)
    rows_copy.start()
    ff[...] = jnp.zeros_like(ff)

    def forward(group, k):
        chunk = x_at(-k)

        @pl.loop(0, 2)
        def _(t):
            tile = chunk * 2 + t
            here = pl.ds(pl.multiple_of(t * TH, TH), TH)
            gate = dot(rows[group], w_up[chunk, here, :], 1, 1)
            sigma = 0.5 * jnp.tanh(0.5 * gate) + 0.5
            act = gate * sigma
            slope[group, tile] = (sigma + act * (1.0 - sigma)).astype(BF16)
            act = act.astype(BF16)
            hidden[group, tile] = act
            ff[group] += dot(act, w_down[chunk, here, :])

    weights_from(0)
    forward(0, 0)

    def linear(b, _):
        linear_out[b] = dot(linear_w[...], embeds[b])
        return 0

    lax.fori_loop(0, SAMPLES, linear, 0)
    rows_copy.wait()
    forward(1, 0)
    for k in range(1, XS):
        weights_from(k)
        forward(1, k)
    ff_out[...] = ff[1].astype(BF16)
    ff_copy = exchange(ff_out, ff_in, 1)
    ff_copy.start()
    for k in range(1, XS):
        forward(0, k)
    rows_t[0] = rows[0].astype(F32).T.astype(BF16)
    rows_t[1] = rows[1].astype(F32).T.astype(BF16)
    ff_copy.wait()

    def finish(values, b, first, count):
        here = slice(first, first + count)
        unit, scale = norm_forward(values + embeds[b, here, :].astype(F32))
        layer_out[b, here, :] = (unit * out_gain[...]).astype(BF16)
        grad = norm_back(unit, scale, out_gain[...], cotangent[b, here, :].astype(F32))
        grad_summed[b, here, :] = grad
        return grad.astype(BF16)

    def finish_ff(b, _):
        total = ff[0, rows_of(b), :] + ff_in[rows_of(b), :].astype(F32)
        grad_rows[0, rows_of(b), :] = finish(total, b, 0, NF)
        return 0

    lax.fori_loop(0, SAMPLES, finish_ff, 0)
    grad_copy = exchange(grad_rows.at[0], grad_rows.at[1], 2)
    grad_copy.start()

    def finish_linear(b, _):
        grad_lin[b] = finish(linear_out[b], b, NF, NL)
        grad_summed[b] += dot(linear_w[...], grad_lin[b], 0, 0)
        return 0

    lax.fori_loop(0, SAMPLES, finish_linear, 0)
    layer_copy = pltpu.make_async_copy(layer_out, layer_out_hbm, local_sem.at[6])
    layer_copy.start()
    grad_rows_t[0] = grad_rows[0].astype(F32).T.astype(BF16)
    ff[...] = jnp.zeros_like(ff)
    grad_copy.wait()
    grad_rows_t[1] = grad_rows[1].astype(F32).T.astype(BF16)

    def gate_back(group, chunk, t):
        here = pl.ds(pl.multiple_of(t * TH, TH), TH)
        tile = chunk * 2 + t
        grad_hidden = dot(grad_rows[group], w_down[chunk, here, :], 1, 1)
        grad_gate = (grad_hidden * slope[group, tile].astype(F32)).astype(BF16)
        ff[group] += dot(grad_gate, w_up[chunk, here, :])
        return grad_gate

    k_mine = pl.ds(pl.multiple_of(core * 128, 128), 128)
    k_other = pl.ds(pl.multiple_of(128 - core * 128, 128), 128)

    def keep(kind, tile, part):
        part = part.astype(BF16)
        for half in range(2):
            grads[kind, tile * 2 + half] = part[:, half * 256 : half * 256 + 256]

    def over_cores(kind, k):
        chunk = pl.ds(x_at(k) * 4, 4)
        return send(
            grads.at[kind, chunk, k_other],
            from_core.at[kind, chunk],
            core_send.at[kind, k],
            core_recv.at[kind, k],
            emb=sibling,
        )

    def over_x(kind, k):
        return send(
            to_x.at[kind, pl.ds(x_at(k) * 4, 4)],
            from_x.at[kind, k - 1],
            sum_send.at[kind, k],
            sum_recv.at[kind, k],
            wide=wide_at(x_at(k)),
        )

    def over_y(kind, k):
        peer = lax.rem(y + k, YS)
        return send(
            to_y.at[kind, peer],
            from_y.at[kind, k - 1],
            sum_send.at[kind, 3 + k],
            sum_recv.at[kind, 3 + k],
            emb=emb_at(z, peer),
        )

    def over_z(kind, k):
        peer = lax.rem(z + k, ZS)
        return send(
            to_z.at[kind, peer],
            from_z.at[kind, k - 1],
            sum_send.at[kind, 6 + k],
            sum_recv.at[kind, 6 + k],
            emb=emb_at(peer, y),
        )

    def along_z(kind, k, z_of, z_to):
        part = done_z.at[kind, z_of]
        return send(part, part, sum_send.at[kind, 9 + k], sum_recv.at[kind, 9 + k], emb=emb_at(z_to, y))

    def band(kind, y_of, columns):
        return whole.at[kind, pl.ds(pl.multiple_of(y_of * 256, 256), 256), columns]

    def along_y(kind, k, y_of, y_to):
        part = band(kind, y_of, k_mine)
        return send(part, part, sum_send.at[kind, 12 + k], sum_recv.at[kind, 12 + k], emb=emb_at(z, y_to))

    def to_sibling(kind, k, columns):
        part = band(kind, lax.rem(y + YS - k, YS), columns)
        return send(part, part, sum_send.at[kind, 16 + k], sum_recv.at[kind, 16 + k], emb=sibling)

    def pass_on(kind, k):
        over_cores(kind, k).wait()

        @pl.loop(0, 4)
        def _(t):
            part = x_at(k) * 4 + t
            to_x[kind, part] = (
                grads[kind, part, k_mine].astype(F32) + from_core[kind, part].astype(F32)
            ).astype(BF16)

        over_x(kind, k).start()

    def sum_x(kind):
        over_cores(kind, 0).wait()
        for k in range(1, XS):
            over_x(kind, k).wait()

        @pl.loop(0, 4)
        def _(t):
            mine = x * 4 + t
            total = grads[kind, mine, k_mine].astype(F32) + from_core[kind, mine].astype(F32)
            for k in range(XS - 1):
                total = total + from_x[kind, k, t].astype(F32)
            to_y[kind, t] = total.astype(BF16)

        for k in range(1, YS):
            over_y(kind, k).start()

    def sum_y(kind):
        for k in range(1, YS):
            over_y(kind, k).wait()
        total = to_y[kind, y].astype(F32)
        for k in range(YS - 1):
            total = total + from_y[kind, k].astype(F32)
        to_z[kind] = total.astype(BF16).reshape(ZS, 128 // ZS, 256)
        for k in range(1, ZS):
            over_z(kind, k).start()

    def sum_z(kind):
        for k in range(1, ZS):
            over_z(kind, k).wait()
        total = to_z[kind, z].astype(F32)
        for k in range(ZS - 1):
            total = total + from_z[kind, k].astype(F32)
        done_z[kind, z] = total.astype(BF16)
        for k in range(1, ZS):
            along_z(kind, k, z, lax.rem(z + k, ZS)).start()

    def spread_y(kind):
        for k in range(1, ZS):
            source = lax.rem(z + ZS - k, ZS)
            along_z(kind, k, z, source).wait_send()
            along_z(kind, k, source, source).wait_recv()
        part = done_z[kind].reshape(128, 256).astype(F32).T.astype(BF16)
        whole[kind, pl.ds(pl.multiple_of(y * 256, 256), 256), k_mine] = part
        for k in range(1, YS):
            along_y(kind, k, y, lax.rem(y + k, YS)).start()
        to_sibling(kind, 0, k_mine).start()

    def spread_cores(kind):
        for k in range(1, YS):
            source = lax.rem(y + YS - k, YS)
            along_y(kind, k, source, source).wait_recv()
            to_sibling(kind, k, k_mine).start()

    def settle(kind):
        for k in range(1, YS):
            along_y(kind, k, y, lax.rem(y + k, YS)).wait_send()
        for k in range(YS):
            to_sibling(kind, k, k_mine).wait_send()
            to_sibling(kind, k, k_other).wait_recv()

    order = (1, 2, 3, 0)
    for k in order:

        @pl.loop(0, 2)
        def _(t):
            tile = x_at(k) * 2 + t
            keep(1, tile, dot(grad_rows_t[0], hidden[0, tile]) + dot(grad_rows_t[1], hidden[1, tile]))

        over_cores(1, k).start()

    def both_back(k, t):
        tile = x_at(k) * 2 + t
        theirs = gate_back(1, x_at(k), t)
        mine = gate_back(0, x_at(k), t)
        keep(0, tile, dot(rows_t[0], mine) + dot(rows_t[1], theirs))

    def chunk_back(k):
        @pl.loop(0, 2)
        def _(t):
            both_back(k, t)

        over_cores(0, k).start()

    pass_on(1, 1)
    pass_on(1, 2)
    chunk_back(1)
    pass_on(1, 3)
    chunk_back(2)
    pass_on(0, 1)
    chunk_back(3)
    pass_on(0, 2)
    both_back(0, 0)
    pass_on(0, 3)
    sum_x(1)
    both_back(0, 1)
    over_cores(0, 0).start()
    norm_out[...] = ff[1].astype(BF16)
    norm_copy = exchange(norm_out, norm_in, 3)
    norm_copy.start()
    sum_y(1)
    sum_x(0)
    norm_copy.wait()

    def tail(b, _):
        upstream = ff[0, rows_of(b), :] + norm_in[rows_of(b), :].astype(F32)
        grad_inter = norm_back(inter_unit[b], inter_scale[b, :, 0:1], fm_gain[...], upstream).astype(BF16)
        grad_mixing = dot(grad_inter, crossed[b], 1, 1).astype(BF16)
        grad_crossed = dot(mixing[b], grad_inter, 0, 0).astype(BF16)
        total = grad_summed[b] + dot(proj_p[...], grad_mixing, 0, 0)
        total = total + dot(proj_y[...], grad_crossed, 1, 1)
        slot_grads[b] = dot(by_slot[...], total.astype(BF16)).astype(BF16)
        return 0

    lax.fori_loop(0, SAMPLES // 2, tail, 0)
    sum_z(1)
    sum_y(0)
    lax.fori_loop(SAMPLES // 2, SAMPLES, tail, 0)

    def bags_back(first, last):
        @pl.loop(first, last)
        def _(k):
            peer = lax.rem(me + k, EMB)
            send(
                slot_grads.at[:, slots_at(peer), :],
                bag_grads.at[samples_at(me)],
                back_send.at[k],
                back_recv.at[k],
                emb=peer,
            ).start()

    bags_back(1, 8)
    own_bags = pltpu.make_async_copy(
        slot_grads.at[:, slots_at(me), :], bag_grads.at[samples_at(me)], local_sem.at[7]
    )
    own_bags.start()
    sum_z(0)
    bags_back(8, 16)
    spread_y(1)
    bags_back(16, 24)
    spread_y(0)
    bags_back(24, EMB)
    spread_cores(1)
    spread_cores(0)
    settle(1)
    settle(0)

    @pl.loop(1, EMB)
    def _(k):
        source = lax.rem(me + EMB - k, EMB)
        copy = send(
            slot_grads.at[:, slots_at(source), :],
            bag_grads.at[samples_at(source)],
            back_send.at[k],
            back_recv.at[k],
            emb=source,
        )
        copy.wait_recv()
        copy.wait_send()

    own_bags.wait()
    layer_copy.wait()


def whole_layer(*operands):
    anywhere = pl.BlockSpec(memory_space=pl.ANY)
    vmem = pl.BlockSpec(memory_space=pltpu.VMEM)
    dma = pltpu.SemaphoreType.DMA
    return pl.pallas_call(
        layer_kernel,
        name="whole_layer",
        out_shape=(
            jax.ShapeDtypeStruct((SAMPLES, FIELDS, E), BF16),
            jax.ShapeDtypeStruct((GROUP_B, SLOTS, E), BF16),
            jax.ShapeDtypeStruct((2, SLICE, E), BF16),
        ),
        in_specs=[vmem] * 5 + [anywhere] * 7,
        out_specs=(anywhere, anywhere, vmem),
        scratch_shapes=[
            pltpu.VMEM((2, GROUP_B * SLOTS, 128), F32),
            pltpu.VMEM((GROUP_B, SLOTS, E), BF16),
            pltpu.VMEM((SAMPLES, FIELDS, E), BF16),
            pltpu.VMEM((XS, SLICE, E), BF16),
            pltpu.VMEM((XS, SLICE, E), BF16),
            pltpu.VMEM((FIELDS, E), BF16),
            pltpu.VMEM((NF, FIELDS), BF16),
            pltpu.VMEM((NL, FIELDS), BF16),
            pltpu.VMEM((SAMPLES, FIELDS, E), BF16),
            pltpu.VMEM((SAMPLES, FIELDS, E), BF16),
            pltpu.VMEM((SAMPLES, FIELDS, E), BF16),
            pltpu.VMEM((SAMPLES, E, E), BF16),
            pltpu.VMEM((SAMPLES, NF, E), BF16),
            pltpu.VMEM((SAMPLES, NF, E), F32),
            pltpu.VMEM((SAMPLES, NF, 128), F32),
            pltpu.VMEM((2, NROW, E), BF16),
            pltpu.VMEM((2, E, NROW), BF16),
            pltpu.VMEM((2, TILES, NROW, TH), BF16),
            pltpu.VMEM((2, TILES, NROW, TH), BF16),
            pltpu.VMEM((2, NROW, E), F32),
            pltpu.VMEM((NROW, E), BF16),
            pltpu.VMEM((NROW, E), BF16),
            pltpu.VMEM((FIELDS, FIELDS), BF16),
            pltpu.VMEM((SAMPLES, NL, E), F32),
            pltpu.VMEM((SAMPLES, FIELDS, E), F32),
            pltpu.VMEM((2, NROW, E), BF16),
            pltpu.VMEM((2, E, NROW), BF16),
            pltpu.VMEM((SAMPLES, NL, E), BF16),
            pltpu.VMEM((NROW, E), BF16),
            pltpu.VMEM((NROW, E), BF16),
            pltpu.VMEM((SAMPLES, FIELDS, E), BF16),
            pltpu.VMEM((2, TILES * 2, 256, 256), BF16),
            pltpu.VMEM((2, TILES * 2, 128, 256), BF16),
            pltpu.VMEM((2, TILES * 2, 128, 256), BF16),
            pltpu.VMEM((2, XS - 1, 4, 128, 256), BF16),
            pltpu.VMEM((2, YS, 128, 256), BF16),
            pltpu.VMEM((2, YS - 1, 128, 256), BF16),
            pltpu.VMEM((2, ZS, 128 // ZS, 256), BF16),
            pltpu.VMEM((2, ZS - 1, 128 // ZS, 256), BF16),
            pltpu.VMEM((2, ZS, 128 // ZS, 256), BF16),
            dma((SLOTS,)),
            dma((8,)),
            dma((EMB,)),
            dma((EMB,)),
            dma((EMB,)),
            dma((EMB,)),
            dma((4, XS - 1)),
            dma((4, XS - 1)),
            dma((4,)),
            dma((4,)),
            dma((2, XS)),
            dma((2, XS)),
            dma((2, 20)),
            dma((2, 20)),
        ],
        compiler_params=pltpu.CompilerParams(
            collective_id=0, has_side_effects=True, vmem_limit_bytes=62 << 20
        ),
    )(*operands)


def finish_kernel(
    layer_out, bag_grads, whole, layer_final, bag_final, up, down, held, sums_in, sums, in_sem, out_sem, sum_sem,
):
    pairs = ((layer_out, layer_final), (bag_grads, bag_final))
    rows = [layer_out.shape[0] // 2, bag_grads.shape[0] // 2]
    incoming, outgoing = [], []
    for n, (src, dst) in enumerate(pairs):
        for half in range(2):
            part = pl.ds(half * rows[n], rows[n])
            here = held[n].at[part]
            incoming.append(pltpu.make_async_copy(src.at[part], here, in_sem.at[n, half]))
            outgoing.append(pltpu.make_async_copy(here, dst.at[part], out_sem.at[n, half]))
    sums_copies = [pltpu.make_async_copy(whole.at[kind], sums_in.at[kind], in_sem.at[2, kind]) for kind in range(2)]
    for copy in sums_copies + incoming:
        copy.start()
    sum_copies = []
    for kind, out in enumerate((up, down)):
        sums_copies[kind].wait()
        for y in range(YS):
            part = pl.ds(y * 256, 256)
            sums[kind, part] = sums_in[kind, part].astype(F32)
            copy = pltpu.make_async_copy(sums.at[kind, part], out.at[part], sum_sem.at[kind, y])
            copy.start()
            sum_copies.append(copy)
            n = kind * YS + y
            if n % 2 == 1:
                incoming[n // 2].wait()
                outgoing[n // 2].start()
    for copy in outgoing + sum_copies:
        copy.wait()


def finish_outputs(layer_out, bag_grads, whole):
    anywhere = pl.BlockSpec(memory_space=pl.ANY)
    dma = pltpu.SemaphoreType.DMA
    return pl.pallas_call(
        finish_kernel,
        name="finish_outputs",
        out_shape=(
            jax.ShapeDtypeStruct(layer_out.shape, BF16),
            jax.ShapeDtypeStruct(bag_grads.shape, BF16),
            jax.ShapeDtypeStruct((SLICE, E), F32),
            jax.ShapeDtypeStruct((SLICE, E), F32),
        ),
        in_specs=[anywhere] * 3,
        out_specs=(anywhere,) * 4,
        scratch_shapes=[
            [pltpu.VMEM(layer_out.shape, BF16), pltpu.VMEM(bag_grads.shape, BF16)],
            pltpu.VMEM((2, SLICE, E), BF16),
            pltpu.VMEM((2, SLICE, E), F32),
            dma((3, 2)),
            dma((2, 2)),
            dma((2, YS)),
        ],
    )(layer_out, bag_grads, whole)


def body(
    tables,
    bag_ids,
    bag_lengths,
    slot_field,
    proj_y,
    proj_p,
    linear_w,
    fm_gain,
    w_up,
    w_down,
    out_gain,
    cotangent,
):
    layer_out, bag_grads, weight_grads = whole_layer(
        bag_ids[0].transpose(1, 2, 0),
        bag_lengths[0].transpose(1, 0),
        slot_field.reshape(1, FIELDS),
        fm_gain.reshape(1, E),
        out_gain.reshape(1, E),
        tables,
        w_up,
        w_down,
        proj_y,
        proj_p,
        linear_w,
        cotangent[0],
    )
    layer_out, bag_grads, grad_up, grad_down = finish_outputs(layer_out, bag_grads, weight_grads)
    return (layer_out[None], bag_grads[None], grad_up, grad_down)


def solution(mesh):
    placed = (
        P("emb", None, None),
        P("wide", None, "emb", None),
        P("wide", None, "emb"),
        P(),
        P(),
        P(),
        P(),
        P(),
        P("wide", None),
        P("wide", None),
        P(),
        P("wide", "emb", None, None),
    )
    return jax.shard_map(
        body,
        mesh=mesh,
        in_specs=placed,
        out_specs=(
            P("wide", "emb", None, None),
            P("wide", None, "emb", None),
            P("wide", None),
            P("wide", None),
        ),
        check_vma=False,
    )
```

```python
import functools

import jax
import jax.numpy as jnp
from jax import lax
from jax.experimental import pallas as pl
from jax.experimental.pallas import tpu as pltpu
from jax.sharding import PartitionSpec as P

MESH = pl.DeviceIdType.MESH
F32 = jnp.float32
BF16 = jnp.bfloat16

E = 256
FIELDS = 512
ROWS = 512
NF = 128
NL = 384
BAG = 4
SAMPLES = 4
SLOTS = 16
GROUP_B = 128
EMB = 32
STEP = 11
XS = 4
YS = 4
ZS = 4
SLICE = 1024
TH = 512
TILES = 8
NROW = SAMPLES * NF
norm_eps = 1e-05


def dot(a, b, ca=1, cb=0):
    return lax.dot_general(a, b, (((ca,), (cb,)), ((), ())), preferred_element_type=F32)


def send(src, dst, send_sem, recv_sem, **device):
    return pltpu.make_async_remote_copy(
        src_ref=src,
        dst_ref=dst,
        send_sem=send_sem,
        recv_sem=recv_sem,
        device_id=device,
        device_id_type=MESH,
    )


def signal(sem, **device):
    pl.semaphore_signal(sem, inc=1, device_id=device, device_id_type=MESH)


def norm_forward(values):
    centre = jnp.mean(values, axis=-1, keepdims=True)
    shifted = values - centre
    scale = lax.rsqrt(jnp.mean(shifted * shifted, axis=-1, keepdims=True) + norm_eps)
    return shifted * scale, scale


def norm_back(unit, scale, gain, upstream):
    scaled = upstream * gain
    return scale * (
        scaled
        - jnp.mean(scaled, axis=-1, keepdims=True)
        - unit * jnp.mean(scaled * unit, axis=-1, keepdims=True)
    )


def layer_kernel(
    ids, lengths, field_row, fm_gain, out_gain,
    tables, w_up_hbm, w_down_hbm, proj_y_hbm, proj_p_hbm, linear_w_hbm, cotangent_hbm,
    layer_out_hbm, bag_grads, whole,
    pooled, outgoing, slots, w_up, w_down, proj_y, proj_p, linear_w, cotangent, layer_out,
    embeds, crossed, mixing, inter_unit, inter_scale, rows, rows_t, hidden, slope, ff, ff_out, ff_in,
    by_slot, linear_out, grad_summed, grad_rows, grad_rows_t, grad_lin, norm_out, norm_in,
    slot_grads, grads, from_core, to_x, from_x, to_y, from_y, to_z, from_z, done_z,
    table_sem, local_sem, bag_send, bag_recv, back_send, back_recv, w_send, w_recv, pair_send, pair_recv,
    core_send, core_recv, sum_send, sum_recv,
):
    me = lax.axis_index("emb")
    wide = lax.axis_index("wide")
    x = wide // 2
    z_lo = lax.rem(wide, 2)
    partner = wide + 1 - 2 * z_lo
    core = lax.rem(me, 2)
    y = lax.rem(me // 2, YS)
    z = me // (2 * YS)
    sibling = me + 1 - 2 * core

    def peer_at(k):
        return lax.rem(me + lax.rem(k * STEP, EMB), EMB)

    def x_at(offset):
        return lax.rem(x + XS + offset, XS)

    def wide_at(x_to):
        return x_to * 2 + z_lo

    def emb_at(z_to, y_to):
        return (z_to * YS + y_to) * 2 + core

    def table(s):
        return hidden.at[s // TILES, s % TILES, :, pl.ds(0, E)]

    def fetch(s):
        return pltpu.make_async_copy(tables.at[s], table(s), table_sem.at[s])

    for s in range(SLOTS):
        fetch(s).start()
    staged = [
        pltpu.make_async_copy(src, dst, local_sem.at[n])
        for n, (src, dst) in enumerate(
            (
                (w_up_hbm, w_up.at[x]),
                (w_down_hbm, w_down.at[x]),
                (proj_y_hbm, proj_y),
                (proj_p_hbm, proj_p),
                (linear_w_hbm, linear_w),
                (cotangent_hbm, cotangent),
            )
        )
    ]
    for copy in staged:
        copy.start()

    barrier = pltpu.get_barrier_semaphore()

    @pl.loop(1, EMB)
    def _(k):
        signal(barrier, emb=lax.rem(me + k, EMB))

    for k in range(1, XS):
        signal(barrier, wide=wide_at(x_at(k)))
    signal(barrier, wide=partner)
    def half_of(which):
        return pl.ds(pl.multiple_of(which * TH, TH), TH)

    weights = ((w_up_hbm, w_up), (w_down_hbm, w_down))
    def weights_from(k):
        if k == 0:
            staged[0].wait()
            staged[1].wait()
            return
        for i, (w, full) in enumerate(weights):
            pass_weights(i, k, 1 - core).wait_recv()
            pass_weights(i, k, core).wait_send()

    def pass_weights(i, k, which):
        part = weights[i][1].at[x_at(-k), half_of(which)]
        return send(part, part, w_send.at[2 + i, k - 1], w_recv.at[2 + i, k - 1], emb=sibling)

    bucket = lax.broadcasted_iota(jnp.int32, (ROWS, GROUP_B), 0)

    for s in range(SLOTS):
        if s == SLOTS // 2:
            pl.semaphore_wait(barrier, EMB - 1 + XS)
            for k in range(1, XS):
                for i, (w, full) in enumerate(weights):
                    send(
                        w.at[half_of(core)],
                        full.at[x, half_of(core)],
                        w_send.at[i, k - 1],
                        w_recv.at[i, k - 1],
                        wide=wide_at(x_at(k)),
                    ).start()
        fetch(s).wait()
        live = lengths[s : s + 1, :]
        counts = jnp.zeros((ROWS, GROUP_B), F32)
        for j in range(BAG):
            wanted = jnp.where(live > j, ids[s, j : j + 1, :], -1)
            counts = counts + jnp.where(bucket == wanted, 1.0, 0.0)
        bags = dot(counts.astype(BF16), table(s)[...], 0, 0)
        for half in range(2):
            pooled[half, pl.ds(s, GROUP_B, stride=SLOTS), :] = bags[:, half * 128 : half * 128 + 128]

    for half in range(2):
        outgoing[:, :, half * 128 : half * 128 + 128] = (
            pooled[half].astype(BF16).reshape(GROUP_B, SLOTS, 128)
        )

    def slots_at(owner):
        return pl.ds(pl.multiple_of(owner * SLOTS, SLOTS), SLOTS)

    def samples_at(owner):
        return pl.ds(owner * SAMPLES, SAMPLES)

    @pl.loop(1, EMB)
    def _(k):
        peer = peer_at(k)
        send(
            outgoing.at[samples_at(peer)], slots.at[:, slots_at(me), :], bag_send.at[k], bag_recv.at[k], emb=peer
        ).start()

    slots[:, slots_at(me), :] = outgoing[samples_at(me)]

    by_field = jnp.where(
        lax.broadcasted_iota(jnp.int32, (FIELDS, FIELDS), 0) == field_row[...], 1.0, 0.0
    ).astype(BF16)
    by_slot[...] = by_field.astype(F32).T.astype(BF16)
    for copy in staged[2:]:
        copy.wait()

    for k in (1, 3, 2):
        for i, (w, full) in enumerate(weights):
            copy = send(
                w.at[half_of(core)],
                full.at[x_at(-k), half_of(core)],
                w_send.at[i, k - 1],
                w_recv.at[i, k - 1],
                wide=wide_at(x_at(-k)),
            )
            copy.wait_recv()
            copy.wait_send()
            pass_weights(i, k, core).start()

    @pl.loop(1, EMB)
    def _(k):
        source = lax.rem(me + EMB - lax.rem(k * STEP, EMB), EMB)
        copy = send(
            outgoing.at[samples_at(source)],
            slots.at[:, slots_at(source), :],
            bag_send.at[k],
            bag_recv.at[k],
            emb=source,
        )
        copy.wait_recv()
        copy.wait_send()

    def exchange(src, dst, n):
        return send(src, dst, pair_send.at[n], pair_recv.at[n], wide=partner)

    def rows_of(b):
        return pl.ds(pl.multiple_of(b * NF, NF), NF)

    def embed(b, _):
        sample = dot(by_field, slots[b]).astype(BF16)
        embeds[b] = sample
        cross = dot(sample, proj_y[...], 0, 0).astype(BF16)
        crossed[b] = cross
        mix = dot(proj_p[...], sample).astype(BF16)
        mixing[b] = mix
        unit, scale = norm_forward(dot(mix, cross))
        inter_unit[b] = unit
        inter_scale[b] = jnp.broadcast_to(scale, (NF, 128))
        rows[0, rows_of(b), :] = (unit * fm_gain[...]).astype(BF16)
        return 0

    lax.fori_loop(0, SAMPLES, embed, 0)
    rows_copy = exchange(rows.at[0], rows.at[1], 0)
    rows_copy.start()
    ff[...] = jnp.zeros_like(ff)

    def forward(group, k):
        chunk = x_at(-k)

        @pl.loop(0, 2, unroll=True)
        def _(t):
            tile = chunk * 2 + t
            here = pl.ds(pl.multiple_of(t * TH, TH), TH)
            gate = dot(rows[group], w_up[chunk, here, :], 1, 1)
            sigma = 0.5 * jnp.tanh(0.5 * gate) + 0.5
            act = gate * sigma
            slope[group, tile] = (sigma + act * (1.0 - sigma)).astype(BF16)
            act = act.astype(BF16)
            hidden[group, tile] = act
            ff[group] += dot(act, w_down[chunk, here, :])

    weights_from(0)
    forward(0, 0)

    def linear(b, _):
        linear_out[b] = dot(linear_w[...], embeds[b])
        return 0

    lax.fori_loop(0, SAMPLES, linear, 0)
    rows_copy.wait()
    forward(1, 0)
    for k in range(1, XS):
        weights_from(k)
        forward(1, k)
    ff_out[...] = ff[1].astype(BF16)
    ff_copy = exchange(ff_out, ff_in, 1)
    ff_copy.start()
    for k in range(1, XS):
        forward(0, k)
    rows_t[0] = rows[0].astype(F32).T.astype(BF16)
    rows_t[1] = rows[1].astype(F32).T.astype(BF16)
    ff_copy.wait()

    def finish(values, b, first, count):
        here = slice(first, first + count)
        unit, scale = norm_forward(values + embeds[b, here, :].astype(F32))
        layer_out[b, here, :] = (unit * out_gain[...]).astype(BF16)
        grad = norm_back(unit, scale, out_gain[...], cotangent[b, here, :].astype(F32))
        grad_summed[b, here, :] = grad
        return grad.astype(BF16)

    def finish_ff(b, _):
        total = ff[0, rows_of(b), :] + ff_in[rows_of(b), :].astype(F32)
        grad_rows[0, rows_of(b), :] = finish(total, b, 0, NF)
        return 0

    lax.fori_loop(0, SAMPLES, finish_ff, 0)
    grad_copy = exchange(grad_rows.at[0], grad_rows.at[1], 2)
    grad_copy.start()

    def finish_linear(b, _):
        grad_lin[b] = finish(linear_out[b], b, NF, NL)
        grad_summed[b] += dot(linear_w[...], grad_lin[b], 0, 0)
        return 0

    lax.fori_loop(0, SAMPLES, finish_linear, 0)
    layer_copy = pltpu.make_async_copy(layer_out, layer_out_hbm, local_sem.at[6])
    layer_copy.start()
    grad_rows_t[0] = grad_rows[0].astype(F32).T.astype(BF16)
    ff[...] = jnp.zeros_like(ff)
    grad_copy.wait()
    grad_rows_t[1] = grad_rows[1].astype(F32).T.astype(BF16)

    def gate_back(group, chunk, t):
        here = pl.ds(pl.multiple_of(t * TH, TH), TH)
        tile = chunk * 2 + t
        grad_hidden = dot(grad_rows[group], w_down[chunk, here, :], 1, 1)
        grad_gate = (grad_hidden * slope[group, tile].astype(F32)).astype(BF16)
        ff[group] += dot(grad_gate, w_up[chunk, here, :])
        return grad_gate

    k_mine = pl.ds(pl.multiple_of(core * 128, 128), 128)
    k_other = pl.ds(pl.multiple_of(128 - core * 128, 128), 128)

    def keep(kind, tile, part):
        part = part.astype(BF16)
        for half in range(2):
            grads[kind, tile * 2 + half] = part[:, half * 256 : half * 256 + 256]

    def over_cores(kind, k):
        chunk = pl.ds(x_at(k) * 4, 4)
        return send(
            grads.at[kind, chunk, k_other],
            from_core.at[kind, chunk],
            core_send.at[kind, k],
            core_recv.at[kind, k],
            emb=sibling,
        )

    def over_x(kind, k):
        return send(
            to_x.at[kind, pl.ds(x_at(k) * 4, 4)],
            from_x.at[kind, k - 1],
            sum_send.at[kind, k],
            sum_recv.at[kind, k],
            wide=wide_at(x_at(k)),
        )

    def over_y(kind, k):
        peer = lax.rem(y + k, YS)
        return send(
            to_y.at[kind, peer],
            from_y.at[kind, k - 1],
            sum_send.at[kind, 3 + k],
            sum_recv.at[kind, 3 + k],
            emb=emb_at(z, peer),
        )

    def over_z(kind, k):
        peer = lax.rem(z + k, ZS)
        return send(
            to_z.at[kind, peer],
            from_z.at[kind, k - 1],
            sum_send.at[kind, 6 + k],
            sum_recv.at[kind, 6 + k],
            emb=emb_at(peer, y),
        )

    def along_z(kind, k, z_of, z_to):
        part = done_z.at[kind, z_of]
        return send(part, part, sum_send.at[kind, 9 + k], sum_recv.at[kind, 9 + k], emb=emb_at(z_to, y))

    def band(kind, y_of, columns):
        return whole.at[kind, pl.ds(pl.multiple_of(y_of * 256, 256), 256), columns]

    def along_y(kind, k, y_of, y_to):
        part = band(kind, y_of, k_mine)
        return send(part, part, sum_send.at[kind, 12 + k], sum_recv.at[kind, 12 + k], emb=emb_at(z, y_to))

    def to_sibling(kind, k, columns):
        part = band(kind, lax.rem(y + YS - k, YS), columns)
        return send(part, part, sum_send.at[kind, 16 + k], sum_recv.at[kind, 16 + k], emb=sibling)

    def pass_on(kind, k):
        over_cores(kind, k).wait()

        @pl.loop(0, 4)
        def _(t):
            part = x_at(k) * 4 + t
            to_x[kind, part] = (
                grads[kind, part, k_mine].astype(F32) + from_core[kind, part].astype(F32)
            ).astype(BF16)

        over_x(kind, k).start()

    def sum_x(kind):
        over_cores(kind, 0).wait()
        for k in range(1, XS):
            over_x(kind, k).wait()

        @pl.loop(0, 4)
        def _(t):
            mine = x * 4 + t
            total = grads[kind, mine, k_mine].astype(F32) + from_core[kind, mine].astype(F32)
            for k in range(XS - 1):
                total = total + from_x[kind, k, t].astype(F32)
            to_y[kind, t] = total.astype(BF16)

        for k in range(1, YS):
            over_y(kind, k).start()

    def sum_y(kind):
        for k in range(1, YS):
            over_y(kind, k).wait()
        total = to_y[kind, y].astype(F32)
        for k in range(YS - 1):
            total = total + from_y[kind, k].astype(F32)
        to_z[kind] = total.astype(BF16).reshape(ZS, 128 // ZS, 256)
        for k in range(1, ZS):
            over_z(kind, k).start()

    def sum_z(kind):
        for k in range(1, ZS):
            over_z(kind, k).wait()
        total = to_z[kind, z].astype(F32)
        for k in range(ZS - 1):
            total = total + from_z[kind, k].astype(F32)
        done_z[kind, z] = total.astype(BF16)
        for k in range(1, ZS):
            along_z(kind, k, z, lax.rem(z + k, ZS)).start()

    def spread_y(kind):
        for k in range(1, ZS):
            source = lax.rem(z + ZS - k, ZS)
            along_z(kind, k, z, source).wait_send()
            along_z(kind, k, source, source).wait_recv()
        part = done_z[kind].reshape(128, 256).astype(F32).T.astype(BF16)
        whole[kind, pl.ds(pl.multiple_of(y * 256, 256), 256), k_mine] = part
        for k in range(1, YS):
            along_y(kind, k, y, lax.rem(y + k, YS)).start()
        to_sibling(kind, 0, k_mine).start()

    def spread_cores(kind):
        for k in range(1, YS):
            source = lax.rem(y + YS - k, YS)
            along_y(kind, k, source, source).wait_recv()
            to_sibling(kind, k, k_mine).start()

    def settle(kind):
        for k in range(1, YS):
            along_y(kind, k, y, lax.rem(y + k, YS)).wait_send()
        for k in range(YS):
            to_sibling(kind, k, k_mine).wait_send()
            to_sibling(kind, k, k_other).wait_recv()

    order = (1, 2, 3, 0)
    for k in order:

        @pl.loop(0, 2)
        def _(t):
            tile = x_at(k) * 2 + t
            keep(1, tile, dot(grad_rows_t[0], hidden[0, tile]) + dot(grad_rows_t[1], hidden[1, tile]))

        over_cores(1, k).start()

    def both_back(k, t):
        tile = x_at(k) * 2 + t
        theirs = gate_back(1, x_at(k), t)
        mine = gate_back(0, x_at(k), t)
        keep(0, tile, dot(rows_t[0], mine) + dot(rows_t[1], theirs))

    def chunk_back(k):
        @pl.loop(0, 2, unroll=True)
        def _(t):
            both_back(k, t)

        over_cores(0, k).start()

    pass_on(1, 1)
    pass_on(1, 2)
    chunk_back(1)
    pass_on(1, 3)
    chunk_back(2)
    pass_on(0, 1)
    chunk_back(3)
    pass_on(0, 2)
    both_back(0, 0)
    pass_on(0, 3)
    sum_x(1)
    both_back(0, 1)
    over_cores(0, 0).start()
    norm_out[...] = ff[1].astype(BF16)
    norm_copy = exchange(norm_out, norm_in, 3)
    norm_copy.start()
    sum_y(1)
    sum_x(0)
    norm_copy.wait()

    def tail(b, _):
        upstream = ff[0, rows_of(b), :] + norm_in[rows_of(b), :].astype(F32)
        grad_inter = norm_back(inter_unit[b], inter_scale[b, :, 0:1], fm_gain[...], upstream).astype(BF16)
        grad_mixing = dot(grad_inter, crossed[b], 1, 1).astype(BF16)
        grad_crossed = dot(mixing[b], grad_inter, 0, 0).astype(BF16)
        total = grad_summed[b] + dot(proj_p[...], grad_mixing, 0, 0)
        total = total + dot(proj_y[...], grad_crossed, 1, 1)
        slot_grads[b] = dot(by_slot[...], total.astype(BF16)).astype(BF16)
        return 0

    lax.fori_loop(0, SAMPLES // 2, tail, 0)
    sum_z(1)
    sum_y(0)
    lax.fori_loop(SAMPLES // 2, SAMPLES, tail, 0)

    def bags_back(first, last):
        @pl.loop(first, last)
        def _(k):
            peer = peer_at(k)
            send(
                slot_grads.at[:, slots_at(peer), :],
                bag_grads.at[samples_at(me)],
                back_send.at[k],
                back_recv.at[k],
                emb=peer,
            ).start()

    bags_back(1, 8)
    own_bags = pltpu.make_async_copy(
        slot_grads.at[:, slots_at(me), :], bag_grads.at[samples_at(me)], local_sem.at[7]
    )
    own_bags.start()
    sum_z(0)
    bags_back(8, 16)
    spread_y(1)
    bags_back(16, 24)
    spread_y(0)
    bags_back(24, EMB)
    spread_cores(1)
    spread_cores(0)
    settle(1)
    settle(0)

    @pl.loop(1, EMB)
    def _(k):
        source = lax.rem(me + EMB - lax.rem(k * STEP, EMB), EMB)
        copy = send(
            slot_grads.at[:, slots_at(source), :],
            bag_grads.at[samples_at(source)],
            back_send.at[k],
            back_recv.at[k],
            emb=source,
        )
        copy.wait_recv()
        copy.wait_send()

    own_bags.wait()
    layer_copy.wait()


def whole_layer(*operands):
    anywhere = pl.BlockSpec(memory_space=pl.ANY)
    vmem = pl.BlockSpec(memory_space=pltpu.VMEM)
    dma = pltpu.SemaphoreType.DMA
    return pl.pallas_call(
        layer_kernel,
        name="whole_layer",
        out_shape=(
            jax.ShapeDtypeStruct((SAMPLES, FIELDS, E), BF16),
            jax.ShapeDtypeStruct((GROUP_B, SLOTS, E), BF16),
            jax.ShapeDtypeStruct((2, SLICE, E), BF16),
        ),
        in_specs=[vmem] * 5 + [anywhere] * 7,
        out_specs=(anywhere, anywhere, vmem),
        scratch_shapes=[
            pltpu.VMEM((2, GROUP_B * SLOTS, 128), F32),
            pltpu.VMEM((GROUP_B, SLOTS, E), BF16),
            pltpu.VMEM((SAMPLES, FIELDS, E), BF16),
            pltpu.VMEM((XS, SLICE, E), BF16),
            pltpu.VMEM((XS, SLICE, E), BF16),
            pltpu.VMEM((FIELDS, E), BF16),
            pltpu.VMEM((NF, FIELDS), BF16),
            pltpu.VMEM((NL, FIELDS), BF16),
            pltpu.VMEM((SAMPLES, FIELDS, E), BF16),
            pltpu.VMEM((SAMPLES, FIELDS, E), BF16),
            pltpu.VMEM((SAMPLES, FIELDS, E), BF16),
            pltpu.VMEM((SAMPLES, E, E), BF16),
            pltpu.VMEM((SAMPLES, NF, E), BF16),
            pltpu.VMEM((SAMPLES, NF, E), F32),
            pltpu.VMEM((SAMPLES, NF, 128), F32),
            pltpu.VMEM((2, NROW, E), BF16),
            pltpu.VMEM((2, E, NROW), BF16),
            pltpu.VMEM((2, TILES, NROW, TH), BF16),
            pltpu.VMEM((2, TILES, NROW, TH), BF16),
            pltpu.VMEM((2, NROW, E), F32),
            pltpu.VMEM((NROW, E), BF16),
            pltpu.VMEM((NROW, E), BF16),
            pltpu.VMEM((FIELDS, FIELDS), BF16),
            pltpu.VMEM((SAMPLES, NL, E), F32),
            pltpu.VMEM((SAMPLES, FIELDS, E), F32),
            pltpu.VMEM((2, NROW, E), BF16),
            pltpu.VMEM((2, E, NROW), BF16),
            pltpu.VMEM((SAMPLES, NL, E), BF16),
            pltpu.VMEM((NROW, E), BF16),
            pltpu.VMEM((NROW, E), BF16),
            pltpu.VMEM((SAMPLES, FIELDS, E), BF16),
            pltpu.VMEM((2, TILES * 2, 256, 256), BF16),
            pltpu.VMEM((2, TILES * 2, 128, 256), BF16),
            pltpu.VMEM((2, TILES * 2, 128, 256), BF16),
            pltpu.VMEM((2, XS - 1, 4, 128, 256), BF16),
            pltpu.VMEM((2, YS, 128, 256), BF16),
            pltpu.VMEM((2, YS - 1, 128, 256), BF16),
            pltpu.VMEM((2, ZS, 128 // ZS, 256), BF16),
            pltpu.VMEM((2, ZS - 1, 128 // ZS, 256), BF16),
            pltpu.VMEM((2, ZS, 128 // ZS, 256), BF16),
            dma((SLOTS,)),
            dma((8,)),
            dma((EMB,)),
            dma((EMB,)),
            dma((EMB,)),
            dma((EMB,)),
            dma((4, XS - 1)),
            dma((4, XS - 1)),
            dma((4,)),
            dma((4,)),
            dma((2, XS)),
            dma((2, XS)),
            dma((2, 20)),
            dma((2, 20)),
        ],
        compiler_params=pltpu.CompilerParams(
            collective_id=0, has_side_effects=True, vmem_limit_bytes=62 << 20
        ),
    )(*operands)


def finish_kernel(
    layer_out, bag_grads, whole, layer_final, bag_final, up, down, held, sums_in, sums, in_sem, out_sem, sum_sem,
):
    pairs = ((layer_out, layer_final), (bag_grads, bag_final))
    rows = [layer_out.shape[0] // 2, bag_grads.shape[0] // 2]
    incoming, outgoing = [], []
    for n, (src, dst) in enumerate(pairs):
        for half in range(2):
            part = pl.ds(half * rows[n], rows[n])
            here = held[n].at[part]
            incoming.append(pltpu.make_async_copy(src.at[part], here, in_sem.at[n, half]))
            outgoing.append(pltpu.make_async_copy(here, dst.at[part], out_sem.at[n, half]))
    sums_copies = [pltpu.make_async_copy(whole.at[kind], sums_in.at[kind], in_sem.at[2, kind]) for kind in range(2)]
    for copy in sums_copies + incoming:
        copy.start()
    sum_copies = []
    for kind, out in enumerate((up, down)):
        sums_copies[kind].wait()
        for y in range(YS):
            part = pl.ds(y * 256, 256)
            sums[kind, part] = sums_in[kind, part].astype(F32)
            copy = pltpu.make_async_copy(sums.at[kind, part], out.at[part], sum_sem.at[kind, y])
            copy.start()
            sum_copies.append(copy)
            n = kind * YS + y
            if n % 2 == 1:
                incoming[n // 2].wait()
                outgoing[n // 2].start()
    for copy in outgoing + sum_copies:
        copy.wait()


def finish_outputs(layer_out, bag_grads, whole):
    anywhere = pl.BlockSpec(memory_space=pl.ANY)
    dma = pltpu.SemaphoreType.DMA
    return pl.pallas_call(
        finish_kernel,
        name="finish_outputs",
        out_shape=(
            jax.ShapeDtypeStruct(layer_out.shape, BF16),
            jax.ShapeDtypeStruct(bag_grads.shape, BF16),
            jax.ShapeDtypeStruct((SLICE, E), F32),
            jax.ShapeDtypeStruct((SLICE, E), F32),
        ),
        in_specs=[anywhere] * 3,
        out_specs=(anywhere,) * 4,
        scratch_shapes=[
            [pltpu.VMEM(layer_out.shape, BF16), pltpu.VMEM(bag_grads.shape, BF16)],
            pltpu.VMEM((2, SLICE, E), BF16),
            pltpu.VMEM((2, SLICE, E), F32),
            dma((3, 2)),
            dma((2, 2)),
            dma((2, YS)),
        ],
    )(layer_out, bag_grads, whole)


def body(
    tables,
    bag_ids,
    bag_lengths,
    slot_field,
    proj_y,
    proj_p,
    linear_w,
    fm_gain,
    w_up,
    w_down,
    out_gain,
    cotangent,
):
    layer_out, bag_grads, weight_grads = whole_layer(
        bag_ids[0].transpose(1, 2, 0),
        bag_lengths[0].transpose(1, 0),
        slot_field.reshape(1, FIELDS),
        fm_gain.reshape(1, E),
        out_gain.reshape(1, E),
        tables,
        w_up,
        w_down,
        proj_y,
        proj_p,
        linear_w,
        cotangent[0],
    )
    layer_out, bag_grads, grad_up, grad_down = finish_outputs(layer_out, bag_grads, weight_grads)
    return (layer_out[None], bag_grads[None], grad_up, grad_down)


def solution(mesh):
    placed = (
        P("emb", None, None),
        P("wide", None, "emb", None),
        P("wide", None, "emb"),
        P(),
        P(),
        P(),
        P(),
        P(),
        P("wide", None),
        P("wide", None),
        P(),
        P("wide", "emb", None, None),
    )
    return jax.shard_map(
        body,
        mesh=mesh,
        in_specs=placed,
        out_specs=(
            P("wide", "emb", None, None),
            P("wide", None, "emb", None),
            P("wide", None),
            P("wide", None),
        ),
        check_vma=False,
    )
```

```python
import functools

import jax
import jax.numpy as jnp
from jax import lax
from jax.experimental import pallas as pl
from jax.experimental.pallas import tpu as pltpu
from jax.sharding import PartitionSpec as P

MESH = pl.DeviceIdType.MESH
F32 = jnp.float32
BF16 = jnp.bfloat16

E = 256
FIELDS = 512
ROWS = 512
NF = 128
NL = 384
BAG = 4
SAMPLES = 4
SLOTS = 16
GROUP_B = 128
EMB = 32
STEP = 11
XS = 4
YS = 4
ZS = 4
SLICE = 1024
TH = 512
TILES = 8
NROW = SAMPLES * NF
norm_eps = 1e-05


def dot(a, b, ca=1, cb=0):
    return lax.dot_general(a, b, (((ca,), (cb,)), ((), ())), preferred_element_type=F32)


def send(src, dst, send_sem, recv_sem, **device):
    return pltpu.make_async_remote_copy(
        src_ref=src,
        dst_ref=dst,
        send_sem=send_sem,
        recv_sem=recv_sem,
        device_id=device,
        device_id_type=MESH,
    )


def signal(sem, **device):
    pl.semaphore_signal(sem, inc=1, device_id=device, device_id_type=MESH)


def norm_forward(values):
    centre = jnp.mean(values, axis=-1, keepdims=True)
    shifted = values - centre
    scale = lax.rsqrt(jnp.mean(shifted * shifted, axis=-1, keepdims=True) + norm_eps)
    return shifted * scale, scale


def norm_back(unit, scale, gain, upstream):
    scaled = upstream * gain
    return scale * (
        scaled
        - jnp.mean(scaled, axis=-1, keepdims=True)
        - unit * jnp.mean(scaled * unit, axis=-1, keepdims=True)
    )


def layer_kernel(
    ids, lengths, field_row, fm_gain, out_gain,
    tables, w_up_hbm, w_down_hbm, proj_y_hbm, proj_p_hbm, linear_w_hbm, cotangent_hbm,
    layer_out_hbm, bag_grads, whole,
    pooled, outgoing, slots, w_up, w_down, proj_y, proj_p, linear_w, cotangent, layer_out,
    embeds, crossed, mixing, inter_unit, inter_scale, rows, rows_t, hidden, slope, ff, ff_out, ff_in,
    by_slot, linear_out, grad_summed, grad_rows, grad_rows_t, grad_lin, norm_out, norm_in,
    slot_grads, grads, from_core, to_x, from_x, to_y, from_y, to_z, from_z, done_z,
    table_sem, local_sem, bag_send, bag_recv, back_send, back_recv, w_send, w_recv, pair_send, pair_recv,
    core_send, core_recv, sum_send, sum_recv,
):
    me = lax.axis_index("emb")
    wide = lax.axis_index("wide")
    x = wide // 2
    z_lo = lax.rem(wide, 2)
    partner = wide + 1 - 2 * z_lo
    core = lax.rem(me, 2)
    y = lax.rem(me // 2, YS)
    z = me // (2 * YS)
    sibling = me + 1 - 2 * core

    def peer_at(k):
        return lax.rem(me + lax.rem(k * STEP, EMB), EMB)

    def x_at(offset):
        return lax.rem(x + XS + offset, XS)

    def wide_at(x_to):
        return x_to * 2 + z_lo

    def emb_at(z_to, y_to):
        return (z_to * YS + y_to) * 2 + core

    def table(s):
        return hidden.at[s // TILES, s % TILES, :, pl.ds(0, E)]

    def fetch(s):
        return pltpu.make_async_copy(tables.at[s], table(s), table_sem.at[s])

    for s in range(SLOTS):
        fetch(s).start()
    staged = [
        pltpu.make_async_copy(src, dst, local_sem.at[n])
        for n, (src, dst) in enumerate(
            (
                (w_up_hbm, w_up.at[x]),
                (w_down_hbm, w_down.at[x]),
                (proj_y_hbm, proj_y),
                (proj_p_hbm, proj_p),
                (linear_w_hbm, linear_w),
                (cotangent_hbm, cotangent),
            )
        )
    ]
    for copy in staged:
        copy.start()

    barrier = pltpu.get_barrier_semaphore()

    @pl.loop(1, EMB)
    def _(k):
        signal(barrier, emb=lax.rem(me + k, EMB))

    for k in range(1, XS):
        signal(barrier, wide=wide_at(x_at(k)))
    signal(barrier, wide=partner)
    def half_of(which):
        return pl.ds(pl.multiple_of(which * TH, TH), TH)

    weights = ((w_up_hbm, w_up), (w_down_hbm, w_down))
    def weights_from(k):
        if k == 0:
            staged[0].wait()
            staged[1].wait()
            return
        for i, (w, full) in enumerate(weights):
            pass_weights(i, k, 1 - core).wait_recv()
            pass_weights(i, k, core).wait_send()

    def pass_weights(i, k, which):
        part = weights[i][1].at[x_at(-k), half_of(which)]
        return send(part, part, w_send.at[2 + i, k - 1], w_recv.at[2 + i, k - 1], emb=sibling)

    bucket = lax.broadcasted_iota(jnp.int32, (ROWS, GROUP_B), 0)

    for s in range(SLOTS):
        if s == SLOTS // 2:
            pl.semaphore_wait(barrier, EMB - 1 + XS)
            for k in range(1, XS):
                for i, (w, full) in enumerate(weights):
                    send(
                        w.at[half_of(core)],
                        full.at[x, half_of(core)],
                        w_send.at[i, k - 1],
                        w_recv.at[i, k - 1],
                        wide=wide_at(x_at(k)),
                    ).start()
        fetch(s).wait()
        live = lengths[s : s + 1, :]
        counts = jnp.zeros((ROWS, GROUP_B), F32)
        for j in range(BAG):
            wanted = jnp.where(live > j, ids[s, j : j + 1, :], -1)
            counts = counts + jnp.where(bucket == wanted, 1.0, 0.0)
        bags = dot(counts.astype(BF16), table(s)[...], 0, 0)
        for half in range(2):
            pooled[half, pl.ds(s, GROUP_B, stride=SLOTS), :] = bags[:, half * 128 : half * 128 + 128]

    for half in range(2):
        outgoing[:, :, half * 128 : half * 128 + 128] = (
            pooled[half].astype(BF16).reshape(GROUP_B, SLOTS, 128)
        )

    def slots_at(owner):
        return pl.ds(pl.multiple_of(owner * SLOTS, SLOTS), SLOTS)

    def samples_at(owner):
        return pl.ds(owner * SAMPLES, SAMPLES)

    @pl.loop(1, EMB)
    def _(k):
        peer = peer_at(k)
        send(
            outgoing.at[samples_at(peer)], slots.at[:, slots_at(me), :], bag_send.at[k], bag_recv.at[k], emb=peer
        ).start()

    slots[:, slots_at(me), :] = outgoing[samples_at(me)]

    by_field = jnp.where(
        lax.broadcasted_iota(jnp.int32, (FIELDS, FIELDS), 0) == field_row[...], 1.0, 0.0
    ).astype(BF16)
    by_slot[...] = by_field.astype(F32).T.astype(BF16)
    for copy in staged[2:]:
        copy.wait()

    for k in (1, 3, 2):
        for i, (w, full) in enumerate(weights):
            copy = send(
                w.at[half_of(core)],
                full.at[x_at(-k), half_of(core)],
                w_send.at[i, k - 1],
                w_recv.at[i, k - 1],
                wide=wide_at(x_at(-k)),
            )
            copy.wait_recv()
            copy.wait_send()
            pass_weights(i, k, core).start()

    @pl.loop(1, EMB)
    def _(k):
        source = lax.rem(me + EMB - lax.rem(k * STEP, EMB), EMB)
        copy = send(
            outgoing.at[samples_at(source)],
            slots.at[:, slots_at(source), :],
            bag_send.at[k],
            bag_recv.at[k],
            emb=source,
        )
        copy.wait_recv()
        copy.wait_send()

    def exchange(src, dst, n):
        return send(src, dst, pair_send.at[n], pair_recv.at[n], wide=partner)

    def rows_of(b):
        return pl.ds(pl.multiple_of(b * NF, NF), NF)

    def embed(b, _):
        sample = dot(by_field, slots[b]).astype(BF16)
        embeds[b] = sample
        cross = dot(sample, proj_y[...], 0, 0).astype(BF16)
        crossed[b] = cross
        mix = dot(proj_p[...], sample).astype(BF16)
        mixing[b] = mix
        unit, scale = norm_forward(dot(mix, cross))
        inter_unit[b] = unit
        inter_scale[b] = jnp.broadcast_to(scale, (NF, 128))
        rows[0, rows_of(b), :] = (unit * fm_gain[...]).astype(BF16)
        return 0

    lax.fori_loop(0, SAMPLES, embed, 0, unroll=True)
    rows_copy = exchange(rows.at[0], rows.at[1], 0)
    rows_copy.start()
    ff[...] = jnp.zeros_like(ff)

    def forward(group, k):
        chunk = x_at(-k)

        @pl.loop(0, 2, unroll=True)
        def _(t):
            tile = chunk * 2 + t
            here = pl.ds(pl.multiple_of(t * TH, TH), TH)
            gate = dot(rows[group], w_up[chunk, here, :], 1, 1)
            sigma = 0.5 * jnp.tanh(0.5 * gate) + 0.5
            act = gate * sigma
            slope[group, tile] = (sigma + act * (1.0 - sigma)).astype(BF16)
            act = act.astype(BF16)
            hidden[group, tile] = act
            ff[group] += dot(act, w_down[chunk, here, :])

    weights_from(0)
    forward(0, 0)

    def linear(b, _):
        linear_out[b] = dot(linear_w[...], embeds[b])
        return 0

    lax.fori_loop(0, SAMPLES, linear, 0)
    rows_copy.wait()
    forward(1, 0)
    for k in range(1, XS):
        weights_from(k)
        forward(1, k)
    ff_out[...] = ff[1].astype(BF16)
    ff_copy = exchange(ff_out, ff_in, 1)
    ff_copy.start()
    for k in range(1, XS):
        forward(0, k)
    rows_t[0] = rows[0].astype(F32).T.astype(BF16)
    rows_t[1] = rows[1].astype(F32).T.astype(BF16)
    ff_copy.wait()

    def finish(values, b, first, count):
        here = slice(first, first + count)
        unit, scale = norm_forward(values + embeds[b, here, :].astype(F32))
        layer_out[b, here, :] = (unit * out_gain[...]).astype(BF16)
        grad = norm_back(unit, scale, out_gain[...], cotangent[b, here, :].astype(F32))
        grad_summed[b, here, :] = grad
        return grad.astype(BF16)

    def finish_ff(b, _):
        total = ff[0, rows_of(b), :] + ff_in[rows_of(b), :].astype(F32)
        grad_rows[0, rows_of(b), :] = finish(total, b, 0, NF)
        return 0

    lax.fori_loop(0, SAMPLES, finish_ff, 0, unroll=True)
    grad_copy = exchange(grad_rows.at[0], grad_rows.at[1], 2)
    grad_copy.start()

    def finish_linear(b, _):
        grad_lin[b] = finish(linear_out[b], b, NF, NL)
        grad_summed[b] += dot(linear_w[...], grad_lin[b], 0, 0)
        return 0

    lax.fori_loop(0, SAMPLES, finish_linear, 0)
    layer_copy = pltpu.make_async_copy(layer_out, layer_out_hbm, local_sem.at[6])
    layer_copy.start()
    grad_rows_t[0] = grad_rows[0].astype(F32).T.astype(BF16)
    ff[...] = jnp.zeros_like(ff)
    grad_copy.wait()
    grad_rows_t[1] = grad_rows[1].astype(F32).T.astype(BF16)

    def gate_back(group, chunk, t):
        here = pl.ds(pl.multiple_of(t * TH, TH), TH)
        tile = chunk * 2 + t
        grad_hidden = dot(grad_rows[group], w_down[chunk, here, :], 1, 1)
        grad_gate = (grad_hidden * slope[group, tile].astype(F32)).astype(BF16)
        ff[group] += dot(grad_gate, w_up[chunk, here, :])
        return grad_gate

    k_mine = pl.ds(pl.multiple_of(core * 128, 128), 128)
    k_other = pl.ds(pl.multiple_of(128 - core * 128, 128), 128)

    def keep(kind, tile, part):
        part = part.astype(BF16)
        for half in range(2):
            grads[kind, tile * 2 + half] = part[:, half * 256 : half * 256 + 256]

    def over_cores(kind, k):
        chunk = pl.ds(x_at(k) * 4, 4)
        return send(
            grads.at[kind, chunk, k_other],
            from_core.at[kind, chunk],
            core_send.at[kind, k],
            core_recv.at[kind, k],
            emb=sibling,
        )

    def over_x(kind, k):
        return send(
            to_x.at[kind, pl.ds(x_at(k) * 4, 4)],
            from_x.at[kind, k - 1],
            sum_send.at[kind, k],
            sum_recv.at[kind, k],
            wide=wide_at(x_at(k)),
        )

    def over_y(kind, k):
        peer = lax.rem(y + k, YS)
        return send(
            to_y.at[kind, peer],
            from_y.at[kind, k - 1],
            sum_send.at[kind, 3 + k],
            sum_recv.at[kind, 3 + k],
            emb=emb_at(z, peer),
        )

    def over_z(kind, k):
        peer = lax.rem(z + k, ZS)
        return send(
            to_z.at[kind, peer],
            from_z.at[kind, k - 1],
            sum_send.at[kind, 6 + k],
            sum_recv.at[kind, 6 + k],
            emb=emb_at(peer, y),
        )

    def along_z(kind, k, z_of, z_to):
        part = done_z.at[kind, z_of]
        return send(part, part, sum_send.at[kind, 9 + k], sum_recv.at[kind, 9 + k], emb=emb_at(z_to, y))

    def band(kind, y_of, columns):
        return whole.at[kind, pl.ds(pl.multiple_of(y_of * 256, 256), 256), columns]

    def along_y(kind, k, y_of, y_to):
        part = band(kind, y_of, k_mine)
        return send(part, part, sum_send.at[kind, 12 + k], sum_recv.at[kind, 12 + k], emb=emb_at(z, y_to))

    def to_sibling(kind, k, columns):
        part = band(kind, lax.rem(y + YS - k, YS), columns)
        return send(part, part, sum_send.at[kind, 16 + k], sum_recv.at[kind, 16 + k], emb=sibling)

    def pass_on(kind, k):
        over_cores(kind, k).wait()

        @pl.loop(0, 4)
        def _(t):
            part = x_at(k) * 4 + t
            to_x[kind, part] = (
                grads[kind, part, k_mine].astype(F32) + from_core[kind, part].astype(F32)
            ).astype(BF16)

        over_x(kind, k).start()

    def sum_x(kind):
        over_cores(kind, 0).wait()
        for k in range(1, XS):
            over_x(kind, k).wait()

        @pl.loop(0, 4)
        def _(t):
            mine = x * 4 + t
            total = grads[kind, mine, k_mine].astype(F32) + from_core[kind, mine].astype(F32)
            for k in range(XS - 1):
                total = total + from_x[kind, k, t].astype(F32)
            to_y[kind, t] = total.astype(BF16)

        for k in range(1, YS):
            over_y(kind, k).start()

    def sum_y(kind):
        for k in range(1, YS):
            over_y(kind, k).wait()
        total = to_y[kind, y].astype(F32)
        for k in range(YS - 1):
            total = total + from_y[kind, k].astype(F32)
        to_z[kind] = total.astype(BF16).reshape(ZS, 128 // ZS, 256)
        for k in range(1, ZS):
            over_z(kind, k).start()

    def sum_z(kind):
        for k in range(1, ZS):
            over_z(kind, k).wait()
        total = to_z[kind, z].astype(F32)
        for k in range(ZS - 1):
            total = total + from_z[kind, k].astype(F32)
        done_z[kind, z] = total.astype(BF16)
        for k in range(1, ZS):
            along_z(kind, k, z, lax.rem(z + k, ZS)).start()

    def spread_y(kind):
        for k in range(1, ZS):
            source = lax.rem(z + ZS - k, ZS)
            along_z(kind, k, z, source).wait_send()
            along_z(kind, k, source, source).wait_recv()
        part = done_z[kind].reshape(128, 256).astype(F32).T.astype(BF16)
        whole[kind, pl.ds(pl.multiple_of(y * 256, 256), 256), k_mine] = part
        for k in range(1, YS):
            along_y(kind, k, y, lax.rem(y + k, YS)).start()
        to_sibling(kind, 0, k_mine).start()

    def spread_cores(kind):
        for k in range(1, YS):
            source = lax.rem(y + YS - k, YS)
            along_y(kind, k, source, source).wait_recv()
            to_sibling(kind, k, k_mine).start()

    def settle(kind):
        for k in range(1, YS):
            along_y(kind, k, y, lax.rem(y + k, YS)).wait_send()
        for k in range(YS):
            to_sibling(kind, k, k_mine).wait_send()
            to_sibling(kind, k, k_other).wait_recv()

    order = (1, 2, 3, 0)
    for k in order:

        @pl.loop(0, 2)
        def _(t):
            tile = x_at(k) * 2 + t
            keep(1, tile, dot(grad_rows_t[0], hidden[0, tile]) + dot(grad_rows_t[1], hidden[1, tile]))

        over_cores(1, k).start()

    def both_back(k, t):
        tile = x_at(k) * 2 + t
        theirs = gate_back(1, x_at(k), t)
        mine = gate_back(0, x_at(k), t)
        keep(0, tile, dot(rows_t[0], mine) + dot(rows_t[1], theirs))

    def chunk_back(k):
        @pl.loop(0, 2, unroll=True)
        def _(t):
            both_back(k, t)

        over_cores(0, k).start()

    pass_on(1, 1)
    pass_on(1, 2)
    chunk_back(1)
    pass_on(1, 3)
    chunk_back(2)
    pass_on(0, 1)
    chunk_back(3)
    pass_on(0, 2)
    both_back(0, 0)
    pass_on(0, 3)
    sum_x(1)
    both_back(0, 1)
    over_cores(0, 0).start()
    norm_out[...] = ff[1].astype(BF16)
    norm_copy = exchange(norm_out, norm_in, 3)
    norm_copy.start()
    sum_y(1)
    sum_x(0)
    norm_copy.wait()

    def tail(b, _):
        upstream = ff[0, rows_of(b), :] + norm_in[rows_of(b), :].astype(F32)
        grad_inter = norm_back(inter_unit[b], inter_scale[b, :, 0:1], fm_gain[...], upstream).astype(BF16)
        grad_mixing = dot(grad_inter, crossed[b], 1, 1).astype(BF16)
        grad_crossed = dot(mixing[b], grad_inter, 0, 0).astype(BF16)
        total = grad_summed[b] + dot(proj_p[...], grad_mixing, 0, 0)
        total = total + dot(proj_y[...], grad_crossed, 1, 1)
        slot_grads[b] = dot(by_slot[...], total.astype(BF16)).astype(BF16)
        return 0

    lax.fori_loop(0, SAMPLES // 2, tail, 0, unroll=True)
    sum_z(1)
    sum_y(0)
    lax.fori_loop(SAMPLES // 2, SAMPLES, tail, 0, unroll=True)

    def bags_back(first, last):
        @pl.loop(first, last)
        def _(k):
            peer = peer_at(k)
            send(
                slot_grads.at[:, slots_at(peer), :],
                bag_grads.at[samples_at(me)],
                back_send.at[k],
                back_recv.at[k],
                emb=peer,
            ).start()

    bags_back(1, 8)
    own_bags = pltpu.make_async_copy(
        slot_grads.at[:, slots_at(me), :], bag_grads.at[samples_at(me)], local_sem.at[7]
    )
    own_bags.start()
    sum_z(0)
    bags_back(8, EMB)
    spread_y(1)
    spread_y(0)
    spread_cores(1)
    spread_cores(0)
    settle(1)
    settle(0)

    @pl.loop(1, EMB)
    def _(k):
        source = lax.rem(me + EMB - lax.rem(k * STEP, EMB), EMB)
        copy = send(
            slot_grads.at[:, slots_at(source), :],
            bag_grads.at[samples_at(source)],
            back_send.at[k],
            back_recv.at[k],
            emb=source,
        )
        copy.wait_recv()
        copy.wait_send()

    own_bags.wait()
    layer_copy.wait()


def whole_layer(*operands):
    anywhere = pl.BlockSpec(memory_space=pl.ANY)
    vmem = pl.BlockSpec(memory_space=pltpu.VMEM)
    dma = pltpu.SemaphoreType.DMA
    return pl.pallas_call(
        layer_kernel,
        name="whole_layer",
        out_shape=(
            jax.ShapeDtypeStruct((SAMPLES, FIELDS, E), BF16),
            jax.ShapeDtypeStruct((GROUP_B, SLOTS, E), BF16),
            jax.ShapeDtypeStruct((2, SLICE, E), BF16),
        ),
        in_specs=[vmem] * 5 + [anywhere] * 7,
        out_specs=(anywhere, anywhere, vmem),
        scratch_shapes=[
            pltpu.VMEM((2, GROUP_B * SLOTS, 128), F32),
            pltpu.VMEM((GROUP_B, SLOTS, E), BF16),
            pltpu.VMEM((SAMPLES, FIELDS, E), BF16),
            pltpu.VMEM((XS, SLICE, E), BF16),
            pltpu.VMEM((XS, SLICE, E), BF16),
            pltpu.VMEM((FIELDS, E), BF16),
            pltpu.VMEM((NF, FIELDS), BF16),
            pltpu.VMEM((NL, FIELDS), BF16),
            pltpu.VMEM((SAMPLES, FIELDS, E), BF16),
            pltpu.VMEM((SAMPLES, FIELDS, E), BF16),
            pltpu.VMEM((SAMPLES, FIELDS, E), BF16),
            pltpu.VMEM((SAMPLES, E, E), BF16),
            pltpu.VMEM((SAMPLES, NF, E), BF16),
            pltpu.VMEM((SAMPLES, NF, E), F32),
            pltpu.VMEM((SAMPLES, NF, 128), F32),
            pltpu.VMEM((2, NROW, E), BF16),
            pltpu.VMEM((2, E, NROW), BF16),
            pltpu.VMEM((2, TILES, NROW, TH), BF16),
            pltpu.VMEM((2, TILES, NROW, TH), BF16),
            pltpu.VMEM((2, NROW, E), F32),
            pltpu.VMEM((NROW, E), BF16),
            pltpu.VMEM((NROW, E), BF16),
            pltpu.VMEM((FIELDS, FIELDS), BF16),
            pltpu.VMEM((SAMPLES, NL, E), F32),
            pltpu.VMEM((SAMPLES, FIELDS, E), F32),
            pltpu.VMEM((2, NROW, E), BF16),
            pltpu.VMEM((2, E, NROW), BF16),
            pltpu.VMEM((SAMPLES, NL, E), BF16),
            pltpu.VMEM((NROW, E), BF16),
            pltpu.VMEM((NROW, E), BF16),
            pltpu.VMEM((SAMPLES, FIELDS, E), BF16),
            pltpu.VMEM((2, TILES * 2, 256, 256), BF16),
            pltpu.VMEM((2, TILES * 2, 128, 256), BF16),
            pltpu.VMEM((2, TILES * 2, 128, 256), BF16),
            pltpu.VMEM((2, XS - 1, 4, 128, 256), BF16),
            pltpu.VMEM((2, YS, 128, 256), BF16),
            pltpu.VMEM((2, YS - 1, 128, 256), BF16),
            pltpu.VMEM((2, ZS, 128 // ZS, 256), BF16),
            pltpu.VMEM((2, ZS - 1, 128 // ZS, 256), BF16),
            pltpu.VMEM((2, ZS, 128 // ZS, 256), BF16),
            dma((SLOTS,)),
            dma((8,)),
            dma((EMB,)),
            dma((EMB,)),
            dma((EMB,)),
            dma((EMB,)),
            dma((4, XS - 1)),
            dma((4, XS - 1)),
            dma((4,)),
            dma((4,)),
            dma((2, XS)),
            dma((2, XS)),
            dma((2, 20)),
            dma((2, 20)),
        ],
        compiler_params=pltpu.CompilerParams(
            collective_id=0, has_side_effects=True, vmem_limit_bytes=62 << 20
        ),
    )(*operands)


def finish_kernel(
    layer_out, bag_grads, whole, layer_final, bag_final, up, down, held, sums_in, sums, in_sem, out_sem, sum_sem,
):
    pairs = ((layer_out, layer_final), (bag_grads, bag_final))
    rows = [layer_out.shape[0] // 2, bag_grads.shape[0] // 2]
    incoming, outgoing = [], []
    for n, (src, dst) in enumerate(pairs):
        for half in range(2):
            part = pl.ds(half * rows[n], rows[n])
            here = held[n].at[part]
            incoming.append(pltpu.make_async_copy(src.at[part], here, in_sem.at[n, half]))
            outgoing.append(pltpu.make_async_copy(here, dst.at[part], out_sem.at[n, half]))
    sums_copies = [pltpu.make_async_copy(whole.at[kind], sums_in.at[kind], in_sem.at[2, kind]) for kind in range(2)]
    for copy in sums_copies + incoming:
        copy.start()
    sum_copies = []
    for kind, out in enumerate((up, down)):
        sums_copies[kind].wait()
        for y in range(YS):
            part = pl.ds(y * 256, 256)
            sums[kind, part] = sums_in[kind, part].astype(F32)
            copy = pltpu.make_async_copy(sums.at[kind, part], out.at[part], sum_sem.at[kind, y])
            copy.start()
            sum_copies.append(copy)
            n = kind * YS + y
            if n % 2 == 1:
                incoming[n // 2].wait()
                outgoing[n // 2].start()
    for copy in outgoing + sum_copies:
        copy.wait()


def finish_outputs(layer_out, bag_grads, whole):
    anywhere = pl.BlockSpec(memory_space=pl.ANY)
    dma = pltpu.SemaphoreType.DMA
    return pl.pallas_call(
        finish_kernel,
        name="finish_outputs",
        out_shape=(
            jax.ShapeDtypeStruct(layer_out.shape, BF16),
            jax.ShapeDtypeStruct(bag_grads.shape, BF16),
            jax.ShapeDtypeStruct((SLICE, E), F32),
            jax.ShapeDtypeStruct((SLICE, E), F32),
        ),
        in_specs=[anywhere] * 3,
        out_specs=(anywhere,) * 4,
        scratch_shapes=[
            [pltpu.VMEM(layer_out.shape, BF16), pltpu.VMEM(bag_grads.shape, BF16)],
            pltpu.VMEM((2, SLICE, E), BF16),
            pltpu.VMEM((2, SLICE, E), F32),
            dma((3, 2)),
            dma((2, 2)),
            dma((2, YS)),
        ],
    )(layer_out, bag_grads, whole)


def body(
    tables,
    bag_ids,
    bag_lengths,
    slot_field,
    proj_y,
    proj_p,
    linear_w,
    fm_gain,
    w_up,
    w_down,
    out_gain,
    cotangent,
):
    layer_out, bag_grads, weight_grads = whole_layer(
        bag_ids[0].transpose(1, 2, 0),
        bag_lengths[0].transpose(1, 0),
        slot_field.reshape(1, FIELDS),
        fm_gain.reshape(1, E),
        out_gain.reshape(1, E),
        tables,
        w_up,
        w_down,
        proj_y,
        proj_p,
        linear_w,
        cotangent[0],
    )
    layer_out, bag_grads, grad_up, grad_down = finish_outputs(layer_out, bag_grads, weight_grads)
    return (layer_out[None], bag_grads[None], grad_up, grad_down)


def solution(mesh):
    placed = (
        P("emb", None, None),
        P("wide", None, "emb", None),
        P("wide", None, "emb"),
        P(),
        P(),
        P(),
        P(),
        P(),
        P("wide", None),
        P("wide", None),
        P(),
        P("wide", "emb", None, None),
    )
    return jax.shard_map(
        body,
        mesh=mesh,
        in_specs=placed,
        out_specs=(
            P("wide", "emb", None, None),
            P("wide", None, "emb", None),
            P("wide", None),
            P("wide", None),
        ),
        check_vma=False,
    )
```
